32 devices in a mesh: dp: 8 (over z, y), tensor: 4 (over x, core).
Axes of the slice: x: 2, y: 2, z: 4, core: 2. Of those that a mesh axis runs over, the one named last changes fastest.
Arguments:
- hidden_in: bfloat16 [8, 1024, 2048], P('dp', 'tensor'), may hold values from -6 to 6
- out_grad: bfloat16 [8, 1024, 2048], P('dp', 'tensor'), may hold values from -6 to 6
- segment_ids: int32 [8, 1024], P('dp'), may hold values from 0 to 3, never falling along the last dimension, each value on 1 to 512 neighbouring positions
- norm1_gain: bfloat16 [2048], P('dp'), may hold values from 0.5 to 1.5
- w_query: bfloat16 [2048, 2048], P('dp', 'tensor'), may hold values from -0.125 to 0.125
- w_key: bfloat16 [2048, 2048], P('dp', 'tensor'), may hold values from -0.125 to 0.125
- w_value: bfloat16 [2048, 3456], P('dp', 'tensor'), may hold values from -0.125 to 0.125
- w_gate: bfloat16 [2048, 3456], P('dp', 'tensor'), may hold values from -0.125 to 0.125
- w_out: bfloat16 [3456, 2048], P('tensor', 'dp'), may hold values from -0.109375 to 0.109375
- norm2_gain: bfloat16 [2048], P('dp'), may hold values from 0.5 to 1.5
- w_mlp_gate: bfloat16 [2048, 3456], P('dp', 'tensor'), may hold values from -0.125 to 0.125
- w_mlp_up: bfloat16 [2048, 3456], P('dp', 'tensor'), may hold values from -0.125 to 0.125
- w_mlp_down: bfloat16 [3456, 2048], P('tensor', 'dp'), may hold values from -0.109375 to 0.109375
Outputs:
- hidden_out: bfloat16 [8, 1024, 2048], P('dp', 'tensor')
- in_grad: float32 [8, 1024, 2048], P('dp', 'tensor')
- norm1_gain_grad: float32 [2048], P('dp')
- w_query_grad: float32 [2048, 2048], P('dp', 'tensor')
- w_key_grad: float32 [2048, 2048], P('dp', 'tensor')
- w_value_grad: float32 [2048, 3456], P('dp', 'tensor')
- w_gate_grad: float32 [2048, 3456], P('dp', 'tensor')
- w_out_grad: float32 [3456, 2048], P('tensor', 'dp')
- norm2_gain_grad: float32 [2048], P('dp')
- w_mlp_gate_grad: float32 [2048, 3456], P('dp', 'tensor')
- w_mlp_up_grad: float32 [2048, 3456], P('dp', 'tensor')
- w_mlp_down_grad: float32 [3456, 2048], P('tensor', 'dp')
The draws below stay inside these ranges and needn't reach their ends.
Inputs may be any that keep to these rules, and one draw needn't show every extreme that they name: `segment_ids`: along a sequence segment numbers never fall; each number marks one document of at most 512 tokens, and some document has exactly that many.
All inputs are finite; a program needn't handle non-finite values.
Results may differ from the reference program's by a relative error of at most 0.015.
Values may be sent and summed in bfloat16 or wider, within the bound.
A program may use at most 192 MiB of HBM per device.

```python
import math
import jax
import jax.numpy as jnp
import numpy as np
from jax import lax

D = 2048
HEADS = 8
KEY = 256
VAL = 432
FF = 3456
LEN = 1024
NSEQ = 8


def shard_levels(rng, extent, pieces, least, high):
    def one(dim, parts):
        heights = jax.random.uniform(jax.random.fold_in(jax.random.fold_in(rng, 6), dim), (parts,), jnp.float32, least / len(pieces), high / len(pieces))
        return jnp.repeat(jnp.exp(heights), extent[dim] // parts).reshape((-1,) + (1,) * (len(extent) - dim - 1))

    loudness = one(*pieces[0])
    for cut in pieces[1:]:
        loudness = loudness * one(*cut)
    return loudness


def split_up(count, total, limit, skew):
    portions = [(1 << 20) // math.isqrt(rank ** skew) + 1 for rank in range(2, count + 1)]
    rest, counts = total - limit - (count - 1), [1] * (count - 1)
    while rest > 0:
        candidates = [i for i in range(count - 1) if counts[i] < limit]
        mass, remaining = sum([portions[i] for i in candidates]), rest
        for i in candidates:
            addition = min(limit - counts[i], max(1, remaining * portions[i] // mass), rest)
            counts[i] = counts[i] + addition
            rest = rest - addition
    return np.array([limit] + counts)


def ragged(own_key, amount, total, reach, lean):
    if amount == 2:
        one = jax.random.randint(own_key, (), max(1, total - reach), min(reach, total - 1) + 1)
        return jnp.stack([one, total - one])
    tallies = jnp.asarray(split_up(amount, total, reach, lean), jnp.int32)
    pairs = (amount - 1) // 2
    source_of, taker = tallies[1:1 + 2 * pairs:2], tallies[2:2 + 2 * pairs:2]
    slack = jnp.minimum(source_of - 1, reach - taker)
    passed = jax.random.randint(jax.random.fold_in(own_key, 1), (pairs,), 0, 1 << 20) % (slack + 1)
    tallies = tallies.at[1:1 + 2 * pairs:2].set(source_of - passed).at[2:2 + 2 * pairs:2].set(taker + passed)
    return tallies[jax.random.permutation(jax.random.fold_in(own_key, 2), amount)]


def noise(rng, shape, scale, most, cuts=(), held_as=jnp.bfloat16):
    drawn = jax.random.normal(rng, shape, jnp.float32) * scale
    if len(cuts) > 0:
        drawn = shard_levels(rng, shape, cuts, -0.22, 0.18) * drawn
    return jnp.clip(drawn, min=-most, max=most).astype(held_as)


def setup_inputs(seed: int = 0) -> dict:
    key_list = jax.random.split(jax.random.key(seed), 14)
    hidden_in = noise(key_list[0], (NSEQ, LEN, D), 1.0, 6.0, ((0, 8), (1, 4)))
    out_grad = noise(key_list[1], (NSEQ, LEN, D), 1.0, 6.0, ((0, 8), (1, 4)))
    segment_ids = jax.vmap(lambda own: jnp.searchsorted(jnp.cumsum(ragged(own, 4, LEN, LEN // 2, 0)), jnp.arange(LEN), side="right"))(jax.random.split(key_list[2], NSEQ)).reshape((NSEQ, LEN)).astype(jnp.int32)
    norm1_gain = jnp.clip(1.0 + 0.1 * jax.random.normal(key_list[3], (D,), jnp.float32), 0.5, 1.5).astype(jnp.bfloat16)
    w_query = noise(key_list[4], (D, HEADS * KEY), D ** -0.5, 0.125, ((0, 8), (1, 4)))
    w_key = noise(key_list[5], (D, HEADS * KEY), D ** -0.5, 0.125, ((0, 8), (1, 4)))
    w_value = noise(key_list[6], (D, HEADS * VAL), D ** -0.5, 0.125, ((0, 8), (1, 4)))
    w_gate = noise(key_list[7], (D, HEADS * VAL), D ** -0.5, 0.125, ((0, 8), (1, 4)))
    w_out = noise(key_list[8], (HEADS * VAL, D), (HEADS * VAL) ** -0.5, 0.109375, ((0, 4), (1, 8)))
    norm2_gain = jnp.clip(1.0 + 0.1 * jax.random.normal(key_list[9], (D,), jnp.float32), 0.5, 1.5).astype(jnp.bfloat16)
    w_mlp_gate = noise(key_list[10], (D, FF), D ** -0.5, 0.125, ((0, 8), (1, 4)))
    w_mlp_up = noise(key_list[11], (D, FF), D ** -0.5, 0.125, ((0, 8), (1, 4)))
    w_mlp_down = noise(key_list[12], (FF, D), FF ** -0.5, 0.109375, ((0, 4), (1, 8)))
    return {"hidden_in": hidden_in, "out_grad": out_grad, "segment_ids": segment_ids, "norm1_gain": norm1_gain, "w_query": w_query, "w_key": w_key, "w_value": w_value, "w_gate": w_gate, "w_out": w_out, "norm2_gain": norm2_gain, "w_mlp_gate": w_mlp_gate, "w_mlp_up": w_mlp_up, "w_mlp_down": w_mlp_down}


@jax.custom_vjp
def low(v):
    return lax.optimization_barrier(v.astype(jnp.bfloat16)).astype(jnp.float32)

@jax.custom_vjp
def low_back(v):
    return v

def low_keep(v):
    return (low(v), None)

def low_pass(kept, grad):
    return (grad,)

def back_keep(v):
    return (v, None)

def back_low(kept, grad):
    return (low(grad),)
low.defvjp(low_keep, low_pass)
low_back.defvjp(back_keep, back_low)
HIGHEST = lax.Precision.HIGHEST

def multiply(left, right):
    return jnp.dot(left, right, precision=HIGHEST)

def rms_scale(values, gain):
    return values * lax.rsqrt(lax.optimization_barrier(jnp.mean(values * values, axis=-1, keepdims=True)) + 1e-06) * gain

def group_norm(values):
    centred = values - lax.optimization_barrier(jnp.mean(values, axis=-1, keepdims=True))
    return centred * lax.rsqrt(lax.optimization_barrier(jnp.mean(centred * centred, axis=-1, keepdims=True)) + 1.0)

def rotary_tables(length, width):
    half = width // 2
    frequency = 10000.0 ** (-2.0 * jnp.arange(half, dtype=jnp.int32).astype(jnp.float32) / width)
    angle = jnp.arange(length, dtype=jnp.int32).astype(jnp.float32)[:, None] * frequency[None, :]
    return (jnp.cos(angle), jnp.sin(angle))

def rotate(values, cosine, sine):
    half = values.shape[-1] // 2
    first = values[..., :half]
    second = values[..., half:]
    return jnp.concatenate([first * cosine - second * sine, second * cosine + first * sine], axis=-1)

def decay_mask(segments, first_head, count):
    length = segments.shape[-1]
    position = jnp.arange(length, dtype=jnp.int32)
    distance = position[:, None] - position[None, :]
    same = (distance >= 0) & (segments.astype(jnp.int32)[..., :, None] == segments.astype(jnp.int32)[..., None, :])
    heads = (jnp.arange(count, dtype=jnp.int32) + first_head).astype(jnp.float32)
    rates = jnp.log1p(-jnp.exp2(-5.0 - heads))
    steps_back = jnp.maximum(distance, 0).astype(jnp.float32)
    decay = jnp.exp(rates[:, None, None] * steps_back[None, :, :])
    return jnp.where(same[..., None, :, :], decay, jnp.zeros((), jnp.float32))

def retain(items):
    query, keys, values, segments = items
    raw = low_back(jnp.einsum('nhk,mhk->hnm', query, keys, precision=HIGHEST))
    scores = low(raw * decay_mask(segments, 0, query.shape[1]))
    return low_back(jnp.einsum('hnm,mhv->nhv', scores, values, precision=HIGHEST))

def block(resid_in, segments, gain_first, query_weight, key_weight, value_weight, gate_weight, out_weight, gain_second, mlp_gate_weight, mlp_up_weight, mlp_down_weight):
    groups, length, width = resid_in.shape
    normed = low(rms_scale(resid_in, gain_first))
    query_pre = low_back(multiply(normed, query_weight)).reshape(groups, length, HEADS, KEY)
    key_pre = low_back(multiply(normed, key_weight)).reshape(groups, length, HEADS, KEY)
    values = low(low_back(multiply(normed, value_weight))).reshape(groups, length, HEADS, VAL)
    gate_pre = low_back(multiply(normed, gate_weight))
    cosine, sine = rotary_tables(length, KEY)
    cosine = cosine[:, None, :]
    sine = sine[:, None, :]
    query = low(rotate(query_pre, cosine, sine) * KEY ** (-0.5))
    keys = low(rotate(key_pre, cosine, sine))
    retained = lax.map(jax.checkpoint(retain), (query, keys, values, segments))
    mixed = low(group_norm(retained).reshape(groups, length, HEADS * VAL) * jax.nn.silu(gate_pre))
    resid_mid = resid_in + low_back(multiply(mixed, out_weight))
    normed_mid = low(rms_scale(resid_mid, gain_second))
    gate_hidden = low_back(multiply(normed_mid, mlp_gate_weight))
    up_hidden = low_back(multiply(normed_mid, mlp_up_weight))
    hidden = low(jax.nn.gelu(gate_hidden, approximate=True) * up_hidden)
    return resid_mid + low_back(multiply(hidden, mlp_down_weight))

def reference(hidden_in, out_grad, segment_ids, norm1_gain, w_query, w_key, w_value, w_gate, w_out, norm2_gain, w_mlp_gate, w_mlp_up, w_mlp_down):
    weights = tuple((weight.astype(jnp.float32) for weight in (norm1_gain, w_query, w_key, w_value, w_gate, w_out, norm2_gain, w_mlp_gate, w_mlp_up, w_mlp_down)))
    group = 4 if NSEQ % 4 == 0 else 1
    steps = NSEQ // group
    inputs = hidden_in.astype(jnp.float32).reshape(steps, group, LEN, D)
    cotangents = out_grad.astype(jnp.float32).reshape(steps, group, LEN, D)
    segment_rows = segment_ids.astype(jnp.int32).reshape(steps, group, LEN)

    def step(totals, items):
        resid, cotangent, seg_rows = items

        def forward(resid_value, *params):
            return block(resid_value, seg_rows, *params)
        result, pull = jax.vjp(forward, resid, *weights)
        grads = pull(cotangent)
        new_totals = tuple((total + grad.astype(jnp.float32) for total, grad in zip(totals, grads[1:])))
        return (new_totals, (result.astype(jnp.bfloat16), grads[0].astype(jnp.float32)))
    zeros = tuple((jnp.zeros(weight.shape, jnp.float32) for weight in weights))
    totals, (results, input_grads) = lax.scan(step, zeros, (inputs, cotangents, segment_rows))
    return (results.reshape(NSEQ, LEN, D), input_grads.reshape(NSEQ, LEN, D), totals[0], totals[1], totals[2], totals[3], totals[4], totals[5], totals[6], totals[7], totals[8], totals[9])
```

```python
import jax
import jax.numpy as jnp
from jax import lax
from jax.sharding import PartitionSpec as P

KEY = 256
VAL = 432
LOW = jnp.bfloat16
WIDE = jnp.float32


def multiply(left, right):
    return jnp.dot(left, right, preferred_element_type=WIDE)


def multiply_left(left, right):
    return lax.dot_general(left, right, (((0,), (0,)), ((), ())), preferred_element_type=WIDE)


def multiply_right(left, right):
    return lax.dot_general(left, right, (((1,), (1,)), ((), ())), preferred_element_type=WIDE)


def rms_scale(values, gain):
    return values * lax.rsqrt(jnp.mean(values * values, axis=-1, keepdims=True) + 1e-06) * gain


def group_norm(values):
    centred = values - jnp.mean(values, axis=-1, keepdims=True)
    return centred * lax.rsqrt(jnp.mean(centred * centred, axis=-1, keepdims=True) + 1.0)


def rotary_tables(position, width):
    half = width // 2
    frequency = 10000.0 ** (-2.0 * jnp.arange(half, dtype=jnp.int32).astype(WIDE) / width)
    angle = position.astype(WIDE)[:, None] * frequency[None, :]
    return (jnp.cos(angle), jnp.sin(angle))


def rotate(values, cosine, sine):
    half = values.shape[-1] // 2
    first = values[..., :half]
    second = values[..., half:]
    return jnp.concatenate(
        [first * cosine - second * sine, second * cosine + first * sine], axis=-1
    )


def decay_mask(position, segments, first_head, count):
    distance = position[:, None] - position[None, :]
    same = (distance >= 0) & (segments[:, None] == segments[None, :])
    heads = (jnp.arange(count, dtype=jnp.int32) + first_head).astype(WIDE)
    rates = jnp.log1p(-jnp.exp2(-5.0 - heads))
    steps_back = jnp.maximum(distance, 0).astype(WIDE)
    decay = jnp.exp(rates[:, None, None] * steps_back[None, :, :])
    return jnp.where(same[None, :, :], decay, jnp.zeros((), WIDE))


def swap_side(value):
    count = lax.axis_size("dp")
    return lax.ppermute(value, "dp", [(i, i ^ 1) for i in range(count)])


def shift_line(value, step):
    count = lax.axis_size("dp")
    lines = count // 2
    pairs = [(i, 2 * ((i // 2 + step) % lines) + i % 2) for i in range(count)]
    return lax.ppermute(value, "dp", pairs)


def swap_tensor(value, bit):
    count = lax.axis_size("tensor")
    return lax.ppermute(value, "tensor", [(i, i ^ bit) for i in range(count)])


def gather_dp(shard, axis):
    lines = lax.axis_size("dp") // 2
    near = [shard] + [shift_line(shard, step) for step in range(1, lines)]
    far = [swap_side(block) for block in near]
    return jnp.concatenate(near + far, axis=axis)


def gather_tensor(block):
    beside = swap_tensor(block, 1)
    across = swap_tensor(block, 2)
    beyond = swap_tensor(across, 1)
    return jnp.concatenate([block, beside, across, beyond], axis=0)


def scatter_tensor(partial):
    rows = partial.shape[0] // 4
    one, two, three, four = [partial[k * rows : (k + 1) * rows] for k in range(4)]
    got = swap_tensor(jnp.concatenate([two, four], axis=0).astype(LOW), 1).astype(WIDE)
    across = swap_tensor((three + got[rows:]).astype(LOW), 2).astype(WIDE)
    return (one + got[:rows]) + across


def scatter_dp(near_product, far_product, axis):
    lines = lax.axis_size("dp") // 2
    got = swap_side(far_product().astype(LOW)).astype(WIDE)
    total = near_product() + got
    width = total.shape[axis] // lines
    parts = [lax.slice_in_dim(total, k * width, (k + 1) * width, axis=axis) for k in range(lines)]
    result = parts[0]
    for step in range(1, lines):
        result = result + shift_line(parts[step].astype(LOW), -step).astype(WIDE)
    return result


def on_device(
    hidden_in,
    out_grad,
    segment_ids,
    norm1_gain,
    w_query,
    w_key,
    w_value,
    w_gate,
    w_out,
    norm2_gain,
    w_mlp_gate,
    w_mlp_up,
    w_mlp_down,
):
    _, rows, width = hidden_in.shape
    parts = lax.axis_size("dp")
    lines = parts // 2
    slice_width = width // parts
    half = width // 2
    me = lax.axis_index("dp")
    line, side = me // 2, me % 2
    own = lax.axis_index("tensor")
    members = lax.axis_size("tensor")
    length = rows * members

    def to_own_order(value):
        owners = [
            2 * ((line + lines - step) % lines) + (side ^ flip)
            for flip in range(2)
            for step in range(lines)
        ]
        return jnp.concatenate(
            [
                lax.dynamic_slice_in_dim(value, owner * slice_width, slice_width, axis=1)
                for owner in owners
            ],
            axis=1,
        )

    def from_own_order(value):
        places = [
            (side ^ (k % 2)) * lines + (line + lines - k // 2) % lines for k in range(parts)
        ]
        return jnp.concatenate(
            [
                lax.dynamic_slice_in_dim(value, place * slice_width, slice_width, axis=1)
                for place in places
            ],
            axis=1,
        )

    gains = gather_dp(jnp.stack([norm1_gain, norm2_gain]), 1).astype(WIDE)
    gain_first, gain_second = gains[0], gains[1]
    heads_here = w_query.shape[1] // KEY
    first_head = own * heads_here
    key_columns = w_query.shape[1]
    value_columns = w_value.shape[1]
    feed_columns = w_mlp_gate.shape[1]

    qk_weight = gather_dp(jnp.concatenate([w_query, w_key], axis=1), 0)
    vg_weight = gather_dp(jnp.concatenate([w_value, w_gate], axis=1), 0)
    out_weight = gather_dp(w_out, 1)
    gu_weight = gather_dp(jnp.concatenate([w_mlp_gate, w_mlp_up], axis=1), 0)
    down_weight = gather_dp(w_mlp_down, 1)

    resid_in = to_own_order(hidden_in.reshape(rows, width)).astype(WIDE)
    grad_local = to_own_order(out_grad.reshape(rows, width))
    normed = gather_tensor(rms_scale(resid_in, gain_first).astype(LOW))
    grad_full = gather_tensor(grad_local)

    position = jnp.concatenate(
        [(own ^ k) * rows + jnp.arange(rows, dtype=jnp.int32) for k in range(members)]
    )
    segments = jnp.concatenate(
        [
            lax.dynamic_slice_in_dim(segment_ids.reshape(length), (own ^ k) * rows, rows)
            for k in range(members)
        ]
    )
    cosine, sine = rotary_tables(position, KEY)
    cosine = cosine[:, None, :]
    sine = sine[:, None, :]

    qk_pre = multiply(normed, qk_weight).reshape(length, 2 * heads_here, KEY)
    turned = rotate(qk_pre, cosine, sine)
    query = (turned[:, :heads_here] * KEY ** (-0.5)).astype(LOW)
    keys = turned[:, heads_here:].astype(LOW)
    vg_pre = multiply(normed, vg_weight)
    values = vg_pre[:, :value_columns].astype(LOW).reshape(length, heads_here, VAL)
    gate_pre = vg_pre[:, value_columns:]

    def retention_scores():
        mask = decay_mask(position, segments, first_head, heads_here)
        raw = jnp.einsum("nhk,mhk->hnm", query, keys, preferred_element_type=WIDE)
        return (raw * mask, mask)

    weighted, mask = retention_scores()
    scores_low = weighted.astype(LOW)
    retained = jnp.einsum(
        "hnm,mhv->nhv", scores_low, values, preferred_element_type=WIDE
    ).reshape(length, value_columns)

    def gate_mix(retained_in, gate_in):
        grouped = group_norm(retained_in.reshape(length, heads_here, VAL)).reshape(
            retained_in.shape
        )
        return grouped * jax.nn.silu(gate_in)

    mixed = gate_mix(retained, gate_pre).astype(LOW)
    resid_mid = resid_in + scatter_tensor(multiply(mixed, out_weight))
    normed_mid = gather_tensor(rms_scale(resid_mid, gain_second).astype(LOW))
    gu_hidden = multiply(normed_mid, gu_weight)
    gate_hidden = gu_hidden[:, :feed_columns]
    up_hidden = gu_hidden[:, feed_columns:]

    def gelu_mix(gate_in, up_in):
        return jax.nn.gelu(gate_in, approximate=True) * up_in

    hidden = gelu_mix(gate_hidden, up_hidden).astype(LOW)
    down_grad = scatter_dp(
        lambda: multiply_left(hidden, grad_full[:, :half]),
        lambda: multiply_left(hidden, grad_full[:, half:]),
        1,
    )
    resid_out = resid_mid + scatter_tensor(multiply(hidden, down_weight))
    hidden_out = from_own_order(resid_out.astype(LOW)).reshape(hidden_in.shape)

    hidden_grad = multiply_right(grad_full, down_weight)
    _, pull_mix = jax.vjp(gelu_mix, gate_hidden, up_hidden)
    gate_hidden_grad, up_hidden_grad = pull_mix(hidden_grad)
    gu_low = jnp.concatenate([gate_hidden_grad.astype(LOW), up_hidden_grad.astype(LOW)], axis=1)
    gu_grad = scatter_dp(
        lambda: multiply_left(normed_mid[:, :half], gu_low),
        lambda: multiply_left(normed_mid[:, half:], gu_low),
        0,
    )
    normed_mid_grad = scatter_tensor(multiply_right(gu_low, gu_weight))
    _, pull_second = jax.vjp(rms_scale, resid_mid, gain_second)
    mid_from_norm, gain_second_part = pull_second(normed_mid_grad)
    resid_mid_grad = grad_local.astype(WIDE) + mid_from_norm
    mid_full = gather_tensor(resid_mid_grad.astype(LOW))
    out_weight_grad = scatter_dp(
        lambda: multiply_left(mixed, mid_full[:, :half]),
        lambda: multiply_left(mixed, mid_full[:, half:]),
        1,
    )
    mixed_grad = multiply_right(mid_full, out_weight)
    _, pull_gate = jax.vjp(gate_mix, retained, gate_pre)
    retained_grad, gate_pre_grad = pull_gate(mixed_grad)
    retained_low = retained_grad.astype(LOW).reshape(length, heads_here, VAL)
    gate_pre_low = gate_pre_grad.astype(LOW)
    score_grad = jnp.einsum("nhv,mhv->hnm", retained_low, values, preferred_element_type=WIDE)
    raw_grad = (score_grad * mask).astype(LOW)
    query_grad = jnp.einsum("hnm,mhk->nhk", raw_grad, keys, preferred_element_type=WIDE)
    key_grad = jnp.einsum("hnm,nhk->mhk", raw_grad, query, preferred_element_type=WIDE)
    value_grad = (
        jnp.einsum("hnm,nhv->mhv", scores_low, retained_low, preferred_element_type=WIDE)
        .astype(LOW)
        .reshape(length, value_columns)
    )
    query_pre_grad = (
        (rotate(query_grad, cosine, -sine) * KEY ** (-0.5)).astype(LOW).reshape(length, key_columns)
    )
    key_pre_grad = rotate(key_grad, cosine, -sine).astype(LOW).reshape(length, key_columns)
    vg_low = jnp.concatenate([value_grad, gate_pre_low], axis=1)
    qk_low = jnp.concatenate([query_pre_grad, key_pre_grad], axis=1)
    vg_grad = scatter_dp(
        lambda: multiply_left(normed[:, :half], vg_low),
        lambda: multiply_left(normed[:, half:], vg_low),
        0,
    )
    qk_grad = scatter_dp(
        lambda: multiply_left(normed[:, :half], qk_low),
        lambda: multiply_left(normed[:, half:], qk_low),
        0,
    )
    normed_grad = scatter_tensor(
        multiply_right(vg_low, vg_weight) + multiply_right(qk_low, qk_weight)
    )
    _, pull_first = jax.vjp(rms_scale, resid_in, gain_first)
    in_from_norm, gain_first_part = pull_first(normed_grad)
    in_grad = from_own_order(resid_mid_grad + in_from_norm).reshape(hidden_in.shape)

    gain_part = jnp.stack([gain_first_part, gain_second_part])
    gain_part = gain_part + swap_tensor(gain_part, 1)
    gain_part = gain_part + swap_tensor(gain_part, 2)
    gain_part = gain_part[:, :half] + swap_side(gain_part[:, half:])
    gain_total = gain_part[:, :slice_width]
    for step in range(1, lines):
        gain_total = gain_total + shift_line(
            gain_part[:, step * slice_width : (step + 1) * slice_width], -step
        )
    return (
        hidden_out,
        in_grad,
        gain_total[0],
        qk_grad[:, :key_columns],
        qk_grad[:, key_columns:],
        vg_grad[:, :value_columns],
        vg_grad[:, value_columns:],
        out_weight_grad,
        gain_total[1],
        gu_grad[:, :feed_columns],
        gu_grad[:, feed_columns:],
        down_grad,
    )


def solution(mesh):
    return jax.shard_map(
        on_device,
        mesh=mesh,
        in_specs=(
            P("dp", "tensor", None),
            P("dp", "tensor", None),
            P("dp", None),
            P("dp"),
            P("dp", "tensor"),
            P("dp", "tensor"),
            P("dp", "tensor"),
            P("dp", "tensor"),
            P("tensor", "dp"),
            P("dp"),
            P("dp", "tensor"),
            P("dp", "tensor"),
            P("tensor", "dp"),
        ),
        out_specs=(
            P("dp", "tensor", None),
            P("dp", "tensor", None),
            P("dp"),
            P("dp", "tensor"),
            P("dp", "tensor"),
            P("dp", "tensor"),
            P("dp", "tensor"),
            P("tensor", "dp"),
            P("dp"),
            P("dp", "tensor"),
            P("dp", "tensor"),
            P("tensor", "dp"),
        ),
        check_vma=False,
    )
```

```python
import functools

import jax
import jax.numpy as jnp
from jax import lax
from jax.experimental import pallas as pl
from jax.experimental.pallas import tpu as pltpu
from jax.sharding import PartitionSpec as P

KEY = 256
VAL = 432
LOW = jnp.bfloat16
WIDE = jnp.float32


def multiply(left, right):
    return jnp.dot(left, right, preferred_element_type=WIDE)


def multiply_left(left, right):
    return lax.dot_general(left, right, (((0,), (0,)), ((), ())), preferred_element_type=WIDE)


def multiply_right(left, right):
    return lax.dot_general(left, right, (((1,), (1,)), ((), ())), preferred_element_type=WIDE)


def rms_scale(values, gain):
    return values * lax.rsqrt(jnp.mean(values * values, axis=-1, keepdims=True) + 1e-06) * gain


def group_norm(values):
    centred = values - jnp.mean(values, axis=-1, keepdims=True)
    return centred * lax.rsqrt(jnp.mean(centred * centred, axis=-1, keepdims=True) + 1.0)


def rotary_tables(position, width):
    half = width // 2
    frequency = 10000.0 ** (-2.0 * jnp.arange(half, dtype=jnp.int32).astype(WIDE) / width)
    angle = position.astype(WIDE)[:, None] * frequency[None, :]
    return (jnp.cos(angle), jnp.sin(angle))


def rotate(values, cosine, sine):
    half = values.shape[-1] // 2
    first = values[..., :half]
    second = values[..., half:]
    return jnp.concatenate(
        [first * cosine - second * sine, second * cosine + first * sine], axis=-1
    )


def decay_mask(position, segments, first_head, count):
    distance = position[:, None] - position[None, :]
    same = (distance >= 0) & (segments[:, None] == segments[None, :])
    heads = (jnp.arange(count, dtype=jnp.int32) + first_head).astype(WIDE)
    rates = jnp.log1p(-jnp.exp2(-5.0 - heads))
    steps_back = jnp.maximum(distance, 0).astype(WIDE)
    decay = jnp.exp(rates[:, None, None] * steps_back[None, :, :])
    return jnp.where(same[None, :, :], decay, jnp.zeros((), WIDE))


def by_place():
    count = lax.axis_size("dp")
    return [list(range(0, count, 2)) + list(range(1, count, 2))]


def gather_dp(shard, axis):
    return lax.all_gather(shard, "dp", axis=axis, tiled=True, axis_index_groups=by_place())


def scatter_dp(value, axis):
    return lax.psum_scatter(
        value, "dp", scatter_dimension=axis, tiled=True, axis_index_groups=by_place()
    )


def swap_tensor(value, bit):
    count = lax.axis_size("tensor")
    return lax.ppermute(value, "tensor", [(i, i ^ bit) for i in range(count)])


def after(value, earlier):
    return value if earlier is None else lax.optimization_barrier((value, earlier))[0]


def gather_tensor(block):
    beside = swap_tensor(block, 1)
    across = swap_tensor(block, 2)
    beyond = swap_tensor(across, 1)
    return jnp.concatenate([block, beside, across, beyond], axis=0)


def scatter_tensor(partial):
    rows = partial.shape[0] // 4
    one, two, three, four = [partial[k * rows : (k + 1) * rows] for k in range(4)]
    got = swap_tensor(jnp.concatenate([two, four], axis=0).astype(LOW), 1).astype(WIDE)
    across = swap_tensor((three + got[rows:]).astype(LOW), 2).astype(WIDE)
    return (one + got[:rows]) + across


MESH = pl.DeviceIdType.MESH
ANY = pl.BlockSpec(memory_space=pl.ANY)
INSIDE = pl.BlockSpec(memory_space=pltpu.VMEM)
ROOM = 60 * 1024 * 1024


def greet(peers):
    barrier = pltpu.get_barrier_semaphore()
    for peer in peers:
        pl.semaphore_signal(barrier, inc=1, device_id=peer, device_id_type=MESH)
    pl.semaphore_wait(barrier, len(peers))


def gather_kernel(lines, members, count, *refs):
    hidden_ref, grad_ref, gain_ref = refs[:3]
    shards = refs[3 : 3 + count]
    normed_all, grad_all, gain_all = refs[3 + count : 6 + count]
    wholes = refs[6 + count : 6 + 2 * count]
    normed_own, line_send, line_recv, side_send, side_recv = refs[6 + 2 * count : 11 + 2 * count]
    near_send, near_recv, gain_send, gain_recv, home = refs[11 + 2 * count :]
    parts = 2 * lines
    me = lax.axis_index("dp")
    line, side = me // 2, lax.rem(me, 2)
    own = lax.axis_index("tensor")
    rest = lax.rem(own, 2)
    half = own // 2
    partners = [
        {"tensor": 2 * lax.rem(half + k // 2, 2) + lax.rem(rest + k % 2, 2)}
        for k in range(1, members)
    ]
    others = [{"dp": lax.rem(me + k, parts)} for k in range(1, parts)]
    greet(others + partners)
    opposite = {"dp": 2 * line + (1 - side)}
    here = side * lines + line

    def remote(source, target, send, recv, device):
        return pltpu.make_async_remote_copy(
            src_ref=source,
            dst_ref=target,
            send_sem=send,
            recv_sem=recv,
            device_id=device,
            device_id_type=MESH,
        )

    gains = []
    for k in range(1, parts):
        gains.append(
            remote(
                gain_ref,
                gain_all.at[here],
                gain_send.at[k],
                gain_recv.at[k],
                others[k - 1],
            )
        )
    for copy in gains:
        copy.start()
    gain_all[here] = gain_ref[...]

    copies = []
    for k in range(1, members):
        copy = remote(
            grad_ref, grad_all.at[k], near_send.at[0, k], near_recv.at[0, k], partners[k - 1]
        )
        copies.append(copy)
    local = [pltpu.make_async_copy(grad_ref, grad_all.at[0], home.at[0])]
    local[0].start()

    steps = {}
    across = {}

    def start_lines(w):
        for step in range(1, lines):
            copy = remote(
                shards[w],
                wholes[w].at[here],
                line_send.at[w, step],
                line_recv.at[w, step],
                {"dp": 2 * lax.rem(line + step, lines) + side},
            )
            copy.start()
            steps[w, step] = copy
        copy = remote(
            shards[w], wholes[w].at[here], side_send.at[w, 0], side_recv.at[w, 0], opposite
        )
        copy.start()
        across[w, 0] = copy
        copy = pltpu.make_async_copy(shards[w], wholes[w].at[here], home.at[2 + w])
        copy.start()
        local.append(copy)

    start_lines(0)
    start_lines(1)

    values = hidden_ref[...].astype(WIDE)
    scaled = values * lax.rsqrt(jnp.mean(values * values, axis=-1, keepdims=True) + 1e-06)
    for copy in gains:
        copy.wait()
    width = gain_ref.shape[1]
    for p in range(parts):
        columns = slice(p * width, (p + 1) * width)
        normed_own[:, columns] = (scaled[:, columns] * gain_all[p][:1]).astype(LOW)
    for k in range(1, members):
        copy = remote(
            normed_own, normed_all.at[k], near_send.at[1, k], near_recv.at[1, k], partners[k - 1]
        )
        copy.start()
        copies.insert(0, copy)
    copy = pltpu.make_async_copy(normed_own, normed_all.at[0], home.at[1])
    copy.start()
    local.append(copy)
    for copy in copies[members - 1 :]:
        copy.start()

    for w in range(count):
        if w + 2 < count:
            start_lines(w + 2)
        for step in range(1, lines):
            steps[w, step].wait_recv()
            place = side * lines + lax.rem(line + lines - step, lines)
            copy = remote(
                wholes[w].at[place],
                wholes[w].at[place],
                side_send.at[w, step],
                side_recv.at[w, step],
                opposite,
            )
            copy.start()
            across[w, step] = copy
    for w in range(count):
        for step in range(1, lines):
            steps[w, step].wait_send()
        for step in range(lines):
            across[w, step].wait()
    for copy in copies:
        copy.wait()
    for copy in local:
        copy.wait()


def gather_all(hidden, grad, gains, shards, lines, members):
    count = len(shards)
    parts = 2 * lines
    rows, width = hidden.shape
    sent = sum(shard.size for shard in shards) * parts * 2
    return pl.pallas_call(
        functools.partial(gather_kernel, lines, members, count),
        out_shape=[
            jax.ShapeDtypeStruct((members, rows, width), LOW),
            jax.ShapeDtypeStruct((members, rows, width), LOW),
            jax.ShapeDtypeStruct((parts,) + gains.shape, WIDE),
        ]
        + [jax.ShapeDtypeStruct((parts,) + shard.shape, LOW) for shard in shards],
        in_specs=[INSIDE, ANY, INSIDE] + [ANY] * count,
        out_specs=[ANY, ANY, INSIDE] + [ANY] * count,
        scratch_shapes=[
            pltpu.VMEM((rows, width), LOW),
            pltpu.SemaphoreType.DMA((count, lines)),
            pltpu.SemaphoreType.DMA((count, lines)),
            pltpu.SemaphoreType.DMA((count, lines)),
            pltpu.SemaphoreType.DMA((count, lines)),
            pltpu.SemaphoreType.DMA((2, members)),
            pltpu.SemaphoreType.DMA((2, members)),
            pltpu.SemaphoreType.DMA((parts,)),
            pltpu.SemaphoreType.DMA((parts,)),
            pltpu.SemaphoreType.DMA((2 + count,)),
        ],
        compiler_params=pltpu.CompilerParams(
            collective_id=0, has_side_effects=True, vmem_limit_bytes=32 * 1024 * 1024
        ),
        cost_estimate=pl.CostEstimate(flops=0, bytes_accessed=20 * sent, transcendentals=0),
        name="gather_all",
    )(hidden, grad, gains, *shards)


def scatter_kernel(lines, count, *refs):
    left_ref = refs[0]
    rights = refs[1 : 1 + count]
    outs = refs[1 + count : 1 + 2 * count]
    buffers = refs[1 + 2 * count :]
    far_held, far_got, near_held, near_got = [
        buffers[k * count : (k + 1) * count] for k in range(4)
    ]
    side_send, side_recv, line_send, line_recv = buffers[4 * count :]
    me = lax.axis_index("dp")
    line, side = me // 2, lax.rem(me, 2)
    opposite = {"dp": 2 * line + (1 - side)}
    greet(
        [{"dp": 2 * lax.rem(line + step, lines) + side} for step in range(1, lines)] + [opposite]
    )
    rows = outs[0].shape[0]

    def product(w, place):
        block = left_ref[pl.ds(pl.multiple_of(place * rows, rows), rows), :]
        return jnp.dot(block, rights[w][...], preferred_element_type=WIDE)

    def far_copy(w, place):
        return pltpu.make_async_remote_copy(
            src_ref=far_held[w].at[place],
            dst_ref=far_got[w].at[place],
            send_sem=side_send.at[w, place],
            recv_sem=side_recv.at[w, place],
            device_id=opposite,
            device_id_type=MESH,
        )

    def near_copy(w, step):
        return pltpu.make_async_remote_copy(
            src_ref=near_held[w].at[step],
            dst_ref=near_got[w].at[step],
            send_sem=line_send.at[w, step],
            recv_sem=line_recv.at[w, step],
            device_id={"dp": 2 * lax.rem(line + step, lines) + side},
            device_id_type=MESH,
        )

    def send_far(w):
        def body(step, carry):
            place = lax.rem(line + step + 1, lines)
            far_held[w][place] = product(w, (1 - side) * lines + place).astype(LOW)
            far_copy(w, place).start()
            return carry

        lax.fori_loop(0, lines, body, 0)

    def send_near(w):
        def body(step, carry):
            place = lax.rem(line + step, lines)
            part = product(w, side * lines + place)
            far_copy(w, place).wait_recv()
            near_held[w][step] = (part + far_got[w][place].astype(WIDE)).astype(LOW)
            near_copy(w, step).start()
            return carry

        lax.fori_loop(1, lines, body, 0)
        part = product(w, side * lines + line)
        far_copy(w, line).wait_recv()
        outs[w][...] = part + far_got[w][line].astype(WIDE)

    def finish(w):
        def body(step, carry):
            near_copy(w, step).wait_recv()
            outs[w][...] += near_got[w][step].astype(WIDE)
            near_copy(w, step).wait_send()
            return carry

        lax.fori_loop(1, lines, body, 0)

        def sent(place, carry):
            far_copy(w, place).wait_send()
            return carry

        lax.fori_loop(0, lines, sent, 0)

    send_far(0)
    for w in range(count):
        if w + 1 < count:
            send_far(w + 1)
        send_near(w)
    for w in range(count):
        finish(w)


def scatter_rows(left, rights, lines, tag):
    count = len(rights)
    rows = left.shape[0] // (2 * lines)
    blocks = [(lines, rows, right.shape[1]) for right in rights]
    columns = sum(right.shape[1] for right in rights)
    return pl.pallas_call(
        functools.partial(scatter_kernel, lines, count),
        out_shape=[jax.ShapeDtypeStruct(block[1:], WIDE) for block in blocks],
        in_specs=[INSIDE] * (1 + count),
        out_specs=[INSIDE] * count,
        scratch_shapes=[pltpu.VMEM(block, LOW) for _ in range(4) for block in blocks]
        + [pltpu.SemaphoreType.DMA((count, lines))] * 4,
        compiler_params=pltpu.CompilerParams(
            collective_id=tag, has_side_effects=True, vmem_limit_bytes=ROOM
        ),
        cost_estimate=pl.CostEstimate(
            flops=2 * left.size * columns,
            bytes_accessed=40 * left.shape[0] * columns,
            transcendentals=0,
        ),
        name="scatter_rows",
    )(left, *rights)


def on_device(
    hidden_in,
    out_grad,
    segment_ids,
    norm1_gain,
    w_query,
    w_key,
    w_value,
    w_gate,
    w_out,
    norm2_gain,
    w_mlp_gate,
    w_mlp_up,
    w_mlp_down,
):
    _, rows, width = hidden_in.shape
    parts = lax.axis_size("dp")
    lines = parts // 2
    slice_width = width // parts
    own = lax.axis_index("tensor")
    members = lax.axis_size("tensor")
    length = rows * members

    def to_places(value):
        blocks = [value[:, k * slice_width : (k + 1) * slice_width] for k in by_place()[0]]
        return jnp.concatenate(blocks, axis=1)

    def from_places(value):
        blocks = [value[:, k * slice_width : (k + 1) * slice_width] for k in range(parts)]
        return jnp.concatenate([blocks[k // 2 + k % 2 * lines] for k in range(parts)], axis=1)

    heads_here = w_query.shape[1] // KEY
    first_head = own * heads_here
    key_columns = w_query.shape[1]
    value_columns = w_value.shape[1]

    resid_low = to_places(hidden_in.reshape(rows, width))
    grad_local = to_places(out_grad.reshape(rows, width))
    gain_rows = jnp.concatenate(
        [norm1_gain[None], norm2_gain[None], jnp.zeros((6, slice_width), LOW)]
    ).astype(WIDE)
    normed, grad_full, gains, *gathered = gather_all(
        resid_low,
        grad_local,
        gain_rows,
        [w_query, w_key, w_value, w_gate, w_out],
        lines,
        members,
    )
    normed = normed.reshape(length, width)
    grad_full = grad_full.reshape(length, width)
    gain_first = gains[:, 0].reshape(width)
    gain_second = gains[:, 1].reshape(width)
    query_weight, key_weight, value_weight, gate_weight = [
        whole.reshape(width, whole.shape[2]) for whole in gathered[:4]
    ]
    out_weight = jnp.concatenate([gathered[4][k] for k in range(parts)], axis=1)
    resid_in = resid_low.astype(WIDE)
    w_mlp_gate = after(w_mlp_gate, gains)
    w_mlp_up = after(w_mlp_up, gains)
    w_mlp_down = after(w_mlp_down, gains)
    mlp_gate_weight = gather_dp(w_mlp_gate, 0)
    mlp_up_weight = gather_dp(w_mlp_up, 0)
    down_weight = gather_dp(w_mlp_down, 1)

    position = jnp.concatenate(
        [(own ^ k) * rows + jnp.arange(rows, dtype=jnp.int32) for k in range(members)]
    )
    segments = jnp.concatenate(
        [
            lax.dynamic_slice_in_dim(segment_ids.reshape(length), (own ^ k) * rows, rows)
            for k in range(members)
        ]
    )
    cosine, sine = rotary_tables(position, KEY)
    cosine = cosine[:, None, :]
    sine = sine[:, None, :]

    key_shape = (length, heads_here, KEY)
    query_pre = multiply(normed, query_weight).reshape(key_shape)
    key_pre = multiply(normed, key_weight).reshape(key_shape)
    query = (rotate(query_pre, cosine, sine) * KEY ** (-0.5)).astype(LOW)
    keys = rotate(key_pre, cosine, sine).astype(LOW)
    values = multiply(normed, value_weight).astype(LOW).reshape(length, heads_here, VAL)
    gate_pre = multiply(normed, gate_weight)

    def retention_scores():
        mask = decay_mask(position, segments, first_head, heads_here)
        raw = jnp.einsum("nhk,mhk->hnm", query, keys, preferred_element_type=WIDE)
        return (raw * mask, mask)

    weighted, mask = retention_scores()
    scores_low = weighted.astype(LOW)
    retained = jnp.einsum(
        "hnm,mhv->nhv", scores_low, values, preferred_element_type=WIDE
    ).reshape(length, value_columns)

    def gate_mix(retained_in, gate_in):
        grouped = group_norm(retained_in.reshape(length, heads_here, VAL)).reshape(
            retained_in.shape
        )
        return grouped * jax.nn.silu(gate_in)

    mixed = gate_mix(retained, gate_pre).astype(LOW)
    resid_mid = resid_in + scatter_tensor(multiply(mixed, out_weight))
    normed_mid = gather_tensor(rms_scale(resid_mid, gain_second).astype(LOW))
    gate_hidden = multiply(normed_mid, mlp_gate_weight)
    up_hidden = multiply(normed_mid, mlp_up_weight)

    def gelu_mix(gate_in, up_in):
        return jax.nn.gelu(gate_in, approximate=True) * up_in

    hidden = gelu_mix(gate_hidden, up_hidden).astype(LOW)
    def grad_of_columns(left, right):
        return scatter_dp(multiply_left(left, right).astype(LOW), 1).astype(WIDE)

    def grad_of_rows(left, right):
        return scatter_dp(multiply_left(left, right).astype(LOW), 0).astype(WIDE)

    down_grad = grad_of_columns(hidden, grad_full)
    resid_out = resid_mid + scatter_tensor(multiply(hidden, down_weight))
    hidden_out = from_places(resid_out.astype(LOW)).reshape(hidden_in.shape)

    hidden_grad = multiply_right(grad_full, down_weight)
    _, pull_mix = jax.vjp(gelu_mix, gate_hidden, up_hidden)
    gate_hidden_grad, up_hidden_grad = pull_mix(hidden_grad)
    gate_hidden_low = gate_hidden_grad.astype(LOW)
    up_hidden_low = up_hidden_grad.astype(LOW)
    mlp_gate_grad = grad_of_rows(normed_mid, gate_hidden_low)
    mlp_up_grad = grad_of_rows(normed_mid, up_hidden_low)
    normed_mid_grad = scatter_tensor(
        multiply_right(gate_hidden_low, mlp_gate_weight)
        + multiply_right(up_hidden_low, mlp_up_weight)
    )
    _, pull_second = jax.vjp(rms_scale, resid_mid, gain_second)
    mid_from_norm, gain_second_part = pull_second(normed_mid_grad)
    resid_mid_grad = grad_local.astype(WIDE) + mid_from_norm
    mid_full = gather_tensor(resid_mid_grad.astype(LOW))
    out_weight_grad = grad_of_columns(mixed, mid_full)
    mixed_grad = multiply_right(mid_full, out_weight)
    _, pull_gate = jax.vjp(gate_mix, retained, gate_pre)
    retained_grad, gate_pre_grad = pull_gate(mixed_grad)
    retained_low = retained_grad.astype(LOW).reshape(length, heads_here, VAL)
    gate_pre_low = gate_pre_grad.astype(LOW)
    score_grad = jnp.einsum("nhv,mhv->hnm", retained_low, values, preferred_element_type=WIDE)
    raw_grad = (score_grad * mask).astype(LOW)
    query_grad = jnp.einsum("hnm,mhk->nhk", raw_grad, keys, preferred_element_type=WIDE)
    key_grad = jnp.einsum("hnm,nhk->mhk", raw_grad, query, preferred_element_type=WIDE)
    value_grad = (
        jnp.einsum("hnm,nhv->mhv", scores_low, retained_low, preferred_element_type=WIDE)
        .astype(LOW)
        .reshape(length, value_columns)
    )
    query_pre_grad = (
        (rotate(query_grad, cosine, -sine) * KEY ** (-0.5)).astype(LOW).reshape(length, key_columns)
    )
    key_pre_grad = rotate(key_grad, cosine, -sine).astype(LOW).reshape(length, key_columns)
    total = multiply_right(query_pre_grad, query_weight)
    total = total + multiply_right(key_pre_grad, key_weight)
    total = total + multiply_right(value_grad, value_weight)
    normed_grad = scatter_tensor(total + multiply_right(gate_pre_low, gate_weight))
    gate_weight_grad, value_weight_grad, query_weight_grad, key_weight_grad = scatter_rows(
        normed.T, [gate_pre_low, value_grad, query_pre_grad, key_pre_grad], lines, 1
    )
    _, pull_first = jax.vjp(rms_scale, resid_in, gain_first)
    in_from_norm, gain_first_part = pull_first(normed_grad)
    in_grad = from_places(resid_mid_grad + in_from_norm).reshape(hidden_in.shape)

    gain_part = jnp.stack([gain_first_part, gain_second_part])
    gain_part = gain_part + swap_tensor(gain_part, 1)
    gain_part = gain_part + swap_tensor(gain_part, 2)
    gain_total = scatter_dp(gain_part, 1)
    return (
        hidden_out,
        in_grad,
        gain_total[0],
        query_weight_grad,
        key_weight_grad,
        value_weight_grad,
        gate_weight_grad,
        out_weight_grad,
        gain_total[1],
        mlp_gate_grad,
        mlp_up_grad,
        down_grad,
    )


def solution(mesh):
    return jax.shard_map(
        on_device,
        mesh=mesh,
        in_specs=(
            P("dp", "tensor", None),
            P("dp", "tensor", None),
            P("dp", None),
            P("dp"),
            P("dp", "tensor"),
            P("dp", "tensor"),
            P("dp", "tensor"),
            P("dp", "tensor"),
            P("tensor", "dp"),
            P("dp"),
            P("dp", "tensor"),
            P("dp", "tensor"),
            P("tensor", "dp"),
        ),
        out_specs=(
            P("dp", "tensor", None),
            P("dp", "tensor", None),
            P("dp"),
            P("dp", "tensor"),
            P("dp", "tensor"),
            P("dp", "tensor"),
            P("dp", "tensor"),
            P("tensor", "dp"),
            P("dp"),
            P("dp", "tensor"),
            P("dp", "tensor"),
            P("tensor", "dp"),
        ),
        check_vma=False,
    )
```

```python
import functools
import math

import jax
import jax.numpy as jnp
from jax import lax
from jax.experimental import pallas as pl
from jax.experimental.pallas import tpu as pltpu
from jax.sharding import PartitionSpec as P

KEY = 256
VAL = 432
LOW = jnp.bfloat16
WIDE = jnp.float32
WEIGHTS = 8
MESH = pl.DeviceIdType.MESH
ANY = pl.BlockSpec(memory_space=pl.ANY)
INSIDE = pl.BlockSpec(memory_space=pltpu.VMEM)
ROOM = 60 * 1024 * 1024

def rotary_tables(position, width):
    half = width // 2
    frequency = 10000.0 ** (-2.0 * jnp.arange(half, dtype=jnp.int32).astype(WIDE) / width)
    angle = position.astype(WIDE)[:, None] * frequency[None, :]
    return (jnp.cos(angle), jnp.sin(angle))


def greet(peers):
    barrier = pltpu.get_barrier_semaphore()
    for peer in peers:
        pl.semaphore_signal(barrier, inc=1, device_id=peer, device_id_type=MESH)
    pl.semaphore_wait(barrier, len(peers))


def remote(source, target, send, recv, device):
    return pltpu.make_async_remote_copy(
        src_ref=source,
        dst_ref=target,
        send_sem=send,
        recv_sem=recv,
        device_id=device,
        device_id_type=MESH,
    )


def forward_kernel(lines, members, *refs):
    hidden_ref, grad_ref, gain_ref, cos_ref, sin_ref, down_seg, along_seg, rate_ref = refs[:8]
    shards = refs[8:16]
    normed_turned, grad_all, gain_all = refs[16:19]
    wholes = refs[19:27]
    query_out, keys_out, values_out, gate_out, grad_turned = refs[27:32]
    retained_out, mixed_out, resid_out, mid_turned, gate_hidden_out, up_hidden_out = refs[32:38]
    hidden_out = refs[38]
    normed, mid, short, wide_one, wide_two, turned = refs[39:45]
    query, keys, scores, values, retained, gate, mixed, hidden = refs[45:53]
    held, got, base = refs[53:56]
    line_send, line_recv, side_send, side_recv = refs[56:60]
    near_send, near_recv, gain_send, gain_recv, home = refs[60:]

    parts = 2 * lines
    rows, width = hidden_ref.shape
    slice_width = gain_ref.shape[1]
    heads = rate_ref.shape[0]
    value_columns = values.shape[2]
    me = lax.axis_index("dp")
    line, side = me // 2, lax.rem(me, 2)
    here = side * lines + line
    own = lax.axis_index("tensor")
    half, rest = own // 2, lax.rem(own, 2)

    def member(k):
        return 2 * lax.rem(half + k // 2, 2) + lax.rem(rest + lax.rem(k, 2), 2)

    partners = [None] + [{"tensor": member(k)} for k in range(1, members)]
    others = [{"dp": lax.rem(me + k, parts)} for k in range(1, parts)]
    opposite = {"dp": 2 * line + (1 - side)}
    greet(others + partners[1:])

    local = {}
    slots = iter(range(32))

    def keep(source, target):
        slot = next(slots)
        local[slot] = pltpu.make_async_copy(source, target, home.at[slot])
        local[slot].start()
        return slot

    def finish(slot):
        local.pop(slot).wait()

    near = {}

    def near_start(tag, source, target, k):
        copy = remote(source, target, near_send.at[tag], near_recv.at[tag], partners[k])
        copy.start()
        near[tag] = copy

    steps = {}
    across = {}
    ours = {}

    def start_lines(w):
        for step in range(1, lines):
            steps[w, step] = remote(
                shards[w],
                wholes[w].at[here],
                line_send.at[w, step],
                line_recv.at[w, step],
                {"dp": 2 * lax.rem(line + step, lines) + side},
            )
            steps[w, step].start()
        across[w, 0] = remote(
            shards[w], wholes[w].at[here], side_send.at[w, 0], side_recv.at[w, 0], opposite
        )
        across[w, 0].start()
        ours[w] = keep(shards[w], wholes[w].at[here])

    def pass_on(w, third):
        for step in range(1 + third * (lines - 1) // 3, 1 + (third + 1) * (lines - 1) // 3):
            steps[w, step].wait_recv()
            place = side * lines + lax.rem(line + lines - step, lines)
            across[w, step] = remote(
                wholes[w].at[place],
                wholes[w].at[place],
                side_send.at[w, step],
                side_recv.at[w, step],
                opposite,
            )
            across[w, step].start()

    def complete(w):
        for step in range(lines):
            across[w, step].wait_recv()
        finish(ours[w])

    def load(w, target, sem):
        copy = pltpu.make_async_copy(wholes[w], target, sem)
        copy.start()
        copy.wait()

    def stage(w, target, body):
        if w + 1 < WEIGHTS:
            pass_on(w + 1, 0)
        complete(w)
        load(w, target, home.at[home.shape[0] - 1 - w])
        lax.fori_loop(0, members // 2, body, 0)
        if w + 1 < WEIGHTS:
            pass_on(w + 1, 1)
        lax.fori_loop(members // 2, members, body, 0)
        if w + 1 < WEIGHTS:
            pass_on(w + 1, 2)
        if w + 3 < WEIGHTS:
            start_lines(w + 3)

    gains = []
    for k in range(1, parts):
        copy = remote(
            gain_ref, gain_all.at[here], gain_send.at[k], gain_recv.at[k], others[k - 1]
        )
        copy.start()
        gains.append(copy)
    gain_all[here] = gain_ref[...]
    for w in range(3):
        start_lines(w)

    def scale_into(target, scaled, which):
        for p in range(parts):
            columns = slice(p * slice_width, (p + 1) * slice_width)
            target[0, :, columns] = (
                scaled[:, columns] * gain_all[p][which : which + 1]
            ).astype(LOW)

    resid = hidden_ref[...].astype(WIDE)
    scaled = resid * lax.rsqrt(jnp.mean(resid * resid, axis=-1, keepdims=True) + 1e-06)
    for copy in gains:
        copy.wait_recv()
    scale_into(normed, scaled, 0)
    for k in range(1, members):
        near_start(k - 1, normed.at[0], normed.at[k], k)
    for k in range(1, members):
        near_start(2 + k, grad_ref, mid.at[k], k)
    grad_kept = keep(grad_ref, mid.at[0])
    for third in range(3):
        pass_on(0, third)
    for k in range(1, members):
        near[k - 1].wait_recv()

    def turn_over(source):
        tile = 256

        def body(k, carry):
            at = pl.ds(pl.multiple_of(k * rows, rows), rows)
            for c in range(width // tile):
                columns = slice(c * tile, (c + 1) * tile)
                turned[columns, at] = source[k, :, columns].T
            return carry

        lax.fori_loop(0, members, body, 0)

    turn_over(normed)
    turned_kept = keep(turned, normed_turned)

    def flat(ref):
        return ref[...].reshape(width, ref.shape[2])

    def turn(source, target, scale):
        def body(k, carry):
            pre = jnp.dot(normed[k], flat(source), preferred_element_type=WIDE)
            at = pl.ds(pl.multiple_of(k * rows, rows), rows)
            cosine, sine = cos_ref[at, :], sin_ref[at, :]
            wing = KEY // 2
            for h in range(heads):
                first = pre[:, h * KEY : h * KEY + wing]
                second = pre[:, h * KEY + wing : (h + 1) * KEY]
                target[k, :, h * KEY : h * KEY + wing] = (
                    (first * cosine - second * sine) * scale
                ).astype(LOW)
                target[k, :, h * KEY + wing : (h + 1) * KEY] = (
                    (second * cosine + first * sine) * scale
                ).astype(LOW)
            return carry

        return body

    stage(0, short, turn(short, query, KEY ** (-0.5)))
    keep(query, query_out)
    stage(1, short, turn(short, keys, 1.0))
    keep(keys, keys_out)

    def score(k, carry):
        place = member(k)
        at = pl.multiple_of(place * rows, rows)
        segment = down_seg[pl.ds(at, rows), :]
        for h in range(heads):
            head = slice(h * KEY, (h + 1) * KEY)
            for m in range(members):
                start = pl.multiple_of(member(m) * rows, rows)
                raw = lax.dot_general(
                    query[k, :, head],
                    keys[m, :, head],
                    (((1,), (1,)), ((), ())),
                    preferred_element_type=WIDE,
                )
                distance = (
                    lax.broadcasted_iota(jnp.int32, (rows, rows), 0)
                    - lax.broadcasted_iota(jnp.int32, (rows, rows), 1)
                    + (at - start)
                )
                same = (distance >= 0) & (segment == along_seg[:, pl.ds(start, rows)])
                decay = jnp.exp(
                    rate_ref[h : h + 1, :1] * jnp.maximum(distance, 0).astype(WIDE)
                )
                scores[h, k, :, m * rows : (m + 1) * rows] = (
                    raw * jnp.where(same, decay, 0.0)
                ).astype(LOW)
        return carry

    lax.fori_loop(0, members, score, 0)
    finish(grad_kept)
    for k in range(1, members):
        near[2 + k].wait_recv()
    finish(turned_kept)
    turn_over(mid)
    turned_kept = keep(turned, grad_turned)
    grad_kept = keep(mid, grad_all)

    column = lax.broadcasted_iota(jnp.int32, (rows, value_columns), 1)

    def by_head(parts_of):
        result = parts_of[0]
        for h in range(1, heads):
            result = jnp.where(column < h * VAL, result, parts_of[h])
        return result

    def head_mean(value):
        means = []
        for h in range(heads):
            inside = (column >= h * VAL) & (column < (h + 1) * VAL)
            total = jnp.sum(jnp.where(inside, value, 0.0), axis=-1, keepdims=True)
            means.append(total * (1.0 / VAL))
        return by_head(means)

    def make_values(k, carry):
        values[k] = jnp.dot(normed[k], flat(wide_one), preferred_element_type=WIDE).astype(LOW)
        return carry

    stage(2, wide_one, make_values)
    keep(values, values_out)

    def retain(k, carry):
        every = values[...].reshape(members * rows, value_columns)
        retained[k] = by_head(
            [
                jnp.dot(scores[h, k], every, preferred_element_type=WIDE)
                for h in range(heads)
            ]
        )
        return carry

    lax.fori_loop(0, members, retain, 0)
    retained_kept = keep(retained, retained_out)

    def make_mixed(k, carry):
        pre = jnp.dot(normed[k], flat(wide_two), preferred_element_type=WIDE)
        gate[k] = pre
        value = retained[k]
        centred = value - head_mean(value)
        grouped = centred * lax.rsqrt(head_mean(centred * centred) + 1.0)
        mixed[k] = (grouped * (pre / (1.0 + jnp.exp(-pre)))).astype(LOW)
        return carry

    stage(3, wide_two, make_mixed)
    gate_kept = keep(gate, gate_out)
    keep(mixed, mixed_out)

    def project(k, put):
        for p in range(parts):
            columns = slice(p * slice_width, (p + 1) * slice_width)
            put(
                columns,
                lax.dot_general(
                    mixed[k],
                    wide_one[p],
                    (((1,), (1,)), ((), ())),
                    preferred_element_type=WIDE,
                ),
            )

    def put_low(slot):
        def put(columns, value):
            held[slot, :, columns] = value.astype(LOW)

        return put

    def put_sum(columns, value):
        base[:, columns] = value

    pass_on(5, 0)
    complete(4)
    load(4, wide_one, home.at[home.shape[0] - 5])
    finish(grad_kept)
    project(3, put_low(0))
    near_start(6, held.at[0], got.at[0], 1)
    project(2, put_sum)
    pass_on(5, 1)
    near[6].wait_recv()
    held[1] = (base[...] + got[0].astype(WIDE)).astype(LOW)
    near_start(8, held.at[1], got.at[1], 2)
    project(1, put_low(2))
    near_start(7, held.at[2], got.at[2], 1)
    project(0, put_sum)
    pass_on(5, 2)
    start_lines(7)
    near[7].wait_recv()
    base[...] = base[...] + got[2].astype(WIDE) + hidden_ref[...].astype(WIDE)
    pass_on(6, 0)
    near[8].wait_recv()
    resid = base[...] + got[1].astype(WIDE)
    resid_out[...] = resid
    scaled = resid * lax.rsqrt(jnp.mean(resid * resid, axis=-1, keepdims=True) + 1e-06)
    scale_into(mid, scaled, 1)
    near_start(10, mid.at[0], mid.at[2], 2)
    near_start(9, mid.at[0], mid.at[1], 1)
    pass_on(6, 1)
    pass_on(6, 2)
    near[10].wait_recv()
    near_start(11, mid.at[2], mid.at[3], 1)
    complete(5)
    load(5, wide_two, home.at[home.shape[0] - 6])
    near[9].wait_recv()
    near[11].wait_recv()
    finish(retained_kept)
    finish(gate_kept)

    def make_gate(k, carry):
        gate[k] = jnp.dot(mid[k], flat(wide_two), preferred_element_type=WIDE)
        return carry

    lax.fori_loop(0, members, make_gate, 0)
    keep(gate, gate_hidden_out)
    finish(turned_kept)
    turn_over(mid)
    keep(turned, mid_turned)
    pass_on(7, 0)
    pass_on(7, 1)
    pass_on(7, 2)
    complete(6)
    load(6, wide_one, home.at[home.shape[0] - 7])

    def make_hidden(k, carry):
        up = jnp.dot(mid[k], flat(wide_one), preferred_element_type=WIDE)
        retained[k] = up
        pre = gate[k]
        inner = (2.0 / math.pi) ** 0.5 * (pre + 0.044715 * (pre * pre * pre))
        hidden[k] = (0.5 * pre * (1.0 + jnp.tanh(inner)) * up).astype(LOW)
        return carry

    lax.fori_loop(0, members, make_hidden, 0)
    keep(retained, up_hidden_out)
    keep(hidden, hidden_out)
    complete(7)
    for w in range(WEIGHTS):
        for step in range(1, lines):
            steps[w, step].wait_send()
        for step in range(lines):
            across[w, step].wait_send()
    for copy in gains:
        copy.wait_send()
    for copy in near.values():
        copy.wait_send()
    for slot in list(local):
        finish(slot)


def forward(hidden, grad, gains, cosine, sine, segments, rates, shards, lines, members):
    parts = 2 * lines
    rows, width = hidden.shape
    heads = rates.shape[0]
    key_columns, value_columns = shards[0].shape[1], shards[2].shape[1]
    length = rows * members
    blocks = (members, rows)
    turned = (width, length)
    outs = [
        (turned, LOW),
        (blocks + (width,), LOW),
        ((parts,) + gains.shape, WIDE),
    ]
    outs += [((parts,) + shard.shape, LOW) for shard in shards]
    outs += [
        (blocks + (key_columns,), LOW),
        (blocks + (key_columns,), LOW),
        (blocks + (value_columns,), LOW),
        (blocks + (value_columns,), WIDE),
        (turned, LOW),
        (blocks + (value_columns,), WIDE),
        (blocks + (value_columns,), LOW),
        ((rows, width), WIDE),
        (turned, LOW),
        (blocks + (value_columns,), WIDE),
        (blocks + (value_columns,), WIDE),
        (blocks + (value_columns,), LOW),
    ]
    places = [ANY] * len(outs)
    places[2] = INSIDE
    places[18] = INSIDE
    tags = 12
    return pl.pallas_call(
        functools.partial(forward_kernel, lines, members),
        out_shape=[jax.ShapeDtypeStruct(shape, dtype) for shape, dtype in outs],
        in_specs=[INSIDE, ANY] + [INSIDE] * 6 + [ANY] * WEIGHTS,
        out_specs=places,
        scratch_shapes=[
            pltpu.VMEM(blocks + (width,), LOW),
            pltpu.VMEM(blocks + (width,), LOW),
            pltpu.VMEM((parts,) + shards[0].shape, LOW),
            pltpu.VMEM((parts,) + shards[2].shape, LOW),
            pltpu.VMEM((parts,) + shards[2].shape, LOW),
            pltpu.VMEM(turned, LOW),
            pltpu.VMEM(blocks + (key_columns,), LOW),
            pltpu.VMEM(blocks + (key_columns,), LOW),
            pltpu.VMEM((heads, members, rows, length), LOW),
            pltpu.VMEM(blocks + (value_columns,), LOW),
            pltpu.VMEM(blocks + (value_columns,), WIDE),
            pltpu.VMEM(blocks + (value_columns,), WIDE),
            pltpu.VMEM(blocks + (value_columns,), LOW),
            pltpu.VMEM(blocks + (value_columns,), LOW),
            pltpu.VMEM((3, rows, width), LOW),
            pltpu.VMEM((3, rows, width), LOW),
            pltpu.VMEM((rows, width), WIDE),
            pltpu.SemaphoreType.DMA((WEIGHTS, lines)),
            pltpu.SemaphoreType.DMA((WEIGHTS, lines)),
            pltpu.SemaphoreType.DMA((WEIGHTS, lines)),
            pltpu.SemaphoreType.DMA((WEIGHTS, lines)),
            pltpu.SemaphoreType.DMA((tags,)),
            pltpu.SemaphoreType.DMA((tags,)),
            pltpu.SemaphoreType.DMA((parts,)),
            pltpu.SemaphoreType.DMA((parts,)),
            pltpu.SemaphoreType.DMA((40,)),
        ],
        compiler_params=pltpu.CompilerParams(
            collective_id=0, has_side_effects=True, vmem_limit_bytes=ROOM
        ),
        cost_estimate=pl.CostEstimate(
            flops=10**11, bytes_accessed=10**9, transcendentals=0
        ),
        name="forward",
    )(hidden, grad, gains, cosine, sine, segments.T, segments, rates, *shards)


class Scatter:
    def __init__(self, lines, held, far_got, near_got, spare, sems):
        self.lines = lines
        self.held, self.far_got, self.near_got, self.spare = held, far_got, near_got, spare
        self.side_send, self.side_recv, self.line_send, self.line_recv, self.home = sems
        me = lax.axis_index("dp")
        self.line, self.side = me // 2, lax.rem(me, 2)
        self.opposite = {"dp": 2 * self.line + (1 - self.side)}

    def peer(self, step):
        return {"dp": 2 * lax.rem(self.line + step, self.lines) + self.side}

    def peers(self):
        return [self.opposite] + [self.peer(step) for step in range(1, self.lines)]

    def far_copy(self, w, place):
        return remote(
            self.held[w].at[place],
            self.far_got[w].at[place],
            self.side_send.at[w, place],
            self.side_recv.at[w, place],
            self.opposite,
        )

    def near_copy(self, w, step):
        place = lax.rem(self.line + step, self.lines)
        return remote(
            self.held[w].at[place],
            self.near_got[w].at[step],
            self.line_send.at[w, step],
            self.line_recv.at[w, step],
            self.peer(step),
        )

    def fetch(self, source):
        spare = self.spare[source.shape[-1]]
        copy = pltpu.make_async_copy(source, spare, self.home)
        copy.start()
        copy.wait()
        return spare[...].astype(WIDE)

    def product(self, left, right, place):
        rows = self.held[0].shape[1]
        block = left[pl.ds(pl.multiple_of(place * rows, rows), rows), :]
        every = right[...]
        return jnp.dot(
            block,
            every.reshape(every.shape[0] * every.shape[1], every.shape[2]),
            preferred_element_type=WIDE,
        )

    def far(self, w, left, right):
        def body(step, carry):
            place = lax.rem(self.line + step + 1, self.lines)
            other = (1 - self.side) * self.lines + place
            self.held[w][place] = self.product(left, right, other).astype(LOW)
            self.far_copy(w, place).start()
            return carry

        lax.fori_loop(0, self.lines, body, 0)

    def near(self, w, left, right):
        def body(step, carry):
            place = lax.rem(self.line + step, self.lines)
            part = self.product(left, right, self.side * self.lines + place)
            self.far_copy(w, place).wait_recv()
            total = part + self.fetch(self.far_got[w].at[place])
            self.far_copy(w, place).wait_send()
            self.held[w][place] = total.astype(LOW)
            self.near_copy(w, step).start()
            return carry

        lax.fori_loop(1, self.lines, body, 0)
        part = self.product(left, right, self.side * self.lines + self.line)
        self.far_copy(w, self.line).wait_recv()
        total = part + self.fetch(self.far_got[w].at[self.line])
        self.far_copy(w, self.line).wait_send()
        self.held[w][self.line] = total.astype(LOW)
        self.own_copy(w).start()

    def own_copy(self, w):
        return pltpu.make_async_copy(
            self.held[w].at[self.line], self.near_got[w].at[0], self.line_send.at[w, 0]
        )

    def finish(self, w):
        def body(step, carry):
            self.near_copy(w, step).wait()
            return carry

        lax.fori_loop(1, self.lines, body, 0)
        self.own_copy(w).wait()


class Near:
    def __init__(self, send, recv):
        self.send, self.recv = send, recv
        self.flight = {}
        own = lax.axis_index("tensor")
        half, rest = own // 2, lax.rem(own, 2)
        self.member = lambda k: 2 * lax.rem(half + k // 2, 2) + lax.rem(rest + lax.rem(k, 2), 2)

    def partners(self, members):
        return [{"tensor": self.member(k)} for k in range(1, members)]

    def start(self, tag, source, target, k):
        copy = remote(source, target, self.send.at[tag], self.recv.at[tag], self.partners(4)[k - 1])
        copy.start()
        self.flight[tag] = copy

    def wait(self, tag):
        self.flight[tag].wait_recv()

    def sent(self, tag):
        self.flight[tag].wait_send()


def dot_across(left, right):
    return lax.dot_general(
        left, right, (((1,), (1,)), ((), ())), preferred_element_type=WIDE
    )


def feed_kernel(lines, members, *refs):
    grad_ref, grad_turned, mid_turned, hidden, resid_ref, gain_all = refs[:6]
    gate_weight, up_weight, down_weight, gate_hidden, up_hidden = refs[6:11]
    near_got, mid_all, mid_grad_out, hidden_out, gain_out = refs[11:14], *refs[14:18]
    far_got = refs[18:21]
    gate_low, up_low, pre, up = refs[21:25]
    scatter_held = refs[25:28]
    spare, held, got, last, base, mid = refs[28:34]
    sems = refs[34:38]
    near_send, near_recv, home = refs[38:]
    parts = 2 * lines
    rows, width = resid_ref.shape
    slice_width = width // parts
    scatter = Scatter(
        lines,
        scatter_held,
        far_got,
        near_got,
        {spare.shape[1]: spare},
        sems + (home.at[0],),
    )
    near = Near(near_send, near_recv)
    greet(scatter.peers() + near.partners(members))
    scatter.far(0, grad_turned, hidden)

    def flat(ref):
        return ref[...].reshape(width, ref.shape[2])

    def pull(k, carry):
        first = pltpu.make_async_copy(gate_hidden.at[k], pre, home.at[1])
        second = pltpu.make_async_copy(up_hidden.at[k], up, home.at[2])
        first.start()
        second.start()
        grad = jnp.dot(grad_ref[k], flat(down_weight), preferred_element_type=WIDE)
        first.wait()
        second.wait()
        value = pre[...]
        root = (2.0 / math.pi) ** 0.5
        square = value * value
        lift = jnp.tanh(root * (value + 0.044715 * (value * square)))
        ramp = 0.5 * (1.0 + lift)
        slope = ramp + 0.5 * value * (1.0 - lift * lift) * root * (1.0 + 0.134145 * square)
        gate_low[k] = (grad * up[...] * slope).astype(LOW)
        up_low[k] = (grad * (value * ramp)).astype(LOW)
        return carry

    lax.fori_loop(0, members, pull, 0)
    scatter.far(1, mid_turned, gate_low)

    def back(k, put):
        for p in range(parts):
            columns = slice(p * slice_width, (p + 1) * slice_width)
            put(
                columns,
                dot_across(gate_low[k], gate_weight[p]) + dot_across(up_low[k], up_weight[p]),
            )

    def put_low(slot):
        def put(columns, value):
            held[slot, :, columns] = value.astype(LOW)

        return put

    def put_sum(columns, value):
        base[:, columns] = value

    back(3, put_low(0))
    near.start(0, held.at[0], got.at[0], 1)
    back(2, put_sum)
    near.wait(0)
    near.sent(0)
    held[0] = (base[...] + got[0].astype(WIDE)).astype(LOW)
    near.start(1, held.at[0], got.at[1], 2)
    back(1, put_low(1))
    near.start(2, held.at[1], got.at[2], 1)
    back(0, put_sum)
    scatter.far(2, mid_turned, up_low)
    near.wait(2)
    base[...] += got[2].astype(WIDE)
    near.wait(1)
    normed_grad = base[...] + got[1].astype(WIDE)
    resid = resid_ref[...]
    scale = lax.rsqrt(jnp.mean(resid * resid, axis=-1, keepdims=True) + 1e-06)
    unit = resid * scale
    base[...] = normed_grad * unit
    gain_out[...] = jnp.broadcast_to(
        jnp.sum(base[...], axis=0, keepdims=True), gain_out.shape
    )
    dot = jnp.zeros((rows, 1), WIDE)
    for p in range(parts):
        columns = slice(p * slice_width, (p + 1) * slice_width)
        dot += jnp.sum(base[:, columns] * gain_all[p][1:2], axis=-1, keepdims=True)
    dot = dot * (1.0 / width)
    base[...] = normed_grad
    for p in range(parts):
        columns = slice(p * slice_width, (p + 1) * slice_width)
        block = resid_ref[:, columns] * scale
        mid_grad = grad_ref[0, :, columns].astype(WIDE) + scale * (
            base[:, columns] * gain_all[p][1:2] - block * dot
        )
        base[:, columns] = mid_grad
        mid[:, columns] = mid_grad.astype(LOW)
    mid_grad_copy = pltpu.make_async_copy(base, mid_grad_out, home.at[1])
    mid_grad_copy.start()
    near.start(3, mid, mid_all.at[2], 2)
    near.start(4, mid, mid_all.at[1], 1)
    own = pltpu.make_async_copy(mid, mid_all.at[0], home.at[3])
    own.start()
    scatter.near(0, grad_turned, hidden)
    near.wait(3)
    near.start(5, mid_all.at[2], mid_all.at[3], 1)
    scatter.near(1, mid_turned, gate_low)

    def down(k, put):
        for p in range(parts):
            columns = slice(p * slice_width, (p + 1) * slice_width)
            put(columns, dot_across(hidden[k], down_weight[p]))

    near.sent(1)
    near.sent(2)
    down(3, put_low(0))
    mid_grad_copy.wait()
    near.start(6, held.at[0], last.at[0], 1)
    down(2, put_sum)
    near.wait(6)
    near.sent(6)
    held[0] = (base[...] + last[0].astype(WIDE)).astype(LOW)
    near.start(7, held.at[0], last.at[1], 2)
    down(1, put_low(1))
    near.start(8, held.at[1], last.at[2], 1)
    down(0, put_sum)
    scatter.near(2, mid_turned, up_low)
    near.wait(8)
    near.wait(7)
    own.wait()
    near.sent(3)
    near.sent(4)
    mid[...] = (
        base[...] + last[2].astype(WIDE) + last[1].astype(WIDE) + resid_ref[...]
    ).astype(LOW)
    own = pltpu.make_async_copy(mid, hidden_out, home.at[3])
    own.start()
    for w in range(3):
        scatter.finish(w)
    near.wait(4)
    near.wait(5)
    own.wait()
    for tag in (5, 7, 8):
        near.sent(tag)


def feed_backward(
    grad, grad_turned, mid_turned, hidden, resid, gains, weights, pres, lines, members
):
    parts = 2 * lines
    rows, width = resid.shape
    columns = hidden.shape[2]
    slice_width = width // parts
    blocks = (members, rows)
    piece = (lines, slice_width, columns)
    outs = [(piece, LOW)] * 3
    outs += [
        (blocks + (width,), LOW),
        ((rows, width), WIDE),
        ((rows, width), LOW),
        ((8, width), WIDE),
    ]
    outs += [(piece, LOW)] * 3
    return pl.pallas_call(
        functools.partial(feed_kernel, lines, members),
        out_shape=[jax.ShapeDtypeStruct(shape, dtype) for shape, dtype in outs],
        in_specs=[INSIDE] * 9 + [ANY] * 2,
        out_specs=[ANY] * 6 + [INSIDE] + [ANY] * 3,
        scratch_shapes=[
            pltpu.VMEM(blocks + (columns,), LOW),
            pltpu.VMEM(blocks + (columns,), LOW),
            pltpu.VMEM((rows, columns), WIDE),
            pltpu.VMEM((rows, columns), WIDE),
            pltpu.VMEM(piece, LOW),
            pltpu.VMEM(piece, LOW),
            pltpu.VMEM(piece, LOW),
            pltpu.VMEM(piece[1:], LOW),
            pltpu.VMEM((2, rows, width), LOW),
            pltpu.VMEM((3, rows, width), LOW),
            pltpu.VMEM((3, rows, width), LOW),
            pltpu.VMEM((rows, width), WIDE),
            pltpu.VMEM((rows, width), LOW),
            pltpu.SemaphoreType.DMA((3, lines)),
            pltpu.SemaphoreType.DMA((3, lines)),
            pltpu.SemaphoreType.DMA((3, lines)),
            pltpu.SemaphoreType.DMA((3, lines)),
            pltpu.SemaphoreType.DMA((9,)),
            pltpu.SemaphoreType.DMA((9,)),
            pltpu.SemaphoreType.DMA((4,)),
        ],
        compiler_params=pltpu.CompilerParams(
            collective_id=1, has_side_effects=True, vmem_limit_bytes=ROOM
        ),
        cost_estimate=pl.CostEstimate(flops=10**11, bytes_accessed=10**9, transcendentals=0),
        name="feed_backward",
    )(grad, grad_turned, mid_turned, hidden, resid, gains, *weights, *pres)[:7]


def retention_kernel(lines, members, *refs):
    mixed, normed_turned, query, keys, values = refs[:5]
    cos_ref, sin_ref, down_seg, along_seg, rate_ref = refs[5:10]
    hidden_ref, gain_all, gain_part = refs[10:13]
    mid_grad_ref, mid_all, retained_all, gate_all = refs[13:17]
    weights = refs[17:22]
    near_got, in_grad_out, gain_out = refs[22:27], refs[27], refs[28]
    far_got = refs[29:34]
    turned, wide_one, wide_two, short_one, short_two = refs[34:39]
    gate_low, retained_low, value_low, query_low, key_low = refs[39:44]
    scatter_held = refs[44:49]
    spare_wide, spare_short, held, got, base, retained, gate = refs[49:56]
    pieces, piece_got, total, total_got = refs[56:60]
    sems = refs[60:64]
    near_send, near_recv, gain_send, gain_recv, home = refs[64:]
    parts = 2 * lines
    rows, width = hidden_ref.shape
    slice_width = width // parts
    heads = rate_ref.shape[0]
    value_columns = values.shape[2]
    length = rows * members
    scatter = Scatter(
        lines,
        scatter_held,
        far_got,
        near_got,
        {spare_wide.shape[1]: spare_wide, spare_short.shape[1]: spare_short},
        sems + (home.at[0],),
    )
    near = Near(near_send, near_recv)
    me = lax.axis_index("dp")
    here = scatter.side * lines + scatter.line
    others = [{"dp": lax.rem(me + k, parts)} for k in range(1, parts)]
    greet(others + near.partners(members))

    def fetch(source, target, sem):
        copy = pltpu.make_async_copy(source, target, home.at[sem])
        copy.start()
        return copy

    out_copy = fetch(weights[0], wide_one, 1)
    value_copy = fetch(weights[2], wide_two, 2)
    query_copy = fetch(weights[3], short_one, 3)
    key_copy = fetch(weights[4], short_two, 4)
    grad_copy = fetch(mid_grad_ref, in_grad_out, 7)

    def turn_over(k, carry):
        fetch(mid_all.at[k], held.at[0], 8).wait()
        at = pl.ds(pl.multiple_of(k * rows, rows), rows)
        for c in range(width // 256):
            columns = slice(c * 256, (c + 1) * 256)
            turned[columns, at] = held[0, :, columns].T
        return carry

    lax.fori_loop(0, members, turn_over, 0)
    scatter.far(0, turned, mixed)
    out_copy.wait()

    column = lax.broadcasted_iota(jnp.int32, (rows, value_columns), 1)

    def by_head(parts_of):
        result = parts_of[0]
        for h in range(1, heads):
            result = jnp.where(column < h * VAL, result, parts_of[h])
        return result

    def inside(h):
        return (column >= h * VAL) & (column < (h + 1) * VAL)

    def head_mean(value):
        return by_head(
            [
                jnp.sum(jnp.where(inside(h), value, 0.0), axis=-1, keepdims=True) * (1.0 / VAL)
                for h in range(heads)
            ]
        )

    def unmix(k, carry):
        first = fetch(retained_all.at[k], retained, 5)
        second = fetch(gate_all.at[k], gate, 6)
        fetch(mid_all.at[k], held.at[0], 8).wait()
        grad = jnp.dot(
            held[0],
            wide_one[...].reshape(width, value_columns),
            preferred_element_type=WIDE,
        )
        first.wait()
        second.wait()
        value = retained[...]
        centred = value - head_mean(value)
        rate = lax.rsqrt(head_mean(centred * centred) + 1.0)
        pre = gate[...]
        sigma = 1.0 / (1.0 + jnp.exp(-pre))
        gate_low[k] = (
            grad * (centred * rate) * (sigma * (1.0 + pre * (1.0 - sigma)))
        ).astype(LOW)
        grouped_grad = grad * (pre * sigma)
        retained_low[k] = (
            rate * (grouped_grad - head_mean(grouped_grad))
            - (rate * rate * rate) * centred * head_mean(grouped_grad * centred)
        ).astype(LOW)
        return carry

    lax.fori_loop(0, members, unmix, 0)
    scatter.far(1, normed_turned, gate_low)
    gate_copy = fetch(weights[1], wide_one, 1)

    def decay(h, late, early, late_segment, early_segment, turn):
        sign = -1 if turn else 1
        distance = (
            sign
            * (
                lax.broadcasted_iota(jnp.int32, (rows, rows), 0)
                - lax.broadcasted_iota(jnp.int32, (rows, rows), 1)
            )
            + (late - early)
        )
        same = (distance >= 0) & (late_segment == early_segment)
        return jnp.where(
            same,
            jnp.exp(rate_ref[h : h + 1, :1] * jnp.maximum(distance, 0).astype(WIDE)),
            0.0,
        )

    def start_of(k):
        return pl.multiple_of(near.member(k) * rows, rows)

    wing = KEY // 2
    along = [along_seg[:, pl.ds(start_of(k), rows)] for k in range(members)]

    def turn_back(target, k, h, grad, scale):
        at = pl.ds(pl.multiple_of(k * rows, rows), rows)
        cosine, sine = cos_ref[at, :], sin_ref[at, :]
        first, second = grad[:, :wing], grad[:, wing:]
        target[k, :, h * KEY : h * KEY + wing] = (
            (first * cosine + second * sine) * scale
        ).astype(LOW)
        target[k, :, h * KEY + wing : (h + 1) * KEY] = (
            (second * cosine - first * sine) * scale
        ).astype(LOW)

    def early_side(m, carry):
        early = start_of(m)
        early_segment = down_seg[pl.ds(early, rows), :]
        value_grads = []
        for h in range(heads):
            head = slice(h * KEY, (h + 1) * KEY)
            masked = jnp.where(inside(h), values[m].astype(WIDE), 0.0).astype(LOW)
            value_grad = jnp.zeros((rows, value_columns), WIDE)
            key_grad = jnp.zeros((rows, KEY), WIDE)
            for n in range(members):
                late = start_of(n)
                late_segment = along[n]
                mask = decay(h, late, early, late_segment, early_segment, True)
                score = (dot_across(keys[m, :, head], query[n, :, head]) * mask).astype(LOW)
                raw = (dot_across(masked, retained_low[n]) * mask).astype(LOW)
                value_grad += jnp.dot(score, retained_low[n], preferred_element_type=WIDE)
                key_grad += jnp.dot(raw, query[n, :, head], preferred_element_type=WIDE)
            value_grads.append(value_grad)
            turn_back(key_low, m, h, key_grad, 1.0)
        value_low[m] = by_head(value_grads).astype(LOW)
        return carry

    lax.fori_loop(0, members, early_side, 0)
    scatter.far(2, normed_turned, value_low)
    scatter.far(4, normed_turned, key_low)
    scatter.near(0, turned, mixed)

    def late_side(n, carry):
        late = start_of(n)
        late_segment = down_seg[pl.ds(late, rows), :]
        for h in range(heads):
            head = slice(h * KEY, (h + 1) * KEY)
            masked = jnp.where(inside(h), retained_low[n].astype(WIDE), 0.0).astype(LOW)
            query_grad = jnp.zeros((rows, KEY), WIDE)
            for m in range(members):
                early = start_of(m)
                early_segment = along[m]
                mask = decay(h, late, early, late_segment, early_segment, False)
                raw = (dot_across(masked, values[m]) * mask).astype(LOW)
                query_grad += jnp.dot(raw, keys[m, :, head], preferred_element_type=WIDE)
            turn_back(query_low, n, h, query_grad, KEY ** (-0.5))
        return carry

    lax.fori_loop(0, members, late_side, 0)
    scatter.far(3, normed_turned, query_low)
    scatter.near(1, normed_turned, gate_low)
    for copy in (gate_copy, value_copy, query_copy, key_copy, grad_copy):
        copy.wait()

    def back(k, put):
        for p in range(parts):
            columns = slice(p * slice_width, (p + 1) * slice_width)
            put(
                columns,
                dot_across(gate_low[k], wide_one[p])
                + dot_across(value_low[k], wide_two[p])
                + dot_across(query_low[k], short_one[p])
                + dot_across(key_low[k], short_two[p]),
            )

    def put_low(slot):
        def put(columns, value):
            held[slot, :, columns] = value.astype(LOW)

        return put

    def put_sum(columns, value):
        base[:, columns] = value

    back(3, put_low(0))
    near.start(0, held.at[0], got.at[0], 1)
    back(2, put_sum)
    near.wait(0)
    near.sent(0)
    held[0] = (base[...] + got[0].astype(WIDE)).astype(LOW)
    near.start(1, held.at[0], got.at[1], 2)
    back(1, put_low(1))
    near.start(2, held.at[1], got.at[2], 1)
    back(0, put_sum)
    scatter.near(2, normed_turned, value_low)
    near.wait(2)
    base[...] += got[2].astype(WIDE)
    near.wait(1)
    normed_grad = base[...] + got[1].astype(WIDE)
    base[...] = normed_grad
    resid = hidden_ref[...].astype(WIDE)
    scale = lax.rsqrt(jnp.mean(resid * resid, axis=-1, keepdims=True) + 1e-06)
    dot = jnp.zeros((rows, 1), WIDE)
    for p in range(parts):
        columns = slice(p * slice_width, (p + 1) * slice_width)
        product = base[:, columns] * (hidden_ref[:, columns].astype(WIDE) * scale)
        row = lax.broadcasted_iota(jnp.int32, (8, slice_width), 0)
        pieces[p] = jnp.where(
            row == 0, jnp.sum(product, axis=0, keepdims=True), gain_part[:, columns]
        )
        dot += jnp.sum(product * gain_all[p][0:1], axis=-1, keepdims=True)
    dot = dot * (1.0 / width)
    gains = []
    for k in range(1, parts):
        other = lax.rem(me + k, parts)
        place = lax.rem(other, 2) * lines + other // 2
        copy = remote(
            pieces.at[place], piece_got.at[k], gain_send.at[k], gain_recv.at[k], others[k - 1]
        )
        copy.start()
        gains.append(copy)
    for p in range(parts):
        columns = slice(p * slice_width, (p + 1) * slice_width)
        block = hidden_ref[:, columns].astype(WIDE) * scale
        in_grad_out[:, columns] += scale * (
            base[:, columns] * gain_all[p][0:1] - block * dot
        )
    value = pieces[here]
    for k in range(1, parts):
        gains[k - 1].wait_recv()
        value = value + piece_got[k]
    total[...] = value
    for k in range(1, members):
        near.start(2 + k, total, total_got.at[k], k)
    scatter.near(4, normed_turned, key_low)
    scatter.near(3, normed_turned, query_low)
    for w in (0, 1, 2, 4, 3):
        scatter.finish(w)
    for k in range(1, members):
        near.wait(2 + k)
        value = value + total_got[k]
    gain_out[...] = value
    for tag in range(1, 2 + members):
        near.sent(tag)
    for copy in gains:
        copy.wait_send()


def retention_backward(inside, streamed, weights, lines, members, slice_width):
    parts = 2 * lines
    rows, width = inside[10].shape
    blocks = (members, rows)
    wide, short = weights[0].shape[2], weights[3].shape[2]
    widths = [wide, wide, wide, short, short]
    pieces = [(lines, slice_width, columns) for columns in widths]
    outs = [(piece, LOW) for piece in pieces]
    outs += [((rows, width), WIDE), ((8, slice_width), WIDE)]
    outs += [(piece, LOW) for piece in pieces]
    return pl.pallas_call(
        functools.partial(retention_kernel, lines, members),
        out_shape=[jax.ShapeDtypeStruct(shape, dtype) for shape, dtype in outs],
        in_specs=[INSIDE] * 13 + [ANY] * 9,
        out_specs=[ANY] * 5 + [INSIDE] * 2 + [ANY] * 5,
        scratch_shapes=[
            pltpu.VMEM((width, rows * members), LOW),
            pltpu.VMEM(weights[0].shape, LOW),
            pltpu.VMEM(weights[0].shape, LOW),
            pltpu.VMEM(weights[3].shape, LOW),
            pltpu.VMEM(weights[3].shape, LOW),
            pltpu.VMEM(blocks + (wide,), LOW),
            pltpu.VMEM(blocks + (wide,), LOW),
            pltpu.VMEM(blocks + (wide,), LOW),
            pltpu.VMEM(blocks + (short,), LOW),
            pltpu.VMEM(blocks + (short,), LOW),
        ]
        + [pltpu.VMEM(piece, LOW) for piece in pieces]
        + [
            pltpu.VMEM((slice_width, wide), LOW),
            pltpu.VMEM((slice_width, short), LOW),
            pltpu.VMEM((2, rows, width), LOW),
            pltpu.VMEM((3, rows, width), LOW),
            pltpu.VMEM((rows, width), WIDE),
            pltpu.VMEM((rows, wide), WIDE),
            pltpu.VMEM((rows, wide), WIDE),
            pltpu.VMEM((parts, 8, slice_width), WIDE),
            pltpu.VMEM((parts, 8, slice_width), WIDE),
            pltpu.VMEM((8, slice_width), WIDE),
            pltpu.VMEM((members, 8, slice_width), WIDE),
            pltpu.SemaphoreType.DMA((5, lines)),
            pltpu.SemaphoreType.DMA((5, lines)),
            pltpu.SemaphoreType.DMA((5, lines)),
            pltpu.SemaphoreType.DMA((5, lines)),
            pltpu.SemaphoreType.DMA((6,)),
            pltpu.SemaphoreType.DMA((6,)),
            pltpu.SemaphoreType.DMA((parts,)),
            pltpu.SemaphoreType.DMA((parts,)),
            pltpu.SemaphoreType.DMA((9,)),
        ],
        compiler_params=pltpu.CompilerParams(
            collective_id=2, has_side_effects=True, vmem_limit_bytes=ROOM
        ),
        cost_estimate=pl.CostEstimate(flops=10**11, bytes_accessed=10**9, transcendentals=0),
        name="retention_backward",
    )(*inside, *streamed, *weights)[:7]


def on_device(
    hidden_in,
    out_grad,
    segment_ids,
    norm1_gain,
    w_query,
    w_key,
    w_value,
    w_gate,
    w_out,
    norm2_gain,
    w_mlp_gate,
    w_mlp_up,
    w_mlp_down,
):
    _, rows, width = hidden_in.shape
    parts = lax.axis_size("dp")
    lines = parts // 2
    slice_width = width // parts
    own = lax.axis_index("tensor")
    members = lax.axis_size("tensor")
    order = list(range(0, parts, 2)) + list(range(1, parts, 2))

    def to_places(value):
        blocks = [value[:, k * slice_width : (k + 1) * slice_width] for k in order]
        return jnp.concatenate(blocks, axis=1)

    def from_places(value):
        blocks = [value[:, k * slice_width : (k + 1) * slice_width] for k in range(parts)]
        return jnp.concatenate([blocks[k // 2 + k % 2 * lines] for k in range(parts)], axis=1)

    heads_here = w_query.shape[1] // KEY
    resid_low = to_places(hidden_in.reshape(rows, width))
    grad_local = to_places(out_grad.reshape(rows, width))
    gain_rows = jnp.concatenate(
        [norm1_gain[None], norm2_gain[None], jnp.zeros((6, slice_width), LOW)]
    ).astype(WIDE)
    position = jnp.concatenate(
        [(own ^ k) * rows + jnp.arange(rows, dtype=jnp.int32) for k in range(members)]
    )
    cosine, sine = rotary_tables(position, KEY)
    head_numbers = (jnp.arange(heads_here, dtype=jnp.int32) + own * heads_here).astype(WIDE)
    rates = jnp.log1p(-jnp.exp2(-5.0 - head_numbers))
    rates = jnp.broadcast_to(rates[:, None], (heads_here, 128))
    outs = forward(
        resid_low,
        grad_local,
        gain_rows,
        cosine,
        sine,
        segment_ids,
        rates,
        [w_query, w_key, w_value, w_gate, w_out.T, w_mlp_gate, w_mlp_up, w_mlp_down.T],
        lines,
        members,
    )
    normed_turned, grad_full, gains = outs[:3]
    query_weight, key_weight, value_weight, gate_weight, out_weight = outs[3:8]
    query, keys, values, gate_pre, grad_turned = outs[11:16]
    retained, mixed, resid_mid, mid_turned, gate_hidden, up_hidden, hidden = outs[16:]
    down_grad, mlp_gate_grad, mlp_up_grad, mid_all, mid_grad, hidden_out, gain_part = feed_backward(
        grad_full,
        grad_turned,
        mid_turned,
        hidden,
        resid_mid,
        gains,
        outs[8:11],
        (gate_hidden, up_hidden),
        lines,
        members,
    )
    out_weight_grad, gate_grad, value_grad, query_grad, key_grad, in_grad, gain_total = (
        retention_backward(
            [
                mixed,
                normed_turned,
                query,
                keys,
                values,
                cosine,
                sine,
                segment_ids.T,
                segment_ids,
                rates,
                resid_low,
                gains,
                gain_part,
            ],
            [mid_grad, mid_all, retained, gate_pre],
            [out_weight, gate_weight, value_weight, query_weight, key_weight],
            lines,
            members,
            slice_width,
        )
    )
    def add_up(pieces):
        return jnp.sum(pieces.astype(WIDE), axis=0)

    return (
        from_places(hidden_out).reshape(hidden_in.shape),
        from_places(in_grad).reshape(hidden_in.shape),
        gain_total[0],
        add_up(query_grad),
        add_up(key_grad),
        add_up(value_grad),
        add_up(gate_grad),
        add_up(out_weight_grad).T,
        gain_total[1],
        add_up(mlp_gate_grad),
        add_up(mlp_up_grad),
        add_up(down_grad).T,
    )


def solution(mesh):
    return jax.shard_map(
        on_device,
        mesh=mesh,
        in_specs=(
            P("dp", "tensor", None),
            P("dp", "tensor", None),
            P("dp", None),
            P("dp"),
            P("dp", "tensor"),
            P("dp", "tensor"),
            P("dp", "tensor"),
            P("dp", "tensor"),
            P("tensor", "dp"),
            P("dp"),
            P("dp", "tensor"),
            P("dp", "tensor"),
            P("tensor", "dp"),
        ),
        out_specs=(
            P("dp", "tensor", None),
            P("dp", "tensor", None),
            P("dp"),
            P("dp", "tensor"),
            P("dp", "tensor"),
            P("dp", "tensor"),
            P("dp", "tensor"),
            P("tensor", "dp"),
            P("dp"),
            P("dp", "tensor"),
            P("dp", "tensor"),
            P("tensor", "dp"),
        ),
        check_vma=False,
    )
```

```python
import functools
import math

import jax
import jax.numpy as jnp
from jax import lax
from jax.experimental import pallas as pl
from jax.experimental.pallas import tpu as pltpu
from jax.sharding import PartitionSpec as P

KEY = 256
VAL = 432
LOW = jnp.bfloat16
WIDE = jnp.float32
WEIGHTS = 8
MESH = pl.DeviceIdType.MESH
ANY = pl.BlockSpec(memory_space=pl.ANY)
INSIDE = pl.BlockSpec(memory_space=pltpu.VMEM)
ROOM = 60 * 1024 * 1024

def rotary_tables(position, width):
    half = width // 2
    frequency = 10000.0 ** (-2.0 * jnp.arange(half, dtype=jnp.int32).astype(WIDE) / width)
    angle = position.astype(WIDE)[:, None] * frequency[None, :]
    return (jnp.cos(angle), jnp.sin(angle))


def greet(peers):
    barrier = pltpu.get_barrier_semaphore()
    for peer in peers:
        pl.semaphore_signal(barrier, inc=1, device_id=peer, device_id_type=MESH)
    pl.semaphore_wait(barrier, len(peers))


def remote(source, target, send, recv, device):
    return pltpu.make_async_remote_copy(
        src_ref=source,
        dst_ref=target,
        send_sem=send,
        recv_sem=recv,
        device_id=device,
        device_id_type=MESH,
    )


def forward_kernel(lines, members, *refs):
    hidden_ref, grad_ref, gain_ref, cos_ref, sin_ref, down_seg, along_seg, rate_ref = refs[:8]
    shards = refs[8:16]
    normed_turned, grad_all, gain_all = refs[16:19]
    wholes = refs[19:27]
    query_out, keys_out, values_out, gate_out, grad_turned = refs[27:32]
    retained_out, mixed_out, resid_out, mid_turned, gate_hidden_out, up_hidden_out = refs[32:38]
    hidden_out = refs[38]
    normed, mid, short, wide_one, wide_two, turned = refs[39:45]
    query, keys, scores, values, retained, gate, mixed, hidden = refs[45:53]
    held, got, base = refs[53:56]
    line_send, line_recv, side_send, side_recv = refs[56:60]
    near_send, near_recv, gain_send, gain_recv, home = refs[60:]

    parts = 2 * lines
    rows, width = hidden_ref.shape
    slice_width = gain_ref.shape[1]
    heads = rate_ref.shape[0]
    value_columns = values.shape[2]
    me = lax.axis_index("dp")
    line, side = me // 2, lax.rem(me, 2)
    here = side * lines + line
    own = lax.axis_index("tensor")
    half, rest = own // 2, lax.rem(own, 2)

    def member(k):
        return 2 * lax.rem(half + k // 2, 2) + lax.rem(rest + lax.rem(k, 2), 2)

    partners = [None] + [{"tensor": member(k)} for k in range(1, members)]
    others = [{"dp": lax.rem(me + k, parts)} for k in range(1, parts)]
    opposite = {"dp": 2 * line + (1 - side)}
    greet(others + partners[1:])

    local = {}
    slots = iter(range(32))

    def keep(source, target):
        slot = next(slots)
        local[slot] = pltpu.make_async_copy(source, target, home.at[slot])
        local[slot].start()
        return slot

    def finish(slot):
        local.pop(slot).wait()

    near = {}

    def near_start(tag, source, target, k):
        copy = remote(source, target, near_send.at[tag], near_recv.at[tag], partners[k])
        copy.start()
        near[tag] = copy

    across = {}
    ours = {}

    inner = lines == 4

    def line_copy(w, step):
        return remote(
            shards[w],
            wholes[w].at[here],
            line_send.at[w, step],
            line_recv.at[w, step],
            {"dp": 2 * lax.rem(line + step, lines) + side},
        )

    def relay_copy(w):
        place = side * lines + 3 * (2 - line)
        return remote(
            wholes[w].at[place],
            wholes[w].at[place],
            line_send.at[w, 0],
            line_recv.at[w, 2 * line - 1],
            {"dp": 6 * (line - 1) + side},
        )

    def side_copy(w, step):
        place = side * lines + lax.rem(line + lines - step, lines)
        return remote(
            wholes[w].at[place],
            wholes[w].at[place],
            side_send.at[w, step],
            side_recv.at[w, step],
            opposite,
        )

    def on_line(w, step, act):
        if inner and step != 2:

            @pl.when(line != (3 if step == 1 else 0))
            def _():
                act(line_copy(w, step))
        else:
            act(line_copy(w, step))

    sends = [2, 1, 3] if inner else list(range(1, lines))

    def start_lines(w):
        for step in sends:
            on_line(w, step, lambda copy: copy.start())
        across[w, 0] = remote(
            shards[w], wholes[w].at[here], side_send.at[w, 0], side_recv.at[w, 0], opposite
        )
        across[w, 0].start()
        ours[w] = keep(shards[w], wholes[w].at[here])

    def pass_on(w, third):
        for at in range(third * (lines - 1) // 3, (third + 1) * (lines - 1) // 3):
            step = at + 1
            if inner:
                late = 3 - 2 * ((3 - line) // 3)
                step = [2, 4 - late, late][at]
            line_copy(w, step).wait_recv()
            if inner and at == 0:

                @pl.when((line == 1) | (line == 2))
                def _():
                    relay_copy(w).start()

            side_copy(w, step).start()

    def complete(w):
        across[w, 0].wait_recv()
        for step in range(1, lines):
            side_copy(w, step).wait_recv()
        finish(ours[w])

    def load(w, target, sem):
        copy = pltpu.make_async_copy(wholes[w], target, sem)
        copy.start()
        copy.wait()

    def stage(w, target, body):
        if w + 1 < WEIGHTS:
            pass_on(w + 1, 0)
        complete(w)
        load(w, target, home.at[home.shape[0] - 1 - w])
        lax.fori_loop(0, members // 2, body, 0)
        if w + 1 < WEIGHTS:
            pass_on(w + 1, 1)
        lax.fori_loop(members // 2, members, body, 0)
        if w + 1 < WEIGHTS:
            pass_on(w + 1, 2)
        if w + 3 < WEIGHTS:
            start_lines(w + 3)

    gains = []
    for k in range(1, parts):
        copy = remote(
            gain_ref, gain_all.at[here], gain_send.at[k], gain_recv.at[k], others[k - 1]
        )
        copy.start()
        gains.append(copy)
    gain_all[here] = gain_ref[...]
    for w in range(3):
        start_lines(w)

    def scale_into(target, scaled, which):
        for p in range(parts):
            columns = slice(p * slice_width, (p + 1) * slice_width)
            target[0, :, columns] = (
                scaled[:, columns] * gain_all[p][which : which + 1]
            ).astype(LOW)

    resid = hidden_ref[...].astype(WIDE)
    scaled = resid * lax.rsqrt(jnp.mean(resid * resid, axis=-1, keepdims=True) + 1e-06)
    for copy in gains:
        copy.wait_recv()
    scale_into(normed, scaled, 0)
    for k in range(1, members):
        near_start(k - 1, normed.at[0], normed.at[k], k)
    for k in range(1, members):
        near_start(2 + k, grad_ref, mid.at[k], k)
    grad_kept = keep(grad_ref, mid.at[0])
    for third in range(3):
        pass_on(0, third)
    for k in range(1, members):
        near[k - 1].wait_recv()

    def turn_over(source):
        tile = 256

        def body(k, carry):
            at = pl.ds(pl.multiple_of(k * rows, rows), rows)
            for c in range(width // tile):
                columns = slice(c * tile, (c + 1) * tile)
                turned[columns, at] = source[k, :, columns].T
            return carry

        lax.fori_loop(0, members, body, 0)

    turn_over(normed)
    turned_kept = keep(turned, normed_turned)

    def flat(ref):
        return ref[...].reshape(width, ref.shape[2])

    def turn(source, target, scale):
        def body(k, carry):
            pre = jnp.dot(normed[k], flat(source), preferred_element_type=WIDE)
            at = pl.ds(pl.multiple_of(k * rows, rows), rows)
            cosine, sine = cos_ref[at, :], sin_ref[at, :]
            wing = KEY // 2
            for h in range(heads):
                first = pre[:, h * KEY : h * KEY + wing]
                second = pre[:, h * KEY + wing : (h + 1) * KEY]
                target[k, :, h * KEY : h * KEY + wing] = (
                    (first * cosine - second * sine) * scale
                ).astype(LOW)
                target[k, :, h * KEY + wing : (h + 1) * KEY] = (
                    (second * cosine + first * sine) * scale
                ).astype(LOW)
            return carry

        return body

    stage(0, short, turn(short, query, KEY ** (-0.5)))
    keep(query, query_out)
    stage(1, short, turn(short, keys, 1.0))
    keep(keys, keys_out)

    def score(k, carry):
        place = member(k)
        at = pl.multiple_of(place * rows, rows)
        segment = down_seg[pl.ds(at, rows), :]
        for h in range(heads):
            head = slice(h * KEY, (h + 1) * KEY)
            for m in range(members):
                start = pl.multiple_of(member(m) * rows, rows)
                raw = lax.dot_general(
                    query[k, :, head],
                    keys[m, :, head],
                    (((1,), (1,)), ((), ())),
                    preferred_element_type=WIDE,
                )
                distance = (
                    lax.broadcasted_iota(jnp.int32, (rows, rows), 0)
                    - lax.broadcasted_iota(jnp.int32, (rows, rows), 1)
                    + (at - start)
                )
                same = (distance >= 0) & (segment == along_seg[:, pl.ds(start, rows)])
                decay = jnp.exp(
                    rate_ref[h : h + 1, :1] * jnp.maximum(distance, 0).astype(WIDE)
                )
                scores[h, k, :, m * rows : (m + 1) * rows] = (
                    raw * jnp.where(same, decay, 0.0)
                ).astype(LOW)
        return carry

    lax.fori_loop(0, members, score, 0)
    finish(grad_kept)
    for k in range(1, members):
        near[2 + k].wait_recv()
    finish(turned_kept)
    turn_over(mid)
    turned_kept = keep(turned, grad_turned)
    grad_kept = keep(mid, grad_all)

    column = lax.broadcasted_iota(jnp.int32, (rows, value_columns), 1)

    def by_head(parts_of):
        result = parts_of[0]
        for h in range(1, heads):
            result = jnp.where(column < h * VAL, result, parts_of[h])
        return result

    def head_mean(value):
        means = []
        for h in range(heads):
            inside = (column >= h * VAL) & (column < (h + 1) * VAL)
            total = jnp.sum(jnp.where(inside, value, 0.0), axis=-1, keepdims=True)
            means.append(total * (1.0 / VAL))
        return by_head(means)

    def make_values(k, carry):
        values[k] = jnp.dot(normed[k], flat(wide_one), preferred_element_type=WIDE).astype(LOW)
        return carry

    stage(2, wide_one, make_values)
    keep(values, values_out)

    def retain(k, carry):
        every = values[...].reshape(members * rows, value_columns)
        retained[k] = by_head(
            [
                jnp.dot(scores[h, k], every, preferred_element_type=WIDE)
                for h in range(heads)
            ]
        )
        return carry

    lax.fori_loop(0, members, retain, 0)
    retained_kept = keep(retained, retained_out)

    def make_mixed(k, carry):
        pre = jnp.dot(normed[k], flat(wide_two), preferred_element_type=WIDE)
        gate[k] = pre
        value = retained[k]
        centred = value - head_mean(value)
        grouped = centred * lax.rsqrt(head_mean(centred * centred) + 1.0)
        mixed[k] = (grouped * (pre / (1.0 + jnp.exp(-pre)))).astype(LOW)
        return carry

    stage(3, wide_two, make_mixed)
    gate_kept = keep(gate, gate_out)
    keep(mixed, mixed_out)

    def project(k, put):
        for p in range(parts):
            columns = slice(p * slice_width, (p + 1) * slice_width)
            put(
                columns,
                lax.dot_general(
                    mixed[k],
                    wide_one[p],
                    (((1,), (1,)), ((), ())),
                    preferred_element_type=WIDE,
                ),
            )

    def put_low(slot):
        def put(columns, value):
            held[slot, :, columns] = value.astype(LOW)

        return put

    def put_sum(columns, value):
        base[:, columns] = value

    pass_on(5, 0)
    complete(4)
    load(4, wide_one, home.at[home.shape[0] - 5])
    finish(grad_kept)
    project(3, put_low(0))
    near_start(6, held.at[0], got.at[0], 1)
    project(2, put_sum)
    pass_on(5, 1)
    near[6].wait_recv()
    held[1] = (base[...] + got[0].astype(WIDE)).astype(LOW)
    near_start(8, held.at[1], got.at[1], 2)
    project(1, put_low(2))
    near_start(7, held.at[2], got.at[2], 1)
    project(0, put_sum)
    pass_on(5, 2)
    start_lines(7)
    near[7].wait_recv()
    base[...] = base[...] + got[2].astype(WIDE) + hidden_ref[...].astype(WIDE)
    pass_on(6, 0)
    near[8].wait_recv()
    resid = base[...] + got[1].astype(WIDE)
    resid_out[...] = resid
    scaled = resid * lax.rsqrt(jnp.mean(resid * resid, axis=-1, keepdims=True) + 1e-06)
    scale_into(mid, scaled, 1)
    near_start(10, mid.at[0], mid.at[2], 2)
    near_start(9, mid.at[0], mid.at[1], 1)
    pass_on(6, 1)
    pass_on(6, 2)
    near[10].wait_recv()
    near_start(11, mid.at[2], mid.at[3], 1)
    complete(5)
    load(5, wide_two, home.at[home.shape[0] - 6])
    near[9].wait_recv()
    near[11].wait_recv()
    finish(retained_kept)
    finish(gate_kept)

    def make_gate(k, carry):
        gate[k] = jnp.dot(mid[k], flat(wide_two), preferred_element_type=WIDE)
        return carry

    lax.fori_loop(0, members, make_gate, 0)
    keep(gate, gate_hidden_out)
    finish(turned_kept)
    turn_over(mid)
    keep(turned, mid_turned)
    pass_on(7, 0)
    pass_on(7, 1)
    pass_on(7, 2)
    complete(6)
    load(6, wide_one, home.at[home.shape[0] - 7])

    def make_hidden(k, carry):
        up = jnp.dot(mid[k], flat(wide_one), preferred_element_type=WIDE)
        retained[k] = up
        pre = gate[k]
        inner = (2.0 / math.pi) ** 0.5 * (pre + 0.044715 * (pre * pre * pre))
        hidden[k] = (0.5 * pre * (1.0 + jnp.tanh(inner)) * up).astype(LOW)
        return carry

    lax.fori_loop(0, members, make_hidden, 0)
    keep(retained, up_hidden_out)
    keep(hidden, hidden_out)
    complete(7)
    for w in range(WEIGHTS):
        for step in sends:
            on_line(w, step, lambda copy: copy.wait_send())
            side_copy(w, step).wait_send()
        across[w, 0].wait_send()
        if inner:

            @pl.when((line == 1) | (line == 2))
            def _():
                relay_copy(w).wait_send()

    for copy in gains:
        copy.wait_send()
    for copy in near.values():
        copy.wait_send()
    for slot in list(local):
        finish(slot)


def forward(hidden, grad, gains, cosine, sine, segments, rates, shards, lines, members):
    parts = 2 * lines
    rows, width = hidden.shape
    heads = rates.shape[0]
    key_columns, value_columns = shards[0].shape[1], shards[2].shape[1]
    length = rows * members
    blocks = (members, rows)
    turned = (width, length)
    outs = [
        (turned, LOW),
        (blocks + (width,), LOW),
        ((parts,) + gains.shape, WIDE),
    ]
    outs += [((parts,) + shard.shape, LOW) for shard in shards]
    outs += [
        (blocks + (key_columns,), LOW),
        (blocks + (key_columns,), LOW),
        (blocks + (value_columns,), LOW),
        (blocks + (value_columns,), WIDE),
        (turned, LOW),
        (blocks + (value_columns,), WIDE),
        (blocks + (value_columns,), LOW),
        ((rows, width), WIDE),
        (turned, LOW),
        (blocks + (value_columns,), WIDE),
        (blocks + (value_columns,), WIDE),
        (blocks + (value_columns,), LOW),
    ]
    places = [ANY] * len(outs)
    places[2] = INSIDE
    places[18] = INSIDE
    tags = 12
    return pl.pallas_call(
        functools.partial(forward_kernel, lines, members),
        out_shape=[jax.ShapeDtypeStruct(shape, dtype) for shape, dtype in outs],
        in_specs=[INSIDE, ANY] + [INSIDE] * 6 + [ANY] * WEIGHTS,
        out_specs=places,
        scratch_shapes=[
            pltpu.VMEM(blocks + (width,), LOW),
            pltpu.VMEM(blocks + (width,), LOW),
            pltpu.VMEM((parts,) + shards[0].shape, LOW),
            pltpu.VMEM((parts,) + shards[2].shape, LOW),
            pltpu.VMEM((parts,) + shards[2].shape, LOW),
            pltpu.VMEM(turned, LOW),
            pltpu.VMEM(blocks + (key_columns,), LOW),
            pltpu.VMEM(blocks + (key_columns,), LOW),
            pltpu.VMEM((heads, members, rows, length), LOW),
            pltpu.VMEM(blocks + (value_columns,), LOW),
            pltpu.VMEM(blocks + (value_columns,), WIDE),
            pltpu.VMEM(blocks + (value_columns,), WIDE),
            pltpu.VMEM(blocks + (value_columns,), LOW),
            pltpu.VMEM(blocks + (value_columns,), LOW),
            pltpu.VMEM((3, rows, width), LOW),
            pltpu.VMEM((3, rows, width), LOW),
            pltpu.VMEM((rows, width), WIDE),
            pltpu.SemaphoreType.DMA((WEIGHTS, lines)),
            pltpu.SemaphoreType.DMA((WEIGHTS, lines)),
            pltpu.SemaphoreType.DMA((WEIGHTS, lines)),
            pltpu.SemaphoreType.DMA((WEIGHTS, lines)),
            pltpu.SemaphoreType.DMA((tags,)),
            pltpu.SemaphoreType.DMA((tags,)),
            pltpu.SemaphoreType.DMA((parts,)),
            pltpu.SemaphoreType.DMA((parts,)),
            pltpu.SemaphoreType.DMA((40,)),
        ],
        compiler_params=pltpu.CompilerParams(
            collective_id=0, has_side_effects=True, vmem_limit_bytes=ROOM
        ),
        cost_estimate=pl.CostEstimate(
            flops=10**11, bytes_accessed=10**9, transcendentals=0
        ),
        name="forward",
    )(hidden, grad, gains, cosine, sine, segments.T, segments, rates, *shards)


class Scatter:
    def __init__(self, lines, held, far_got, near_got, spare, sems):
        self.lines = lines
        self.held, self.far_got, self.near_got, self.spare = held, far_got, near_got, spare
        self.side_send, self.side_recv, self.line_send, self.line_recv, self.home = sems
        me = lax.axis_index("dp")
        self.line, self.side = me // 2, lax.rem(me, 2)
        self.opposite = {"dp": 2 * self.line + (1 - self.side)}

    def peer(self, step):
        return {"dp": 2 * lax.rem(self.line + step, self.lines) + self.side}

    def peers(self):
        return [self.opposite] + [self.peer(step) for step in range(1, self.lines)]

    def far_copy(self, w, place):
        return remote(
            self.held[w].at[place],
            self.far_got[w].at[place],
            self.side_send.at[w, place],
            self.side_recv.at[w, place],
            self.opposite,
        )

    def near_copy(self, w, step):
        place = lax.rem(self.line + step, self.lines)
        return remote(
            self.held[w].at[place],
            self.near_got[w].at[step],
            self.line_send.at[w, step],
            self.line_recv.at[w, step],
            self.peer(step),
        )

    def fetch(self, source):
        spare = self.spare[source.shape[-1]]
        copy = pltpu.make_async_copy(source, spare, self.home)
        copy.start()
        copy.wait()
        return spare[...].astype(WIDE)

    def product(self, left, right, place):
        rows = self.held[0].shape[1]
        block = left[pl.ds(pl.multiple_of(place * rows, rows), rows), :]
        every = right[...]
        return jnp.dot(
            block,
            every.reshape(every.shape[0] * every.shape[1], every.shape[2]),
            preferred_element_type=WIDE,
        )


    def extra_copy(self, w, step):
        place = lax.rem(self.line + step, self.lines)
        return remote(
            self.held[w].at[place],
            self.far_got[w].at[self.lines],
            self.line_send.at[w, step],
            self.line_recv.at[w, 0],
            {"dp": 2 * (2 if step == 1 else 1) + self.side},
        )

    def far(self, w, left, right):
        def body(at, carry):
            step = 1 + at
            if self.lines == 4:
                step = 1 + 2 * at - 3 * (at // 2)
            place = lax.rem(self.line + step, self.lines)
            other = (1 - self.side) * self.lines + place
            self.held[w][place] = self.product(left, right, other).astype(LOW)
            self.far_copy(w, place).start()
            return carry

        lax.fori_loop(0, self.lines, body, 0)

    def near(self, w, left, right, quarter):
        def add(place):
            part = self.product(left, right, self.side * self.lines + place)
            self.far_copy(w, place).wait_recv()
            total = part + self.fetch(self.far_got[w].at[place])
            self.far_copy(w, place).wait_send()
            return total

        def body(step, carry):
            place = lax.rem(self.line + step, self.lines)
            self.held[w][place] = add(place).astype(LOW)
            self.near_copy(w, step).start()
            return carry

        if self.lines != 4:
            first, last = [1 + (quarter + k) * self.lines // 4 for k in range(2)]
            lax.fori_loop(first, min(last, self.lines), body, 0)
        elif quarter < 2:
            step = 1 + 2 * quarter
            end = 3 - 3 * quarter
            place = lax.rem(self.line + step, self.lines)
            self.held[w][place] = add(place).astype(LOW)

            @pl.when(self.line == end)
            def _():
                self.extra_copy(w, step).start()

            @pl.when(self.line != end)
            def _():
                self.near_copy(w, step).start()
        elif quarter == 2:
            place = lax.rem(self.line + 2, self.lines)
            total = add(place)
            self.held[w][place] = total.astype(LOW)

            @pl.when((self.line == 1) | (self.line == 2))
            def _():
                self.extra_copy(w, 1).wait_recv()
                self.held[w][place] = (
                    self.held[w][place].astype(WIDE)
                    + self.fetch(self.far_got[w].at[self.lines])
                ).astype(LOW)

            self.near_copy(w, 2).start()
        if quarter < 3:
            return
        self.held[w][self.line] = add(self.line).astype(LOW)
        self.own_copy(w).start()
        if self.lines == 4:

            @pl.when((self.line == 0) | (self.line == 3))
            def _():
                spare = self.spare[self.held[w].shape[2]]
                spare[...] = jnp.zeros(spare.shape, LOW)
                slot = 1 + 2 * (self.line // 3)
                copy = pltpu.make_async_copy(spare, self.near_got[w].at[slot], self.home)
                copy.start()
                copy.wait()

    def own_copy(self, w):
        return pltpu.make_async_copy(
            self.held[w].at[self.line], self.near_got[w].at[0], self.line_send.at[w, 0]
        )

    def finish(self, w):
        if self.lines != 4:

            def body(step, carry):
                self.near_copy(w, step).wait()
                return carry

            lax.fori_loop(1, self.lines, body, 0)
        else:
            for step in range(1, 4):
                copy = self.near_copy(w, step)
                copy.wait_send()
                if step == 2:
                    copy.wait_recv()
                else:

                    @pl.when(self.line != (0 if step == 1 else 3))
                    def _():
                        copy.wait_recv()

        self.own_copy(w).wait()


class Near:
    def __init__(self, send, recv):
        self.send, self.recv = send, recv
        self.flight = {}
        own = lax.axis_index("tensor")
        half, rest = own // 2, lax.rem(own, 2)
        self.member = lambda k: 2 * lax.rem(half + k // 2, 2) + lax.rem(rest + lax.rem(k, 2), 2)

    def partners(self, members):
        return [{"tensor": self.member(k)} for k in range(1, members)]

    def start(self, tag, source, target, k):
        copy = remote(source, target, self.send.at[tag], self.recv.at[tag], self.partners(4)[k - 1])
        copy.start()
        self.flight[tag] = copy

    def wait(self, tag):
        self.flight[tag].wait_recv()

    def sent(self, tag):
        self.flight[tag].wait_send()


def dot_across(left, right):
    return lax.dot_general(
        left, right, (((1,), (1,)), ((), ())), preferred_element_type=WIDE
    )


def feed_kernel(lines, members, *refs):
    grad_turned, hidden, gain_all = refs[:3]
    later = refs[3:9]
    gate_hidden, up_hidden = refs[9:11]
    near_got, mid_all, mid_grad_out, hidden_out, gain_out = refs[11:14], *refs[14:18]
    far_got = refs[18:21]
    gate_low, up_low, pre, up = refs[21:25]
    scatter_held = refs[25:28]
    spare, held, got, last, base, mid = refs[28:34]
    sems = refs[34:38]
    near_send, near_recv, home = refs[38:41]
    loaded = refs[41:]
    grad_ref, mid_turned, resid_ref, gate_weight, up_weight, down_weight = loaded
    parts = 2 * lines
    rows, width = resid_ref.shape
    loads = []
    for k, order in enumerate((5, 0, 1, 3, 4, 2)):
        loads.append(pltpu.make_async_copy(later[order], loaded[order], home.at[4 + k]))
        loads[k].start()
    slice_width = width // parts
    scatter = Scatter(
        lines,
        scatter_held,
        far_got,
        near_got,
        {spare.shape[1]: spare},
        sems + (home.at[0],),
    )
    near = Near(near_send, near_recv)
    greet(scatter.peers() + near.partners(members))
    scatter.far(0, grad_turned, hidden)

    def flat(ref):
        return ref[...].reshape(width, ref.shape[2])

    def pull(k, carry):
        first = pltpu.make_async_copy(gate_hidden.at[k], pre, home.at[1])
        second = pltpu.make_async_copy(up_hidden.at[k], up, home.at[2])
        first.start()
        second.start()
        grad = jnp.dot(grad_ref[k], flat(down_weight), preferred_element_type=WIDE)
        first.wait()
        second.wait()
        value = pre[...]
        root = (2.0 / math.pi) ** 0.5
        square = value * value
        lift = jnp.tanh(root * (value + 0.044715 * (value * square)))
        ramp = 0.5 * (1.0 + lift)
        slope = ramp + 0.5 * value * (1.0 - lift * lift) * root * (1.0 + 0.134145 * square)
        gate_low[k] = (grad * up[...] * slope).astype(LOW)
        up_low[k] = (grad * (value * ramp)).astype(LOW)
        return carry

    for load in loads:
        load.wait()
    lax.fori_loop(0, members // 2, pull, 0)
    scatter.near(0, grad_turned, hidden, 0)
    lax.fori_loop(members // 2, members, pull, 0)
    scatter.near(0, grad_turned, hidden, 1)
    scatter.far(1, mid_turned, gate_low)

    def back(k, put):
        for p in range(parts):
            columns = slice(p * slice_width, (p + 1) * slice_width)
            put(
                columns,
                dot_across(gate_low[k], gate_weight[p]) + dot_across(up_low[k], up_weight[p]),
            )

    def put_low(slot):
        def put(columns, value):
            held[slot, :, columns] = value.astype(LOW)

        return put

    def put_sum(columns, value):
        base[:, columns] = value

    back(3, put_low(0))
    near.start(0, held.at[0], got.at[0], 1)
    scatter.near(0, grad_turned, hidden, 2)
    back(2, put_sum)
    near.wait(0)
    near.sent(0)
    held[0] = (base[...] + got[0].astype(WIDE)).astype(LOW)
    near.start(1, held.at[0], got.at[1], 2)
    back(1, put_low(1))
    near.start(2, held.at[1], got.at[2], 1)
    scatter.near(0, grad_turned, hidden, 3)
    back(0, put_sum)
    scatter.far(2, mid_turned, up_low)
    scatter.near(1, mid_turned, gate_low, 0)
    near.wait(2)
    base[...] += got[2].astype(WIDE)
    scatter.near(1, mid_turned, gate_low, 1)
    near.wait(1)
    normed_grad = base[...] + got[1].astype(WIDE)
    resid = resid_ref[...]
    scale = lax.rsqrt(jnp.mean(resid * resid, axis=-1, keepdims=True) + 1e-06)
    unit = resid * scale
    base[...] = normed_grad * unit
    gain_out[...] = jnp.broadcast_to(
        jnp.sum(base[...], axis=0, keepdims=True), gain_out.shape
    )
    dot = jnp.zeros((rows, 1), WIDE)
    for p in range(parts):
        columns = slice(p * slice_width, (p + 1) * slice_width)
        dot += jnp.sum(base[:, columns] * gain_all[p][1:2], axis=-1, keepdims=True)
    dot = dot * (1.0 / width)
    base[...] = normed_grad
    for p in range(parts):
        columns = slice(p * slice_width, (p + 1) * slice_width)
        block = resid_ref[:, columns] * scale
        mid_grad = grad_ref[0, :, columns].astype(WIDE) + scale * (
            base[:, columns] * gain_all[p][1:2] - block * dot
        )
        base[:, columns] = mid_grad
        mid[:, columns] = mid_grad.astype(LOW)
    mid_grad_copy = pltpu.make_async_copy(base, mid_grad_out, home.at[1])
    mid_grad_copy.start()
    near.start(3, mid, mid_all.at[2], 2)
    near.start(4, mid, mid_all.at[1], 1)
    own = pltpu.make_async_copy(mid, mid_all.at[0], home.at[3])
    own.start()
    scatter.near(1, mid_turned, gate_low, 2)
    scatter.near(1, mid_turned, gate_low, 3)

    def down(k, put):
        for p in range(parts):
            columns = slice(p * slice_width, (p + 1) * slice_width)
            put(columns, dot_across(hidden[k], down_weight[p]))

    near.sent(1)
    near.sent(2)
    down(3, put_low(0))
    mid_grad_copy.wait()
    near.start(6, held.at[0], last.at[0], 1)
    down(2, put_sum)
    scatter.near(2, mid_turned, up_low, 0)
    near.wait(3)
    near.start(5, mid_all.at[2], mid_all.at[3], 1)
    near.wait(6)
    near.sent(6)
    held[0] = (base[...] + last[0].astype(WIDE)).astype(LOW)
    near.start(7, held.at[0], last.at[1], 2)
    down(1, put_low(1))
    near.start(8, held.at[1], last.at[2], 1)
    scatter.near(2, mid_turned, up_low, 1)
    down(0, put_sum)
    scatter.near(2, mid_turned, up_low, 2)
    scatter.near(2, mid_turned, up_low, 3)
    near.wait(8)
    near.wait(7)
    own.wait()
    near.sent(3)
    near.sent(4)
    mid[...] = (
        base[...] + last[2].astype(WIDE) + last[1].astype(WIDE) + resid_ref[...]
    ).astype(LOW)
    own = pltpu.make_async_copy(mid, hidden_out, home.at[3])
    own.start()
    for w in range(3):
        scatter.finish(w)
    near.wait(4)
    near.wait(5)
    own.wait()
    for tag in (5, 7, 8):
        near.sent(tag)


def feed_backward(
    grad, grad_turned, mid_turned, hidden, resid, gains, weights, pres, lines, members
):
    parts = 2 * lines
    rows, width = resid.shape
    columns = hidden.shape[2]
    slice_width = width // parts
    blocks = (members, rows)
    piece = (lines, slice_width, columns)
    later = [grad, mid_turned, resid, *weights]
    outs = [(piece, LOW)] * 3
    outs += [
        (blocks + (width,), LOW),
        ((rows, width), WIDE),
        ((rows, width), LOW),
        ((8, width), WIDE),
    ]
    outs += [((lines + 1,) + piece[1:], LOW)] * 3
    return pl.pallas_call(
        functools.partial(feed_kernel, lines, members),
        out_shape=[jax.ShapeDtypeStruct(shape, dtype) for shape, dtype in outs],
        in_specs=[INSIDE] * 3 + [ANY] * 8,
        out_specs=[ANY] * 6 + [INSIDE] + [ANY] * 3,
        scratch_shapes=[
            pltpu.VMEM(blocks + (columns,), LOW),
            pltpu.VMEM(blocks + (columns,), LOW),
            pltpu.VMEM((rows, columns), WIDE),
            pltpu.VMEM((rows, columns), WIDE),
            pltpu.VMEM(piece, LOW),
            pltpu.VMEM(piece, LOW),
            pltpu.VMEM(piece, LOW),
            pltpu.VMEM(piece[1:], LOW),
            pltpu.VMEM((2, rows, width), LOW),
            pltpu.VMEM((3, rows, width), LOW),
            pltpu.VMEM((3, rows, width), LOW),
            pltpu.VMEM((rows, width), WIDE),
            pltpu.VMEM((rows, width), LOW),
            pltpu.SemaphoreType.DMA((3, lines)),
            pltpu.SemaphoreType.DMA((3, lines)),
            pltpu.SemaphoreType.DMA((3, lines)),
            pltpu.SemaphoreType.DMA((3, lines)),
            pltpu.SemaphoreType.DMA((9,)),
            pltpu.SemaphoreType.DMA((9,)),
            pltpu.SemaphoreType.DMA((10,)),
        ]
        + [pltpu.VMEM(value.shape, value.dtype) for value in later],
        compiler_params=pltpu.CompilerParams(
            collective_id=1, has_side_effects=True, vmem_limit_bytes=ROOM
        ),
        cost_estimate=pl.CostEstimate(flops=10**11, bytes_accessed=10**9, transcendentals=0),
        name="feed_backward",
    )(grad_turned, hidden, gains, *later, *pres)[:7]


def retention_kernel(lines, members, *refs):
    later = refs[:5]
    cos_ref, sin_ref, down_seg, along_seg, rate_ref = refs[5:10]
    hidden_ref, gain_all, gain_part = refs[10:13]
    mid_grad_ref, mid_all, retained_all, gate_all = refs[13:17]
    weights = refs[17:22]
    near_got, in_grad_out, gain_out = refs[22:27], refs[27], refs[28]
    far_got = refs[29:34]
    turned, wide_one, wide_two, short_one, short_two = refs[34:39]
    gate_low, retained_low, query_low, key_low = refs[39:43]
    scatter_held = refs[43:48]
    spare_wide, spare_short, held, got, base, retained, gate = refs[48:55]
    pieces, piece_got, total, total_got = refs[55:59]
    sems = refs[59:63]
    near_send, near_recv, gain_send, gain_recv, home = refs[63:68]
    loaded = refs[68:]
    mixed, normed_turned, query, keys, values = loaded
    value_low = mixed
    parts = 2 * lines
    rows, width = hidden_ref.shape
    slice_width = width // parts
    heads = rate_ref.shape[0]
    value_columns = values.shape[2]
    length = rows * members
    scatter = Scatter(
        lines,
        scatter_held,
        far_got,
        near_got,
        {spare_wide.shape[1]: spare_wide, spare_short.shape[1]: spare_short},
        sems + (home.at[0],),
    )
    near = Near(near_send, near_recv)
    me = lax.axis_index("dp")
    here = scatter.side * lines + scatter.line
    others = [{"dp": lax.rem(me + k, parts)} for k in range(1, parts)]
    greet(others + near.partners(members))

    def fetch(source, target, sem):
        copy = pltpu.make_async_copy(source, target, home.at[sem])
        copy.start()
        return copy

    out_copy = fetch(weights[0], wide_one, 1)
    value_copy = fetch(weights[2], wide_two, 2)
    query_copy = fetch(weights[3], short_one, 3)
    key_copy = fetch(weights[4], short_two, 4)
    grad_copy = fetch(mid_grad_ref, in_grad_out, 7)
    loads = [fetch(later[k], loaded[k], 9 + k) for k in range(5)]

    def turn_over(k, carry):
        fetch(mid_all.at[k], held.at[0], 8).wait()
        at = pl.ds(pl.multiple_of(k * rows, rows), rows)
        for c in range(width // 256):
            columns = slice(c * 256, (c + 1) * 256)
            turned[columns, at] = held[0, :, columns].T
        return carry

    lax.fori_loop(0, members, turn_over, 0)
    loads[0].wait()
    scatter.far(0, turned, mixed)
    out_copy.wait()
    for load in loads[1:]:
        load.wait()

    column = lax.broadcasted_iota(jnp.int32, (rows, value_columns), 1)

    def by_head(parts_of):
        result = parts_of[0]
        for h in range(1, heads):
            result = jnp.where(column < h * VAL, result, parts_of[h])
        return result

    def inside(h):
        return (column >= h * VAL) & (column < (h + 1) * VAL)

    def head_mean(value):
        return by_head(
            [
                jnp.sum(jnp.where(inside(h), value, 0.0), axis=-1, keepdims=True) * (1.0 / VAL)
                for h in range(heads)
            ]
        )

    def unmix(k, carry):
        first = fetch(retained_all.at[k], retained, 5)
        second = fetch(gate_all.at[k], gate, 6)
        fetch(mid_all.at[k], held.at[0], 8).wait()
        grad = jnp.dot(
            held[0],
            wide_one[...].reshape(width, value_columns),
            preferred_element_type=WIDE,
        )
        first.wait()
        second.wait()
        value = retained[...]
        centred = value - head_mean(value)
        rate = lax.rsqrt(head_mean(centred * centred) + 1.0)
        pre = gate[...]
        sigma = 1.0 / (1.0 + jnp.exp(-pre))
        gate_low[k] = (
            grad * (centred * rate) * (sigma * (1.0 + pre * (1.0 - sigma)))
        ).astype(LOW)
        grouped_grad = grad * (pre * sigma)
        retained_low[k] = (
            rate * (grouped_grad - head_mean(grouped_grad))
            - (rate * rate * rate) * centred * head_mean(grouped_grad * centred)
        ).astype(LOW)
        return carry

    lax.fori_loop(0, members // 2, unmix, 0)
    scatter.near(0, turned, mixed, 0)
    lax.fori_loop(members // 2, members, unmix, 0)
    scatter.near(0, turned, mixed, 1)
    scatter.far(1, normed_turned, gate_low)
    gate_copy = fetch(weights[1], wide_one, 1)

    def decay(h, late, early, late_segment, early_segment, turn):
        sign = -1 if turn else 1
        distance = (
            sign
            * (
                lax.broadcasted_iota(jnp.int32, (rows, rows), 0)
                - lax.broadcasted_iota(jnp.int32, (rows, rows), 1)
            )
            + (late - early)
        )
        same = (distance >= 0) & (late_segment == early_segment)
        return jnp.where(
            same,
            jnp.exp(rate_ref[h : h + 1, :1] * jnp.maximum(distance, 0).astype(WIDE)),
            0.0,
        )

    def start_of(k):
        return pl.multiple_of(near.member(k) * rows, rows)

    wing = KEY // 2
    along = [along_seg[:, pl.ds(start_of(k), rows)] for k in range(members)]

    def turn_back(target, k, h, grad, scale):
        at = pl.ds(pl.multiple_of(k * rows, rows), rows)
        cosine, sine = cos_ref[at, :], sin_ref[at, :]
        first, second = grad[:, :wing], grad[:, wing:]
        target[k, :, h * KEY : h * KEY + wing] = (
            (first * cosine + second * sine) * scale
        ).astype(LOW)
        target[k, :, h * KEY + wing : (h + 1) * KEY] = (
            (second * cosine - first * sine) * scale
        ).astype(LOW)

    def early_side(m, carry):
        early = start_of(m)
        early_segment = down_seg[pl.ds(early, rows), :]
        value_grads = []
        for h in range(heads):
            head = slice(h * KEY, (h + 1) * KEY)
            masked = jnp.where(inside(h), values[m].astype(WIDE), 0.0).astype(LOW)
            value_grad = jnp.zeros((rows, value_columns), WIDE)
            key_grad = jnp.zeros((rows, KEY), WIDE)
            for n in range(members):
                late = start_of(n)
                late_segment = along[n]
                mask = decay(h, late, early, late_segment, early_segment, True)
                score = (dot_across(keys[m, :, head], query[n, :, head]) * mask).astype(LOW)
                raw = (dot_across(masked, retained_low[n]) * mask).astype(LOW)
                value_grad += jnp.dot(score, retained_low[n], preferred_element_type=WIDE)
                key_grad += jnp.dot(raw, query[n, :, head], preferred_element_type=WIDE)
            value_grads.append(value_grad)
            turn_back(key_low, m, h, key_grad, 1.0)
        value_low[m] = by_head(value_grads).astype(LOW)
        return carry

    scatter.near(0, turned, mixed, 2)
    scatter.near(0, turned, mixed, 3)
    early_side(0, 0)
    for m in range(1, members):
        early_side(m, 0)
        scatter.near(1, normed_turned, gate_low, m - 1)
    scatter.far(2, normed_turned, value_low)
    scatter.far(4, normed_turned, key_low)
    scatter.near(1, normed_turned, gate_low, 3)

    def late_side(n, carry):
        late = start_of(n)
        late_segment = down_seg[pl.ds(late, rows), :]
        for h in range(heads):
            head = slice(h * KEY, (h + 1) * KEY)
            masked = jnp.where(inside(h), retained_low[n].astype(WIDE), 0.0).astype(LOW)
            query_grad = jnp.zeros((rows, KEY), WIDE)
            for m in range(members):
                early = start_of(m)
                early_segment = along[m]
                mask = decay(h, late, early, late_segment, early_segment, False)
                raw = (dot_across(masked, values[m]) * mask).astype(LOW)
                query_grad += jnp.dot(raw, keys[m, :, head], preferred_element_type=WIDE)
            turn_back(query_low, n, h, query_grad, KEY ** (-0.5))
        return carry

    lax.fori_loop(0, members // 2, late_side, 0)
    scatter.near(2, normed_turned, value_low, 0)
    lax.fori_loop(members // 2, members, late_side, 0)
    scatter.near(2, normed_turned, value_low, 1)
    scatter.far(3, normed_turned, query_low)
    for copy in (gate_copy, value_copy, query_copy, key_copy, grad_copy):
        copy.wait()

    def back(k, put):
        for p in range(parts):
            columns = slice(p * slice_width, (p + 1) * slice_width)
            put(
                columns,
                dot_across(gate_low[k], wide_one[p])
                + dot_across(value_low[k], wide_two[p])
                + dot_across(query_low[k], short_one[p])
                + dot_across(key_low[k], short_two[p]),
            )

    def put_low(slot):
        def put(columns, value):
            held[slot, :, columns] = value.astype(LOW)

        return put

    def put_sum(columns, value):
        base[:, columns] = value

    back(3, put_low(0))
    near.start(0, held.at[0], got.at[0], 1)
    back(2, put_sum)
    scatter.near(2, normed_turned, value_low, 2)
    near.wait(0)
    near.sent(0)
    held[0] = (base[...] + got[0].astype(WIDE)).astype(LOW)
    near.start(1, held.at[0], got.at[1], 2)
    back(1, put_low(1))
    near.start(2, held.at[1], got.at[2], 1)
    scatter.near(2, normed_turned, value_low, 3)
    back(0, put_sum)
    for quarter in range(4):
        scatter.near(4, normed_turned, key_low, quarter)
    near.wait(2)
    base[...] += got[2].astype(WIDE)
    near.wait(1)
    normed_grad = base[...] + got[1].astype(WIDE)
    base[...] = normed_grad
    resid = hidden_ref[...].astype(WIDE)
    scale = lax.rsqrt(jnp.mean(resid * resid, axis=-1, keepdims=True) + 1e-06)
    dot = jnp.zeros((rows, 1), WIDE)
    for p in range(parts):
        columns = slice(p * slice_width, (p + 1) * slice_width)
        product = base[:, columns] * (hidden_ref[:, columns].astype(WIDE) * scale)
        row = lax.broadcasted_iota(jnp.int32, (8, slice_width), 0)
        pieces[p] = jnp.where(
            row == 0, jnp.sum(product, axis=0, keepdims=True), gain_part[:, columns]
        )
        dot += jnp.sum(product * gain_all[p][0:1], axis=-1, keepdims=True)
    dot = dot * (1.0 / width)
    gains = []
    for k in range(1, parts):
        other = lax.rem(me + k, parts)
        place = lax.rem(other, 2) * lines + other // 2
        copy = remote(
            pieces.at[place], piece_got.at[k], gain_send.at[k], gain_recv.at[k], others[k - 1]
        )
        copy.start()
        gains.append(copy)
    for p in range(parts):
        columns = slice(p * slice_width, (p + 1) * slice_width)
        block = hidden_ref[:, columns].astype(WIDE) * scale
        in_grad_out[:, columns] += scale * (
            base[:, columns] * gain_all[p][0:1] - block * dot
        )
    value = pieces[here]
    for k in range(1, parts):
        gains[k - 1].wait_recv()
        value = value + piece_got[k]
    total[...] = value
    for k in range(1, members):
        near.start(2 + k, total, total_got.at[k], k)
    for quarter in range(4):
        scatter.near(3, normed_turned, query_low, quarter)
    for w in (0, 1, 2, 4, 3):
        scatter.finish(w)
    for k in range(1, members):
        near.wait(2 + k)
        value = value + total_got[k]
    gain_out[...] = value
    for tag in range(1, 2 + members):
        near.sent(tag)
    for copy in gains:
        copy.wait_send()


def retention_backward(inside, streamed, weights, lines, members, slice_width):
    parts = 2 * lines
    rows, width = inside[10].shape
    blocks = (members, rows)
    wide, short = weights[0].shape[2], weights[3].shape[2]
    widths = [wide, wide, wide, short, short]
    pieces = [(lines, slice_width, columns) for columns in widths]
    outs = [(piece, LOW) for piece in pieces]
    outs += [((rows, width), WIDE), ((8, slice_width), WIDE)]
    outs += [((lines + 1,) + piece[1:], LOW) for piece in pieces]
    return pl.pallas_call(
        functools.partial(retention_kernel, lines, members),
        out_shape=[jax.ShapeDtypeStruct(shape, dtype) for shape, dtype in outs],
        in_specs=[ANY] * 5 + [INSIDE] * 8 + [ANY] * 9,
        out_specs=[ANY] * 5 + [INSIDE] * 2 + [ANY] * 5,
        scratch_shapes=[
            pltpu.VMEM((width, rows * members), LOW),
            pltpu.VMEM(weights[0].shape, LOW),
            pltpu.VMEM(weights[0].shape, LOW),
            pltpu.VMEM(weights[3].shape, LOW),
            pltpu.VMEM(weights[3].shape, LOW),
            pltpu.VMEM(blocks + (wide,), LOW),
            pltpu.VMEM(blocks + (wide,), LOW),
            pltpu.VMEM(blocks + (short,), LOW),
            pltpu.VMEM(blocks + (short,), LOW),
        ]
        + [pltpu.VMEM(piece, LOW) for piece in pieces]
        + [
            pltpu.VMEM((slice_width, wide), LOW),
            pltpu.VMEM((slice_width, short), LOW),
            pltpu.VMEM((2, rows, width), LOW),
            pltpu.VMEM((3, rows, width), LOW),
            pltpu.VMEM((rows, width), WIDE),
            pltpu.VMEM((rows, wide), WIDE),
            pltpu.VMEM((rows, wide), WIDE),
            pltpu.VMEM((parts, 8, slice_width), WIDE),
            pltpu.VMEM((parts, 8, slice_width), WIDE),
            pltpu.VMEM((8, slice_width), WIDE),
            pltpu.VMEM((members, 8, slice_width), WIDE),
            pltpu.SemaphoreType.DMA((5, lines)),
            pltpu.SemaphoreType.DMA((5, lines)),
            pltpu.SemaphoreType.DMA((5, lines)),
            pltpu.SemaphoreType.DMA((5, lines)),
            pltpu.SemaphoreType.DMA((6,)),
            pltpu.SemaphoreType.DMA((6,)),
            pltpu.SemaphoreType.DMA((parts,)),
            pltpu.SemaphoreType.DMA((parts,)),
            pltpu.SemaphoreType.DMA((14,)),
        ]
        + [pltpu.VMEM(value.shape, value.dtype) for value in inside[:5]],
        compiler_params=pltpu.CompilerParams(
            collective_id=2, has_side_effects=True, vmem_limit_bytes=ROOM
        ),
        cost_estimate=pl.CostEstimate(flops=10**11, bytes_accessed=10**9, transcendentals=0),
        name="retention_backward",
    )(*inside, *streamed, *weights)[:7]


def on_device(
    hidden_in,
    out_grad,
    segment_ids,
    norm1_gain,
    w_query,
    w_key,
    w_value,
    w_gate,
    w_out,
    norm2_gain,
    w_mlp_gate,
    w_mlp_up,
    w_mlp_down,
):
    _, rows, width = hidden_in.shape
    parts = lax.axis_size("dp")
    lines = parts // 2
    slice_width = width // parts
    own = lax.axis_index("tensor")
    members = lax.axis_size("tensor")
    order = list(range(0, parts, 2)) + list(range(1, parts, 2))

    def to_places(value):
        blocks = [value[:, k * slice_width : (k + 1) * slice_width] for k in order]
        return jnp.concatenate(blocks, axis=1)

    def from_places(value):
        blocks = [value[:, k * slice_width : (k + 1) * slice_width] for k in range(parts)]
        return jnp.concatenate([blocks[k // 2 + k % 2 * lines] for k in range(parts)], axis=1)

    heads_here = w_query.shape[1] // KEY
    resid_low = to_places(hidden_in.reshape(rows, width))
    grad_local = to_places(out_grad.reshape(rows, width))
    gain_rows = jnp.concatenate(
        [norm1_gain[None], norm2_gain[None], jnp.zeros((6, slice_width), LOW)]
    ).astype(WIDE)
    position = jnp.concatenate(
        [(own ^ k) * rows + jnp.arange(rows, dtype=jnp.int32) for k in range(members)]
    )
    cosine, sine = rotary_tables(position, KEY)
    head_numbers = (jnp.arange(heads_here, dtype=jnp.int32) + own * heads_here).astype(WIDE)
    rates = jnp.log1p(-jnp.exp2(-5.0 - head_numbers))
    rates = jnp.broadcast_to(rates[:, None], (heads_here, 128))
    outs = forward(
        resid_low,
        grad_local,
        gain_rows,
        cosine,
        sine,
        segment_ids,
        rates,
        [w_query, w_key, w_value, w_gate, w_out.T, w_mlp_gate, w_mlp_up, w_mlp_down.T],
        lines,
        members,
    )
    normed_turned, grad_full, gains = outs[:3]
    query_weight, key_weight, value_weight, gate_weight, out_weight = outs[3:8]
    query, keys, values, gate_pre, grad_turned = outs[11:16]
    retained, mixed, resid_mid, mid_turned, gate_hidden, up_hidden, hidden = outs[16:]
    down_grad, mlp_gate_grad, mlp_up_grad, mid_all, mid_grad, hidden_out, gain_part = feed_backward(
        grad_full,
        grad_turned,
        mid_turned,
        hidden,
        resid_mid,
        gains,
        outs[8:11],
        (gate_hidden, up_hidden),
        lines,
        members,
    )
    out_weight_grad, gate_grad, value_grad, query_grad, key_grad, in_grad, gain_total = (
        retention_backward(
            [
                mixed,
                normed_turned,
                query,
                keys,
                values,
                cosine,
                sine,
                segment_ids.T,
                segment_ids,
                rates,
                resid_low,
                gains,
                gain_part,
            ],
            [mid_grad, mid_all, retained, gate_pre],
            [out_weight, gate_weight, value_weight, query_weight, key_weight],
            lines,
            members,
            slice_width,
        )
    )
    def add_up(pieces):
        return jnp.sum(pieces.astype(WIDE), axis=0)

    return (
        from_places(hidden_out).reshape(hidden_in.shape),
        from_places(in_grad).reshape(hidden_in.shape),
        gain_total[0],
        add_up(query_grad),
        add_up(key_grad),
        add_up(value_grad),
        add_up(gate_grad),
        add_up(out_weight_grad).T,
        gain_total[1],
        add_up(mlp_gate_grad),
        add_up(mlp_up_grad),
        add_up(down_grad).T,
    )


def solution(mesh):
    return jax.shard_map(
        on_device,
        mesh=mesh,
        in_specs=(
            P("dp", "tensor", None),
            P("dp", "tensor", None),
            P("dp", None),
            P("dp"),
            P("dp", "tensor"),
            P("dp", "tensor"),
            P("dp", "tensor"),
            P("dp", "tensor"),
            P("tensor", "dp"),
            P("dp"),
            P("dp", "tensor"),
            P("dp", "tensor"),
            P("tensor", "dp"),
        ),
        out_specs=(
            P("dp", "tensor", None),
            P("dp", "tensor", None),
            P("dp"),
            P("dp", "tensor"),
            P("dp", "tensor"),
            P("dp", "tensor"),
            P("dp", "tensor"),
            P("tensor", "dp"),
            P("dp"),
            P("dp", "tensor"),
            P("dp", "tensor"),
            P("tensor", "dp"),
        ),
        check_vma=False,
    )
```

```python
import functools
import math

import jax
import jax.numpy as jnp
from jax import lax
from jax.experimental import pallas as pl
from jax.experimental.pallas import tpu as pltpu
from jax.sharding import PartitionSpec as P

KEY = 256
VAL = 432
LOW = jnp.bfloat16
WIDE = jnp.float32
WEIGHTS = 8
MESH = pl.DeviceIdType.MESH
ANY = pl.BlockSpec(memory_space=pl.ANY)
INSIDE = pl.BlockSpec(memory_space=pltpu.VMEM)
ROOM = 60 * 1024 * 1024

def rotary_tables(position, width):
    half = width // 2
    frequency = 10000.0 ** (-2.0 * jnp.arange(half, dtype=jnp.int32).astype(WIDE) / width)
    angle = position.astype(WIDE)[:, None] * frequency[None, :]
    return (jnp.cos(angle), jnp.sin(angle))


def greet(peers):
    barrier = pltpu.get_barrier_semaphore()
    for peer in peers:
        pl.semaphore_signal(barrier, inc=1, device_id=peer, device_id_type=MESH)
    pl.semaphore_wait(barrier, len(peers))


def remote(source, target, send, recv, device):
    return pltpu.make_async_remote_copy(
        src_ref=source,
        dst_ref=target,
        send_sem=send,
        recv_sem=recv,
        device_id=device,
        device_id_type=MESH,
    )


def forward_kernel(lines, members, *refs):
    hidden_ref, grad_ref, gain_ref, cos_ref, sin_ref, down_seg, along_seg, rate_ref = refs[:8]
    shards = refs[8:16]
    normed_turned, grad_all, gain_all = refs[16:19]
    wholes = refs[19:27]
    query_out, keys_out, values_out, gate_out, grad_turned = refs[27:32]
    retained_out, mixed_out, resid_out, mid_turned, gate_hidden_out, up_hidden_out = refs[32:38]
    hidden_out = refs[38]
    normed, mid, short, wide_one, wide_two, turned = refs[39:45]
    query, keys, scores, values, retained, gate, mixed, hidden = refs[45:53]
    held, got, base = refs[53:56]
    line_send, line_recv, side_send, side_recv = refs[56:60]
    near_send, near_recv, gain_send, gain_recv, home, tail_send, tail_recv, gain_rows = refs[60:]

    parts = 2 * lines
    rows, width = hidden_ref.shape
    slice_width = gain_rows.shape[1]
    heads = rate_ref.shape[0]
    value_columns = values.shape[2]
    me = lax.axis_index("dp")
    line, side = me // 2, lax.rem(me, 2)
    here = side * lines + line
    own = lax.axis_index("tensor")
    half, rest = own // 2, lax.rem(own, 2)

    def member(k):
        return 2 * lax.rem(half + k // 2, 2) + lax.rem(rest + lax.rem(k, 2), 2)

    partners = [None] + [{"tensor": member(k)} for k in range(1, members)]
    others = [{"dp": lax.rem(me + k, parts)} for k in range(1, parts)]
    opposite = {"dp": 2 * line + (1 - side)}
    greet(others + partners[1:])

    local = {}
    slots = iter(range(32))

    def keep(source, target):
        slot = next(slots)
        local[slot] = pltpu.make_async_copy(source, target, home.at[slot])
        local[slot].start()
        return slot

    def finish(slot):
        local.pop(slot).wait()

    near = {}

    def near_start(tag, source, target, k):
        copy = remote(source, target, near_send.at[tag], near_recv.at[tag], partners[k])
        copy.start()
        near[tag] = copy

    across = {}
    ours = {}

    inner = lines == 4

    def line_copy(w, step):
        return remote(
            shards[w],
            wholes[w].at[here],
            line_send.at[w, step],
            line_recv.at[w, step],
            {"dp": 2 * lax.rem(line + step, lines) + side},
        )

    def relay_copy(w):
        place = side * lines + 3 * (2 - line)
        return remote(
            wholes[w].at[place],
            wholes[w].at[place],
            line_send.at[w, 0],
            line_recv.at[w, 2 * line - 1],
            {"dp": 6 * (line - 1) + side},
        )

    tail = slice_width // 8 // 16 * 16
    most = slice_width - tail

    def side_copy(w, step):
        place = side * lines + lax.rem(line + lines - step, lines)
        return remote(
            wholes[w].at[place, pl.ds(0, most)],
            wholes[w].at[place, pl.ds(0, most)],
            side_send.at[w, step],
            side_recv.at[w, step],
            opposite,
        )

    there = (1 - side) * lines + line

    def tail_copy(w, step):
        return remote(
            wholes[w].at[there, pl.ds(most, tail)],
            wholes[w].at[there, pl.ds(most, tail)],
            tail_send.at[w, step],
            tail_recv.at[w, step],
            {"dp": 2 * lax.rem(line + step, lines) + side},
        )

    def on_line(w, step, act):
        if inner and step != 2:

            @pl.when(line != (3 if step == 1 else 0))
            def _():
                act(line_copy(w, step))
        else:
            act(line_copy(w, step))

    sends = [2, 1, 3] if inner else list(range(1, lines))

    def start_lines(w):
        for step in sends:
            on_line(w, step, lambda copy: copy.start())
        across[w, 0] = remote(
            shards[w], wholes[w].at[here], side_send.at[w, 0], side_recv.at[w, 0], opposite
        )
        across[w, 0].start()
        ours[w] = keep(shards[w], wholes[w].at[here])

    def pass_on(w, third):
        for at in range(third * (lines - 1) // 3, (third + 1) * (lines - 1) // 3):
            step = at + 1
            if inner:
                late = 3 - 2 * ((3 - line) // 3)
                step = [2, 4 - late, late][at]
            if tail and at == 0:
                across[w, 0].wait_recv()
                for hop in range(1, lines):
                    tail_copy(w, hop).start()
            line_copy(w, step).wait_recv()
            if inner and at == 0:

                @pl.when((line == 1) | (line == 2))
                def _():
                    relay_copy(w).start()

            side_copy(w, step).start()

    def complete(w):
        if not tail:
            across[w, 0].wait_recv()
        for step in range(1, lines):
            side_copy(w, step).wait_recv()
            if tail:
                tail_copy(w, step).wait_recv()
        finish(ours[w])

    def load(w, target, sem):
        copy = pltpu.make_async_copy(wholes[w], target, sem)
        copy.start()
        copy.wait()

    def stage(w, target, body):
        if w + 1 < WEIGHTS:
            for third in range(3):
                pass_on(w + 1, third)
        if w + 3 < WEIGHTS:
            start_lines(w + 3)
        complete(w)
        load(w, target, home.at[home.shape[0] - 1 - w])
        lax.fori_loop(0, members, body, 0)

    gain_rows[...] = jnp.where(
        lax.broadcasted_iota(jnp.int32, gain_rows.shape, 0) == 0,
        gain_ref[0:1, :].astype(WIDE),
        gain_ref[1:2, :].astype(WIDE),
    )
    gains = []
    for k in range(1, parts):
        copy = remote(
            gain_rows, gain_all.at[here], gain_send.at[k], gain_recv.at[k], others[k - 1]
        )
        copy.start()
        gains.append(copy)
    gain_all[here] = gain_rows[...]
    for w in range(3):
        start_lines(w)

    def scale_into(target, scaled, which):
        for p in range(parts):
            columns = slice(p * slice_width, (p + 1) * slice_width)
            target[0, :, columns] = (
                scaled[:, columns] * gain_all[p][which : which + 1]
            ).astype(LOW)

    resid = hidden_ref[...].astype(WIDE)
    scaled = resid * lax.rsqrt(jnp.mean(resid * resid, axis=-1, keepdims=True) + 1e-06)
    for copy in gains:
        copy.wait_recv()
    scale_into(normed, scaled, 0)
    for k in range(1, members):
        near_start(k - 1, normed.at[0], normed.at[k], k)
    for k in range(1, members):
        near_start(2 + k, grad_ref, mid.at[k], k)
    grad_kept = keep(grad_ref, mid.at[0])
    for third in range(3):
        pass_on(0, third)
    for k in range(1, members):
        near[k - 1].wait_recv()

    def turn_over(source):
        tile = 256

        def body(k, carry):
            at = pl.ds(pl.multiple_of(k * rows, rows), rows)
            for c in range(width // tile):
                columns = slice(c * tile, (c + 1) * tile)
                turned[columns, at] = source[k, :, columns].T
            return carry

        lax.fori_loop(0, members, body, 0)

    turn_over(normed)
    turned_kept = keep(turned, normed_turned)

    def flat(ref):
        return ref[...].reshape(width, ref.shape[2])

    def turn(source, target, scale):
        def body(k, carry):
            pre = jnp.dot(normed[k], flat(source), preferred_element_type=WIDE)
            at = pl.ds(pl.multiple_of(k * rows, rows), rows)
            cosine, sine = cos_ref[at, :], sin_ref[at, :]
            wing = KEY // 2
            for h in range(heads):
                first = pre[:, h * KEY : h * KEY + wing]
                second = pre[:, h * KEY + wing : (h + 1) * KEY]
                target[k, :, h * KEY : h * KEY + wing] = (
                    (first * cosine - second * sine) * scale
                ).astype(LOW)
                target[k, :, h * KEY + wing : (h + 1) * KEY] = (
                    (second * cosine + first * sine) * scale
                ).astype(LOW)
            return carry

        return body

    stage(0, short, turn(short, query, KEY ** (-0.5)))
    keep(query, query_out)
    stage(1, short, turn(short, keys, 1.0))
    keep(keys, keys_out)

    def score(k, carry):
        place = member(k)
        at = pl.multiple_of(place * rows, rows)
        segment = down_seg[pl.ds(at, rows), :]
        for h in range(heads):
            head = slice(h * KEY, (h + 1) * KEY)
            for m in range(members):
                start = pl.multiple_of(member(m) * rows, rows)
                raw = lax.dot_general(
                    query[k, :, head],
                    keys[m, :, head],
                    (((1,), (1,)), ((), ())),
                    preferred_element_type=WIDE,
                )
                distance = (
                    lax.broadcasted_iota(jnp.int32, (rows, rows), 0)
                    - lax.broadcasted_iota(jnp.int32, (rows, rows), 1)
                    + (at - start)
                )
                same = (distance >= 0) & (segment == along_seg[:, pl.ds(start, rows)])
                decay = jnp.exp(
                    rate_ref[h : h + 1, :1] * jnp.maximum(distance, 0).astype(WIDE)
                )
                scores[h, k, :, m * rows : (m + 1) * rows] = (
                    raw * jnp.where(same, decay, 0.0)
                ).astype(LOW)
        return carry

    lax.fori_loop(0, members, score, 0)
    finish(grad_kept)
    for k in range(1, members):
        near[2 + k].wait_recv()
    finish(turned_kept)
    turn_over(mid)
    turned_kept = keep(turned, grad_turned)
    grad_kept = keep(mid, grad_all)

    column = lax.broadcasted_iota(jnp.int32, (rows, value_columns), 1)

    def by_head(parts_of):
        result = parts_of[0]
        for h in range(1, heads):
            result = jnp.where(column < h * VAL, result, parts_of[h])
        return result

    def head_mean(value):
        means = []
        for h in range(heads):
            inside = (column >= h * VAL) & (column < (h + 1) * VAL)
            total = jnp.sum(jnp.where(inside, value, 0.0), axis=-1, keepdims=True)
            means.append(total * (1.0 / VAL))
        return by_head(means)

    def make_values(k, carry):
        values[k] = jnp.dot(normed[k], flat(wide_one), preferred_element_type=WIDE).astype(LOW)
        return carry

    stage(2, wide_one, make_values)
    keep(values, values_out)

    def retain(k, carry):
        every = values[...].reshape(members * rows, value_columns)
        retained[k] = by_head(
            [
                jnp.dot(scores[h, k], every, preferred_element_type=WIDE)
                for h in range(heads)
            ]
        )
        return carry

    lax.fori_loop(0, members, retain, 0)
    retained_kept = keep(retained, retained_out)

    def make_mixed(k, carry):
        pre = jnp.dot(normed[k], flat(wide_two), preferred_element_type=WIDE)
        gate[k] = pre
        value = retained[k]
        centred = value - head_mean(value)
        grouped = centred * lax.rsqrt(head_mean(centred * centred) + 1.0)
        mixed[k] = (grouped * (pre / (1.0 + jnp.exp(-pre)))).astype(LOW)
        return carry

    stage(3, wide_two, make_mixed)
    gate_kept = keep(gate, gate_out)
    keep(mixed, mixed_out)

    def project(k, put):
        for p in range(parts):
            columns = slice(p * slice_width, (p + 1) * slice_width)
            put(
                columns,
                lax.dot_general(
                    mixed[k],
                    wide_one[p],
                    (((1,), (1,)), ((), ())),
                    preferred_element_type=WIDE,
                ),
            )

    def put_low(slot):
        def put(columns, value):
            held[slot, :, columns] = value.astype(LOW)

        return put

    def put_sum(columns, value):
        base[:, columns] = value

    pass_on(5, 0)
    complete(4)
    load(4, wide_one, home.at[home.shape[0] - 5])
    finish(grad_kept)
    project(3, put_low(0))
    near_start(6, held.at[0], got.at[0], 1)
    project(2, put_sum)
    pass_on(5, 1)
    near[6].wait_recv()
    held[1] = (base[...] + got[0].astype(WIDE)).astype(LOW)
    near_start(8, held.at[1], got.at[1], 2)
    project(1, put_low(2))
    near_start(7, held.at[2], got.at[2], 1)
    project(0, put_sum)
    pass_on(5, 2)
    start_lines(7)
    near[7].wait_recv()
    base[...] = base[...] + got[2].astype(WIDE) + hidden_ref[...].astype(WIDE)
    pass_on(6, 0)
    near[8].wait_recv()
    resid = base[...] + got[1].astype(WIDE)
    resid_out[...] = resid
    scaled = resid * lax.rsqrt(jnp.mean(resid * resid, axis=-1, keepdims=True) + 1e-06)
    scale_into(mid, scaled, 1)
    near_start(10, mid.at[0], mid.at[2], 2)
    near_start(9, mid.at[0], mid.at[1], 1)
    pass_on(6, 1)
    pass_on(6, 2)
    near[10].wait_recv()
    near_start(11, mid.at[2], mid.at[3], 1)
    complete(5)
    load(5, wide_two, home.at[home.shape[0] - 6])
    near[9].wait_recv()
    near[11].wait_recv()
    finish(retained_kept)
    finish(gate_kept)

    def make_gate(k, carry):
        gate[k] = jnp.dot(mid[k], flat(wide_two), preferred_element_type=WIDE)
        return carry

    lax.fori_loop(0, members, make_gate, 0)
    keep(gate, gate_hidden_out)
    finish(turned_kept)
    turn_over(mid)
    keep(turned, mid_turned)
    pass_on(7, 0)
    pass_on(7, 1)
    pass_on(7, 2)
    complete(6)
    load(6, wide_one, home.at[home.shape[0] - 7])

    def make_hidden(k, carry):
        up = jnp.dot(mid[k], flat(wide_one), preferred_element_type=WIDE)
        retained[k] = up
        pre = gate[k]
        inner = (2.0 / math.pi) ** 0.5 * (pre + 0.044715 * (pre * pre * pre))
        hidden[k] = (0.5 * pre * (1.0 + jnp.tanh(inner)) * up).astype(LOW)
        return carry

    lax.fori_loop(0, members, make_hidden, 0)
    keep(retained, up_hidden_out)
    keep(hidden, hidden_out)
    complete(7)
    for w in range(WEIGHTS):
        for step in sends:
            on_line(w, step, lambda copy: copy.wait_send())
            side_copy(w, step).wait_send()
            if tail:
                tail_copy(w, step).wait_send()
        across[w, 0].wait_send()
        if inner:

            @pl.when((line == 1) | (line == 2))
            def _():
                relay_copy(w).wait_send()

    for copy in gains:
        copy.wait_send()
    for copy in near.values():
        copy.wait_send()
    for slot in list(local):
        finish(slot)


def forward(hidden, grad, gains, cosine, sine, segments, rates, shards, lines, members):
    parts = 2 * lines
    rows, width = hidden.shape
    heads = rates.shape[0]
    key_columns, value_columns = shards[0].shape[1], shards[2].shape[1]
    length = rows * members
    blocks = (members, rows)
    turned = (width, length)
    outs = [
        (turned, LOW),
        (blocks + (width,), LOW),
        ((parts, 8, gains.shape[1]), WIDE),
    ]
    outs += [((parts,) + shard.shape, LOW) for shard in shards]
    outs += [
        (blocks + (key_columns,), LOW),
        (blocks + (key_columns,), LOW),
        (blocks + (value_columns,), LOW),
        (blocks + (value_columns,), WIDE),
        (turned, LOW),
        (blocks + (value_columns,), WIDE),
        (blocks + (value_columns,), LOW),
        ((rows, width), WIDE),
        (turned, LOW),
        (blocks + (value_columns,), WIDE),
        (blocks + (value_columns,), WIDE),
        (blocks + (value_columns,), LOW),
    ]
    places = [ANY] * len(outs)
    places[2] = INSIDE
    places[18] = INSIDE
    tags = 12
    return pl.pallas_call(
        functools.partial(forward_kernel, lines, members),
        out_shape=[jax.ShapeDtypeStruct(shape, dtype) for shape, dtype in outs],
        in_specs=[INSIDE, ANY] + [INSIDE] * 6 + [ANY] * WEIGHTS,
        out_specs=places,
        scratch_shapes=[
            pltpu.VMEM(blocks + (width,), LOW),
            pltpu.VMEM(blocks + (width,), LOW),
            pltpu.VMEM((parts,) + shards[0].shape, LOW),
            pltpu.VMEM((parts,) + shards[2].shape, LOW),
            pltpu.VMEM((parts,) + shards[2].shape, LOW),
            pltpu.VMEM(turned, LOW),
            pltpu.VMEM(blocks + (key_columns,), LOW),
            pltpu.VMEM(blocks + (key_columns,), LOW),
            pltpu.VMEM((heads, members, rows, length), LOW),
            pltpu.VMEM(blocks + (value_columns,), LOW),
            pltpu.VMEM(blocks + (value_columns,), WIDE),
            pltpu.VMEM(blocks + (value_columns,), WIDE),
            pltpu.VMEM(blocks + (value_columns,), LOW),
            pltpu.VMEM(blocks + (value_columns,), LOW),
            pltpu.VMEM((3, rows, width), LOW),
            pltpu.VMEM((3, rows, width), LOW),
            pltpu.VMEM((rows, width), WIDE),
            pltpu.SemaphoreType.DMA((WEIGHTS, lines)),
            pltpu.SemaphoreType.DMA((WEIGHTS, lines)),
            pltpu.SemaphoreType.DMA((WEIGHTS, lines)),
            pltpu.SemaphoreType.DMA((WEIGHTS, lines)),
            pltpu.SemaphoreType.DMA((tags,)),
            pltpu.SemaphoreType.DMA((tags,)),
            pltpu.SemaphoreType.DMA((parts,)),
            pltpu.SemaphoreType.DMA((parts,)),
            pltpu.SemaphoreType.DMA((40,)),
            pltpu.SemaphoreType.DMA((WEIGHTS, lines)),
            pltpu.SemaphoreType.DMA((WEIGHTS, lines)),
            pltpu.VMEM((8, gains.shape[1]), WIDE),
        ],
        compiler_params=pltpu.CompilerParams(
            collective_id=0, has_side_effects=True, vmem_limit_bytes=ROOM
        ),
        cost_estimate=pl.CostEstimate(
            flops=10**11, bytes_accessed=10**9, transcendentals=0
        ),
        name="forward",
    )(hidden, grad, gains, cosine, sine, segments.T, segments, rates, *shards)


def tail_rows(rows, lines):
    return rows // 8 // 16 * 16 if lines == 4 else 0


class Scatter:
    def __init__(self, lines, held, far_got, near_got, tail_got, spare, tails, sems):
        self.lines = lines
        self.held, self.far_got, self.near_got, self.spare = held, far_got, near_got, spare
        self.tail_got, self.tails = tail_got, tails
        self.side_send, self.side_recv, self.line_send, self.line_recv = sems[:4]
        self.tail_send, self.tail_recv, self.home = sems[4:]
        self.rows = held[0].shape[1]
        self.tail = tail_rows(self.rows, lines)
        self.most = self.rows - self.tail
        me = lax.axis_index("dp")
        self.line, self.side = me // 2, lax.rem(me, 2)
        self.opposite = {"dp": 2 * self.line + (1 - self.side)}

    def peer(self, step):
        return {"dp": 2 * lax.rem(self.line + step, self.lines) + self.side}

    def peers(self):
        return [self.opposite] + [self.peer(step) for step in range(1, self.lines)]

    def far_copy(self, w, place):
        return remote(
            self.held[w].at[place, pl.ds(0, self.most)],
            self.far_got[w].at[place, pl.ds(0, self.most)],
            self.side_send.at[w, place],
            self.side_recv.at[w, place],
            self.opposite,
        )

    def near_copy(self, w, step):
        place = lax.rem(self.line + step, self.lines)
        return remote(
            self.held[w].at[place],
            self.near_got[w].at[step],
            self.line_send.at[w, step],
            self.line_recv.at[w, step],
            self.peer(step),
        )

    def fetch(self, source):
        rows, columns = source.shape
        spare = self.spare[columns].at[pl.ds(0, rows)]
        copy = pltpu.make_async_copy(source, spare, self.home)
        copy.start()
        copy.wait()
        return spare[...].astype(WIDE)


    def tail_copy(self, w, step):
        place = lax.rem(self.line + step, self.lines)
        return remote(
            self.held[w].at[place, pl.ds(self.most, self.tail)],
            self.tail_got[w].at[step],
            self.tail_send.at[w, step],
            self.tail_recv.at[w, step],
            self.peer(step),
        )

    def tail_across(self, w):
        return remote(
            self.tails[w],
            self.tail_got[w].at[0],
            self.tail_send.at[w, 0],
            self.tail_recv.at[w, 0],
            self.opposite,
        )

    def add_tails(self, w):
        total = self.held[w][self.line, self.most :].astype(WIDE)
        for step in range(1, self.lines):
            self.tail_copy(w, step).wait_recv()
            total = total + self.fetch(self.tail_got[w].at[step])
        self.tails[w][...] = total.astype(LOW)
        self.tail_across(w).start()

    def product(self, left, right, place):
        rows = self.held[0].shape[1]
        block = left[pl.ds(pl.multiple_of(place * rows, rows), rows), :]
        every = right[...]
        return jnp.dot(
            block,
            every.reshape(every.shape[0] * every.shape[1], every.shape[2]),
            preferred_element_type=WIDE,
        )


    def extra_copy(self, w, step):
        place = lax.rem(self.line + step, self.lines)
        return remote(
            self.held[w].at[place],
            self.far_got[w].at[self.lines],
            self.line_send.at[w, step],
            self.line_recv.at[w, 0],
            {"dp": 2 * (2 if step == 1 else 1) + self.side},
        )

    def far(self, w, left, right):
        def body(at, carry):
            step = 1 + at
            if self.lines == 4:
                step = 1 + 2 * at - 3 * (at // 2)
            place = lax.rem(self.line + step, self.lines)
            other = (1 - self.side) * self.lines + place
            self.held[w][place] = self.product(left, right, other).astype(LOW)
            self.far_copy(w, place).start()
            if self.tail:

                @pl.when(at < self.lines - 1)
                def _():
                    self.tail_copy(w, step).start()

            return carry

        lax.fori_loop(0, self.lines, body, 0)

    def near(self, w, left, right, quarter):
        def put(place, step):
            part = self.product(left, right, self.side * self.lines + place)
            self.far_copy(w, place).wait_recv()
            got = self.fetch(self.far_got[w].at[place, pl.ds(0, self.most)])
            self.far_copy(w, place).wait_send()
            if self.tail and step is not None:
                self.tail_copy(w, step).wait_send()
            self.held[w][place, : self.most] = (part[: self.most] + got).astype(LOW)
            if self.tail:
                self.held[w][place, self.most :] = part[self.most :].astype(LOW)

        def body(step, carry):
            place = lax.rem(self.line + step, self.lines)
            put(place, step)
            self.near_copy(w, step).start()
            return carry

        if self.lines != 4:
            first, last = [1 + (quarter + k) * self.lines // 4 for k in range(2)]
            lax.fori_loop(first, min(last, self.lines), body, 0)
        elif quarter < 2:
            step = 1 + 2 * quarter
            end = 3 - 3 * quarter
            place = lax.rem(self.line + step, self.lines)
            put(place, step)

            @pl.when(self.line == end)
            def _():
                self.extra_copy(w, step).start()

            @pl.when(self.line != end)
            def _():
                self.near_copy(w, step).start()
        elif quarter == 2:
            place = lax.rem(self.line + 2, self.lines)
            put(place, 2)

            @pl.when((self.line == 1) | (self.line == 2))
            def _():
                self.extra_copy(w, 1).wait_recv()
                self.held[w][place] = (
                    self.held[w][place].astype(WIDE)
                    + self.fetch(self.far_got[w].at[self.lines])
                ).astype(LOW)

            self.near_copy(w, 2).start()
        if quarter < 3:
            return
        if self.tail:
            self.add_tails(w)
        put(self.line, None)
        if not self.tail:
            self.own_copy(w).start()
        if self.lines == 4:

            @pl.when((self.line == 0) | (self.line == 3))
            def _():
                spare = self.spare[self.held[w].shape[2]]
                spare[...] = jnp.zeros(spare.shape, LOW)
                slot = 1 + 2 * (self.line // 3)
                copy = pltpu.make_async_copy(spare, self.near_got[w].at[slot], self.home)
                copy.start()
                copy.wait()

    def own_copy(self, w):
        return pltpu.make_async_copy(
            self.held[w].at[self.line], self.near_got[w].at[0], self.line_send.at[w, 0]
        )

    def finish(self, w):
        if self.lines != 4:

            def body(step, carry):
                self.near_copy(w, step).wait()
                return carry

            lax.fori_loop(1, self.lines, body, 0)
        else:
            for step in range(1, 4):
                copy = self.near_copy(w, step)
                copy.wait_send()
                if step == 2:
                    copy.wait_recv()
                else:

                    @pl.when(self.line != (0 if step == 1 else 3))
                    def _():
                        copy.wait_recv()

        if self.tail:
            self.tail_across(w).wait()
            self.held[w][self.line, self.most :] = (
                self.held[w][self.line, self.most :].astype(WIDE)
                + self.fetch(self.tail_got[w].at[0])
            ).astype(LOW)
            self.own_copy(w).start()
        self.own_copy(w).wait()


class Near:
    def __init__(self, send, recv):
        self.send, self.recv = send, recv
        self.flight = {}
        own = lax.axis_index("tensor")
        half, rest = own // 2, lax.rem(own, 2)
        self.member = lambda k: 2 * lax.rem(half + k // 2, 2) + lax.rem(rest + lax.rem(k, 2), 2)

    def partners(self, members):
        return [{"tensor": self.member(k)} for k in range(1, members)]

    def start(self, tag, source, target, k):
        copy = remote(source, target, self.send.at[tag], self.recv.at[tag], self.partners(4)[k - 1])
        copy.start()
        self.flight[tag] = copy

    def wait(self, tag):
        self.flight[tag].wait_recv()

    def sent(self, tag):
        self.flight[tag].wait_send()


def dot_across(left, right):
    return lax.dot_general(
        left, right, (((1,), (1,)), ((), ())), preferred_element_type=WIDE
    )


def feed_kernel(lines, members, *refs):
    grad_turned, hidden, gain_all = refs[:3]
    later = refs[3:9]
    gate_hidden, up_hidden = refs[9:11]
    near_got, mid_all, mid_grad_out, hidden_out, gain_out = refs[11:14], *refs[14:18]
    far_got, tail_got = refs[18:21], refs[21:24]
    gate_low, up_low, pre, up = refs[24:28]
    scatter_held = refs[28:31]
    spare, held, got, last, base, mid = refs[31:37]
    sems = refs[37:43]
    near_send, near_recv, home = refs[43:46]
    loaded, tails = refs[46:52], refs[52:]
    grad_ref, mid_turned, resid_ref, gate_weight, up_weight, down_weight = loaded
    parts = 2 * lines
    rows, width = resid_ref.shape
    loads = []
    for k, order in enumerate((5, 0, 1, 3, 4, 2)):
        loads.append(pltpu.make_async_copy(later[order], loaded[order], home.at[4 + k]))
        loads[k].start()
    slice_width = width // parts
    scatter = Scatter(
        lines,
        scatter_held,
        far_got,
        near_got,
        tail_got,
        {spare.shape[1]: spare},
        tails,
        sems + (home.at[0],),
    )
    near = Near(near_send, near_recv)
    greet(scatter.peers() + near.partners(members))
    scatter.far(0, grad_turned, hidden)

    def flat(ref):
        return ref[...].reshape(width, ref.shape[2])

    def pull(k, carry):
        first = pltpu.make_async_copy(gate_hidden.at[k], pre, home.at[1])
        second = pltpu.make_async_copy(up_hidden.at[k], up, home.at[2])
        first.start()
        second.start()
        grad = jnp.dot(grad_ref[k], flat(down_weight), preferred_element_type=WIDE)
        first.wait()
        second.wait()
        value = pre[...]
        root = (2.0 / math.pi) ** 0.5
        square = value * value
        lift = jnp.tanh(root * (value + 0.044715 * (value * square)))
        ramp = 0.5 * (1.0 + lift)
        slope = ramp + 0.5 * value * (1.0 - lift * lift) * root * (1.0 + 0.134145 * square)
        gate_low[k] = (grad * up[...] * slope).astype(LOW)
        up_low[k] = (grad * (value * ramp)).astype(LOW)
        return carry

    for load in loads:
        load.wait()
    lax.fori_loop(0, members // 2, pull, 0)
    scatter.near(0, grad_turned, hidden, 0)
    lax.fori_loop(members // 2, members, pull, 0)
    scatter.near(0, grad_turned, hidden, 1)
    scatter.far(1, mid_turned, gate_low)

    def back(k, put):
        for p in range(parts):
            columns = slice(p * slice_width, (p + 1) * slice_width)
            put(
                columns,
                dot_across(gate_low[k], gate_weight[p]) + dot_across(up_low[k], up_weight[p]),
            )

    def put_low(slot):
        def put(columns, value):
            held[slot, :, columns] = value.astype(LOW)

        return put

    def put_sum(columns, value):
        base[:, columns] = value

    back(3, put_low(0))
    near.start(0, held.at[0], got.at[0], 1)
    scatter.near(0, grad_turned, hidden, 2)
    back(2, put_sum)
    near.wait(0)
    near.sent(0)
    held[0] = (base[...] + got[0].astype(WIDE)).astype(LOW)
    near.start(1, held.at[0], got.at[1], 2)
    back(1, put_low(1))
    near.start(2, held.at[1], got.at[2], 1)
    scatter.near(0, grad_turned, hidden, 3)
    back(0, put_sum)
    scatter.far(2, mid_turned, up_low)
    scatter.near(1, mid_turned, gate_low, 0)
    near.wait(2)
    base[...] += got[2].astype(WIDE)
    scatter.near(1, mid_turned, gate_low, 1)
    near.wait(1)
    normed_grad = base[...] + got[1].astype(WIDE)
    resid = resid_ref[...]
    scale = lax.rsqrt(jnp.mean(resid * resid, axis=-1, keepdims=True) + 1e-06)
    unit = resid * scale
    base[...] = normed_grad * unit
    gain_out[...] = jnp.broadcast_to(
        jnp.sum(base[...], axis=0, keepdims=True), gain_out.shape
    )
    dot = jnp.zeros((rows, 1), WIDE)
    for p in range(parts):
        columns = slice(p * slice_width, (p + 1) * slice_width)
        dot += jnp.sum(base[:, columns] * gain_all[p][1:2], axis=-1, keepdims=True)
    dot = dot * (1.0 / width)
    base[...] = normed_grad
    for p in range(parts):
        columns = slice(p * slice_width, (p + 1) * slice_width)
        block = resid_ref[:, columns] * scale
        mid_grad = grad_ref[0, :, columns].astype(WIDE) + scale * (
            base[:, columns] * gain_all[p][1:2] - block * dot
        )
        base[:, columns] = mid_grad
        mid[:, columns] = mid_grad.astype(LOW)
    mid_grad_copy = pltpu.make_async_copy(base, mid_grad_out, home.at[1])
    mid_grad_copy.start()
    near.start(3, mid, mid_all.at[2], 2)
    near.start(4, mid, mid_all.at[1], 1)
    own = pltpu.make_async_copy(mid, mid_all.at[0], home.at[3])
    own.start()
    scatter.near(1, mid_turned, gate_low, 2)
    scatter.near(1, mid_turned, gate_low, 3)

    def down(k, put):
        for p in range(parts):
            columns = slice(p * slice_width, (p + 1) * slice_width)
            put(columns, dot_across(hidden[k], down_weight[p]))

    near.sent(1)
    near.sent(2)
    down(3, put_low(0))
    mid_grad_copy.wait()
    near.start(6, held.at[0], last.at[0], 1)
    down(2, put_sum)
    scatter.near(2, mid_turned, up_low, 0)
    near.wait(3)
    near.start(5, mid_all.at[2], mid_all.at[3], 1)
    near.wait(6)
    near.sent(6)
    held[0] = (base[...] + last[0].astype(WIDE)).astype(LOW)
    near.start(7, held.at[0], last.at[1], 2)
    down(1, put_low(1))
    near.start(8, held.at[1], last.at[2], 1)
    scatter.near(2, mid_turned, up_low, 1)
    down(0, put_sum)
    scatter.near(2, mid_turned, up_low, 2)
    scatter.near(2, mid_turned, up_low, 3)
    near.wait(8)
    near.wait(7)
    own.wait()
    near.sent(3)
    near.sent(4)
    for p in range(parts):
        columns = slice(p * slice_width, (p + 1) * slice_width)
        value = base[:, columns] + last[2, :, columns].astype(WIDE)
        value = value + last[1, :, columns].astype(WIDE) + resid_ref[:, columns]
        start = (2 * (p % lines) + p // lines) * slice_width
        mid[:, start : start + slice_width] = value.astype(LOW)
    own = pltpu.make_async_copy(mid, hidden_out, home.at[3])
    own.start()
    for w in range(3):
        scatter.finish(w)
    near.wait(4)
    near.wait(5)
    own.wait()
    for tag in (5, 7, 8):
        near.sent(tag)


def feed_backward(
    grad, grad_turned, mid_turned, hidden, resid, gains, weights, pres, lines, members
):
    parts = 2 * lines
    rows, width = resid.shape
    columns = hidden.shape[2]
    slice_width = width // parts
    blocks = (members, rows)
    piece = (lines, slice_width, columns)
    later = [grad, mid_turned, resid, *weights]
    outs = [(piece, LOW)] * 3
    outs += [
        (blocks + (width,), LOW),
        ((rows, width), WIDE),
        ((rows, width), LOW),
        ((8, width), WIDE),
    ]
    outs += [((lines + 1,) + piece[1:], LOW)] * 3
    tail = max(tail_rows(slice_width, lines), 16)
    outs += [((lines, tail, columns), LOW)] * 3
    return pl.pallas_call(
        functools.partial(feed_kernel, lines, members),
        out_shape=[jax.ShapeDtypeStruct(shape, dtype) for shape, dtype in outs],
        in_specs=[INSIDE] * 3 + [ANY] * 8,
        out_specs=[ANY] * 6 + [INSIDE] + [ANY] * 6,
        scratch_shapes=[
            pltpu.VMEM(blocks + (columns,), LOW),
            pltpu.VMEM(blocks + (columns,), LOW),
            pltpu.VMEM((rows, columns), WIDE),
            pltpu.VMEM((rows, columns), WIDE),
            pltpu.VMEM(piece, LOW),
            pltpu.VMEM(piece, LOW),
            pltpu.VMEM(piece, LOW),
            pltpu.VMEM(piece[1:], LOW),
            pltpu.VMEM((2, rows, width), LOW),
            pltpu.VMEM((3, rows, width), LOW),
            pltpu.VMEM((3, rows, width), LOW),
            pltpu.VMEM((rows, width), WIDE),
            pltpu.VMEM((rows, width), LOW),
            pltpu.SemaphoreType.DMA((3, lines)),
            pltpu.SemaphoreType.DMA((3, lines)),
            pltpu.SemaphoreType.DMA((3, lines)),
            pltpu.SemaphoreType.DMA((3, lines)),
            pltpu.SemaphoreType.DMA((3, lines)),
            pltpu.SemaphoreType.DMA((3, lines)),
            pltpu.SemaphoreType.DMA((9,)),
            pltpu.SemaphoreType.DMA((9,)),
            pltpu.SemaphoreType.DMA((10,)),
        ]
        + [pltpu.VMEM(value.shape, value.dtype) for value in later]
        + [pltpu.VMEM((tail, columns), LOW)] * 3,
        compiler_params=pltpu.CompilerParams(
            collective_id=1, has_side_effects=True, vmem_limit_bytes=ROOM
        ),
        cost_estimate=pl.CostEstimate(flops=10**11, bytes_accessed=10**9, transcendentals=0),
        name="feed_backward",
    )(grad_turned, hidden, gains, *later, *pres)[:7]


def retention_kernel(lines, members, *refs):
    later = refs[:5]
    cos_ref, sin_ref, down_seg, along_seg, rate_ref = refs[5:10]
    hidden_ref, gain_all, gain_part = refs[10:13]
    mid_grad_ref, mid_all, retained_all, gate_all = refs[13:17]
    weights = refs[17:22]
    near_got, in_grad_out, gain_out = refs[22:27], refs[27], refs[28]
    far_got, tail_got = refs[29:34], refs[34:39]
    turned, wide_one, wide_two, short_one, short_two = refs[39:44]
    gate_low, retained_low, query_low, key_low = refs[44:48]
    scatter_held = refs[48:53]
    spare_wide, spare_short, held, got, base, retained, gate = refs[53:60]
    pieces, piece_got, total, total_got = refs[60:64]
    sems = refs[64:70]
    near_send, near_recv, gain_send, gain_recv, home = refs[70:75]
    loaded, tails = refs[75:80], refs[80:]
    mixed, normed_turned, query, keys, values = loaded
    value_low = mixed
    parts = 2 * lines
    rows, width = hidden_ref.shape
    slice_width = width // parts
    heads = rate_ref.shape[0]
    value_columns = values.shape[2]
    length = rows * members
    scatter = Scatter(
        lines,
        scatter_held,
        far_got,
        near_got,
        tail_got,
        {spare_wide.shape[1]: spare_wide, spare_short.shape[1]: spare_short},
        tails,
        sems + (home.at[0],),
    )
    near = Near(near_send, near_recv)
    me = lax.axis_index("dp")
    here = scatter.side * lines + scatter.line
    others = [{"dp": lax.rem(me + k, parts)} for k in range(1, parts)]
    greet(others + near.partners(members))

    def fetch(source, target, sem):
        copy = pltpu.make_async_copy(source, target, home.at[sem])
        copy.start()
        return copy

    out_copy = fetch(weights[0], wide_one, 1)
    value_copy = fetch(weights[2], wide_two, 2)
    query_copy = fetch(weights[3], short_one, 3)
    key_copy = fetch(weights[4], short_two, 4)
    grad_copy = fetch(mid_grad_ref, in_grad_out, 7)
    loads = [fetch(later[k], loaded[k], 9 + k) for k in range(5)]

    def turn_over(k, carry):
        fetch(mid_all.at[k], held.at[0], 8).wait()
        at = pl.ds(pl.multiple_of(k * rows, rows), rows)
        for c in range(width // 256):
            columns = slice(c * 256, (c + 1) * 256)
            turned[columns, at] = held[0, :, columns].T
        return carry

    lax.fori_loop(0, members, turn_over, 0)
    loads[0].wait()
    scatter.far(0, turned, mixed)
    out_copy.wait()
    for load in loads[1:]:
        load.wait()

    column = lax.broadcasted_iota(jnp.int32, (rows, value_columns), 1)

    def by_head(parts_of):
        result = parts_of[0]
        for h in range(1, heads):
            result = jnp.where(column < h * VAL, result, parts_of[h])
        return result

    def inside(h):
        return (column >= h * VAL) & (column < (h + 1) * VAL)

    def head_mean(value):
        return by_head(
            [
                jnp.sum(jnp.where(inside(h), value, 0.0), axis=-1, keepdims=True) * (1.0 / VAL)
                for h in range(heads)
            ]
        )

    def unmix(k, carry):
        first = fetch(retained_all.at[k], retained, 5)
        second = fetch(gate_all.at[k], gate, 6)
        fetch(mid_all.at[k], held.at[0], 8).wait()
        grad = jnp.dot(
            held[0],
            wide_one[...].reshape(width, value_columns),
            preferred_element_type=WIDE,
        )
        first.wait()
        second.wait()
        value = retained[...]
        centred = value - head_mean(value)
        rate = lax.rsqrt(head_mean(centred * centred) + 1.0)
        pre = gate[...]
        sigma = 1.0 / (1.0 + jnp.exp(-pre))
        gate_low[k] = (
            grad * (centred * rate) * (sigma * (1.0 + pre * (1.0 - sigma)))
        ).astype(LOW)
        grouped_grad = grad * (pre * sigma)
        retained_low[k] = (
            rate * (grouped_grad - head_mean(grouped_grad))
            - (rate * rate * rate) * centred * head_mean(grouped_grad * centred)
        ).astype(LOW)
        return carry

    lax.fori_loop(0, members // 2, unmix, 0)
    scatter.near(0, turned, mixed, 0)
    lax.fori_loop(members // 2, members, unmix, 0)
    scatter.near(0, turned, mixed, 1)
    scatter.far(1, normed_turned, gate_low)
    gate_copy = fetch(weights[1], wide_one, 1)

    def decay(h, late, early, late_segment, early_segment, turn):
        sign = -1 if turn else 1
        distance = (
            sign
            * (
                lax.broadcasted_iota(jnp.int32, (rows, rows), 0)
                - lax.broadcasted_iota(jnp.int32, (rows, rows), 1)
            )
            + (late - early)
        )
        same = (distance >= 0) & (late_segment == early_segment)
        return jnp.where(
            same,
            jnp.exp(rate_ref[h : h + 1, :1] * jnp.maximum(distance, 0).astype(WIDE)),
            0.0,
        )

    def start_of(k):
        return pl.multiple_of(near.member(k) * rows, rows)

    wing = KEY // 2
    along = [along_seg[:, pl.ds(start_of(k), rows)] for k in range(members)]

    def turn_back(target, k, h, grad, scale):
        at = pl.ds(pl.multiple_of(k * rows, rows), rows)
        cosine, sine = cos_ref[at, :], sin_ref[at, :]
        first, second = grad[:, :wing], grad[:, wing:]
        target[k, :, h * KEY : h * KEY + wing] = (
            (first * cosine + second * sine) * scale
        ).astype(LOW)
        target[k, :, h * KEY + wing : (h + 1) * KEY] = (
            (second * cosine - first * sine) * scale
        ).astype(LOW)

    def early_side(m, carry):
        early = start_of(m)
        early_segment = down_seg[pl.ds(early, rows), :]
        value_grads = []
        for h in range(heads):
            head = slice(h * KEY, (h + 1) * KEY)
            masked = jnp.where(inside(h), values[m].astype(WIDE), 0.0).astype(LOW)
            value_grad = jnp.zeros((rows, value_columns), WIDE)
            key_grad = jnp.zeros((rows, KEY), WIDE)
            for n in range(members):
                late = start_of(n)
                late_segment = along[n]
                mask = decay(h, late, early, late_segment, early_segment, True)
                score = (dot_across(keys[m, :, head], query[n, :, head]) * mask).astype(LOW)
                raw = (dot_across(masked, retained_low[n]) * mask).astype(LOW)
                value_grad += jnp.dot(score, retained_low[n], preferred_element_type=WIDE)
                key_grad += jnp.dot(raw, query[n, :, head], preferred_element_type=WIDE)
            value_grads.append(value_grad)
            turn_back(key_low, m, h, key_grad, 1.0)
        value_low[m] = by_head(value_grads).astype(LOW)
        return carry

    scatter.near(0, turned, mixed, 2)
    scatter.near(0, turned, mixed, 3)
    early_side(0, 0)
    for m in range(1, members):
        early_side(m, 0)
        scatter.near(1, normed_turned, gate_low, m - 1)
    scatter.far(2, normed_turned, value_low)
    scatter.far(4, normed_turned, key_low)
    scatter.near(1, normed_turned, gate_low, 3)

    def late_side(n, carry):
        late = start_of(n)
        late_segment = down_seg[pl.ds(late, rows), :]
        for h in range(heads):
            head = slice(h * KEY, (h + 1) * KEY)
            masked = jnp.where(inside(h), retained_low[n].astype(WIDE), 0.0).astype(LOW)
            query_grad = jnp.zeros((rows, KEY), WIDE)
            for m in range(members):
                early = start_of(m)
                early_segment = along[m]
                mask = decay(h, late, early, late_segment, early_segment, False)
                raw = (dot_across(masked, values[m]) * mask).astype(LOW)
                query_grad += jnp.dot(raw, keys[m, :, head], preferred_element_type=WIDE)
            turn_back(query_low, n, h, query_grad, KEY ** (-0.5))
        return carry

    lax.fori_loop(0, members // 2, late_side, 0)
    scatter.near(2, normed_turned, value_low, 0)
    lax.fori_loop(members // 2, members, late_side, 0)
    scatter.near(2, normed_turned, value_low, 1)
    scatter.far(3, normed_turned, query_low)
    for copy in (gate_copy, value_copy, query_copy, key_copy, grad_copy):
        copy.wait()

    def back(k, put):
        for p in range(parts):
            columns = slice(p * slice_width, (p + 1) * slice_width)
            put(
                columns,
                dot_across(gate_low[k], wide_one[p])
                + dot_across(value_low[k], wide_two[p])
                + dot_across(query_low[k], short_one[p])
                + dot_across(key_low[k], short_two[p]),
            )

    def put_low(slot):
        def put(columns, value):
            held[slot, :, columns] = value.astype(LOW)

        return put

    def put_sum(columns, value):
        base[:, columns] = value

    back(3, put_low(0))
    near.start(0, held.at[0], got.at[0], 1)
    back(2, put_sum)
    scatter.near(2, normed_turned, value_low, 2)
    near.wait(0)
    near.sent(0)
    held[0] = (base[...] + got[0].astype(WIDE)).astype(LOW)
    near.start(1, held.at[0], got.at[1], 2)
    back(1, put_low(1))
    near.start(2, held.at[1], got.at[2], 1)
    scatter.near(2, normed_turned, value_low, 3)
    back(0, put_sum)
    for quarter in range(4):
        scatter.near(4, normed_turned, key_low, quarter)
    near.wait(2)
    base[...] += got[2].astype(WIDE)
    near.wait(1)
    normed_grad = base[...] + got[1].astype(WIDE)
    base[...] = normed_grad
    resid = hidden_ref[...].astype(WIDE)
    scale = lax.rsqrt(jnp.mean(resid * resid, axis=-1, keepdims=True) + 1e-06)
    dot = jnp.zeros((rows, 1), WIDE)
    for p in range(parts):
        columns = slice(p * slice_width, (p + 1) * slice_width)
        product = base[:, columns] * (hidden_ref[:, columns].astype(WIDE) * scale)
        row = lax.broadcasted_iota(jnp.int32, (8, slice_width), 0)
        pieces[p] = jnp.where(
            row == 0, jnp.sum(product, axis=0, keepdims=True), gain_part[:, columns]
        )
        dot += jnp.sum(product * gain_all[p][0:1], axis=-1, keepdims=True)
    dot = dot * (1.0 / width)
    gains = []
    for k in range(1, parts):
        other = lax.rem(me + k, parts)
        place = lax.rem(other, 2) * lines + other // 2
        copy = remote(
            pieces.at[place], piece_got.at[k], gain_send.at[k], gain_recv.at[k], others[k - 1]
        )
        copy.start()
        gains.append(copy)
    for p in range(parts):
        columns = slice(p * slice_width, (p + 1) * slice_width)
        block = hidden_ref[:, columns].astype(WIDE) * scale
        base[:, columns] = in_grad_out[:, columns] + scale * (
            base[:, columns] * gain_all[p][0:1] - block * dot
        )
    for p in range(parts):
        start = (2 * (p % lines) + p // lines) * slice_width
        in_grad_out[:, start : start + slice_width] = base[
            :, p * slice_width : (p + 1) * slice_width
        ]
    value = pieces[here]
    for k in range(1, parts):
        gains[k - 1].wait_recv()
        value = value + piece_got[k]
    total[...] = value
    for k in range(1, members):
        near.start(2 + k, total, total_got.at[k], k)
    for quarter in range(4):
        scatter.near(3, normed_turned, query_low, quarter)
    for w in (0, 1, 2, 4, 3):
        scatter.finish(w)
    for k in range(1, members):
        near.wait(2 + k)
        value = value + total_got[k]
    gain_out[...] = value
    for tag in range(1, 2 + members):
        near.sent(tag)
    for copy in gains:
        copy.wait_send()


def retention_backward(inside, streamed, weights, lines, members, slice_width):
    parts = 2 * lines
    rows, width = inside[10].shape
    blocks = (members, rows)
    wide, short = weights[0].shape[2], weights[3].shape[2]
    widths = [wide, wide, wide, short, short]
    pieces = [(lines, slice_width, columns) for columns in widths]
    outs = [(piece, LOW) for piece in pieces]
    outs += [((rows, width), WIDE), ((8, slice_width), WIDE)]
    outs += [((lines + 1,) + piece[1:], LOW) for piece in pieces]
    tail = max(tail_rows(slice_width, lines), 16)
    outs += [((lines, tail, columns), LOW) for columns in widths]
    return pl.pallas_call(
        functools.partial(retention_kernel, lines, members),
        out_shape=[jax.ShapeDtypeStruct(shape, dtype) for shape, dtype in outs],
        in_specs=[ANY] * 5 + [INSIDE] * 8 + [ANY] * 9,
        out_specs=[ANY] * 5 + [INSIDE] * 2 + [ANY] * 10,
        scratch_shapes=[
            pltpu.VMEM((width, rows * members), LOW),
            pltpu.VMEM(weights[0].shape, LOW),
            pltpu.VMEM(weights[0].shape, LOW),
            pltpu.VMEM(weights[3].shape, LOW),
            pltpu.VMEM(weights[3].shape, LOW),
            pltpu.VMEM(blocks + (wide,), LOW),
            pltpu.VMEM(blocks + (wide,), LOW),
            pltpu.VMEM(blocks + (short,), LOW),
            pltpu.VMEM(blocks + (short,), LOW),
        ]
        + [pltpu.VMEM(piece, LOW) for piece in pieces]
        + [
            pltpu.VMEM((slice_width, wide), LOW),
            pltpu.VMEM((slice_width, short), LOW),
            pltpu.VMEM((2, rows, width), LOW),
            pltpu.VMEM((3, rows, width), LOW),
            pltpu.VMEM((rows, width), WIDE),
            pltpu.VMEM((rows, wide), WIDE),
            pltpu.VMEM((rows, wide), WIDE),
            pltpu.VMEM((parts, 8, slice_width), WIDE),
            pltpu.VMEM((parts, 8, slice_width), WIDE),
            pltpu.VMEM((8, slice_width), WIDE),
            pltpu.VMEM((members, 8, slice_width), WIDE),
            pltpu.SemaphoreType.DMA((5, lines)),
            pltpu.SemaphoreType.DMA((5, lines)),
            pltpu.SemaphoreType.DMA((5, lines)),
            pltpu.SemaphoreType.DMA((5, lines)),
            pltpu.SemaphoreType.DMA((5, lines)),
            pltpu.SemaphoreType.DMA((5, lines)),
            pltpu.SemaphoreType.DMA((6,)),
            pltpu.SemaphoreType.DMA((6,)),
            pltpu.SemaphoreType.DMA((parts,)),
            pltpu.SemaphoreType.DMA((parts,)),
            pltpu.SemaphoreType.DMA((14,)),
        ]
        + [pltpu.VMEM(value.shape, value.dtype) for value in inside[:5]]
        + [pltpu.VMEM((tail, columns), LOW) for columns in widths],
        compiler_params=pltpu.CompilerParams(
            collective_id=2, has_side_effects=True, vmem_limit_bytes=ROOM
        ),
        cost_estimate=pl.CostEstimate(flops=10**11, bytes_accessed=10**9, transcendentals=0),
        name="retention_backward",
    )(*inside, *streamed, *weights)[:7]


def on_device(
    hidden_in,
    out_grad,
    segment_ids,
    norm1_gain,
    w_query,
    w_key,
    w_value,
    w_gate,
    w_out,
    norm2_gain,
    w_mlp_gate,
    w_mlp_up,
    w_mlp_down,
):
    _, rows, width = hidden_in.shape
    parts = lax.axis_size("dp")
    lines = parts // 2
    slice_width = width // parts
    own = lax.axis_index("tensor")
    members = lax.axis_size("tensor")
    order = list(range(0, parts, 2)) + list(range(1, parts, 2))

    def to_places(value):
        blocks = [value[:, k * slice_width : (k + 1) * slice_width] for k in order]
        return jnp.concatenate(blocks, axis=1)

    heads_here = w_query.shape[1] // KEY
    resid_low = to_places(hidden_in.reshape(rows, width))
    grad_local = to_places(out_grad.reshape(rows, width))
    gain_rows = jnp.stack([norm1_gain, norm2_gain])
    position = jnp.concatenate(
        [(own ^ k) * rows + jnp.arange(rows, dtype=jnp.int32) for k in range(members)]
    )
    cosine, sine = rotary_tables(position, KEY)
    head_numbers = (jnp.arange(heads_here, dtype=jnp.int32) + own * heads_here).astype(WIDE)
    rates = jnp.log1p(-jnp.exp2(-5.0 - head_numbers))
    rates = jnp.broadcast_to(rates[:, None], (heads_here, 128))
    outs = forward(
        resid_low,
        grad_local,
        gain_rows,
        cosine,
        sine,
        segment_ids,
        rates,
        [w_query, w_key, w_value, w_gate, w_out.T, w_mlp_gate, w_mlp_up, w_mlp_down.T],
        lines,
        members,
    )
    normed_turned, grad_full, gains = outs[:3]
    query_weight, key_weight, value_weight, gate_weight, out_weight = outs[3:8]
    query, keys, values, gate_pre, grad_turned = outs[11:16]
    retained, mixed, resid_mid, mid_turned, gate_hidden, up_hidden, hidden = outs[16:]
    down_grad, mlp_gate_grad, mlp_up_grad, mid_all, mid_grad, hidden_out, gain_part = feed_backward(
        grad_full,
        grad_turned,
        mid_turned,
        hidden,
        resid_mid,
        gains,
        outs[8:11],
        (gate_hidden, up_hidden),
        lines,
        members,
    )
    out_weight_grad, gate_grad, value_grad, query_grad, key_grad, in_grad, gain_total = (
        retention_backward(
            [
                mixed,
                normed_turned,
                query,
                keys,
                values,
                cosine,
                sine,
                segment_ids.T,
                segment_ids,
                rates,
                resid_low,
                gains,
                gain_part,
            ],
            [mid_grad, mid_all, retained, gate_pre],
            [out_weight, gate_weight, value_weight, query_weight, key_weight],
            lines,
            members,
            slice_width,
        )
    )
    def add_up(pieces):
        return jnp.sum(pieces.astype(WIDE), axis=0)

    return (
        hidden_out.reshape(hidden_in.shape),
        in_grad.reshape(hidden_in.shape),
        gain_total[0],
        add_up(query_grad),
        add_up(key_grad),
        add_up(value_grad),
        add_up(gate_grad),
        add_up(out_weight_grad).T,
        gain_total[1],
        add_up(mlp_gate_grad),
        add_up(mlp_up_grad),
        add_up(down_grad).T,
    )


def solution(mesh):
    return jax.shard_map(
        on_device,
        mesh=mesh,
        in_specs=(
            P("dp", "tensor", None),
            P("dp", "tensor", None),
            P("dp", None),
            P("dp"),
            P("dp", "tensor"),
            P("dp", "tensor"),
            P("dp", "tensor"),
            P("dp", "tensor"),
            P("tensor", "dp"),
            P("dp"),
            P("dp", "tensor"),
            P("dp", "tensor"),
            P("tensor", "dp"),
        ),
        out_specs=(
            P("dp", "tensor", None),
            P("dp", "tensor", None),
            P("dp"),
            P("dp", "tensor"),
            P("dp", "tensor"),
            P("dp", "tensor"),
            P("dp", "tensor"),
            P("tensor", "dp"),
            P("dp"),
            P("dp", "tensor"),
            P("dp", "tensor"),
            P("tensor", "dp"),
        ),
        check_vma=False,
    )
```

```python
import functools
import math

import jax
import jax.numpy as jnp
from jax import lax
from jax.experimental import pallas as pl
from jax.experimental.pallas import tpu as pltpu
from jax.sharding import PartitionSpec as P

KEY = 256
VAL = 432
LOW = jnp.bfloat16
WIDE = jnp.float32
WEIGHTS = 8
MESH = pl.DeviceIdType.MESH
ANY = pl.BlockSpec(memory_space=pl.ANY)
INSIDE = pl.BlockSpec(memory_space=pltpu.VMEM)
ROOM = 60 * 1024 * 1024

def rotary_tables(position, width):
    half = width // 2
    frequency = 10000.0 ** (-2.0 * jnp.arange(half, dtype=jnp.int32).astype(WIDE) / width)
    angle = position.astype(WIDE)[:, None] * frequency[None, :]
    return (jnp.cos(angle), jnp.sin(angle))


def greet(peers):
    barrier = pltpu.get_barrier_semaphore()
    for peer in peers:
        pl.semaphore_signal(barrier, inc=1, device_id=peer, device_id_type=MESH)
    pl.semaphore_wait(barrier, len(peers))


def remote(source, target, send, recv, device):
    return pltpu.make_async_remote_copy(
        src_ref=source,
        dst_ref=target,
        send_sem=send,
        recv_sem=recv,
        device_id=device,
        device_id_type=MESH,
    )


def forward_kernel(lines, members, *refs):
    hidden_ref, grad_ref, gain_ref, cos_ref, sin_ref, down_seg, along_seg, rate_ref = refs[:8]
    shards = refs[8:16]
    normed_turned, grad_all, gain_all = refs[16:19]
    wholes = refs[19:27]
    query_out, keys_out, values_out, gate_out, grad_turned = refs[27:32]
    retained_out, mixed_out, resid_out, mid_turned, gate_hidden_out, up_hidden_out = refs[32:38]
    hidden_out = refs[38]
    normed, mid, short, wide_one, wide_two, turned = refs[39:45]
    query, keys, scores, values, retained, gate, mixed, hidden = refs[45:53]
    held, got, base = refs[53:56]
    line_send, line_recv, side_send, side_recv = refs[56:60]
    near_send, near_recv, gain_send, gain_recv, home, tail_send, tail_recv, gain_rows, raw, flip = refs[60:]

    parts = 2 * lines
    rows, width = hidden_ref.shape
    slice_width = gain_rows.shape[1]
    heads = rate_ref.shape[0]
    value_columns = values.shape[2]
    me = lax.axis_index("dp")
    line, side = me // 2, lax.rem(me, 2)
    here = side * lines + line
    own = lax.axis_index("tensor")
    half, rest = own // 2, lax.rem(own, 2)

    def member(k):
        return 2 * lax.rem(half + k // 2, 2) + lax.rem(rest + lax.rem(k, 2), 2)

    partners = [None] + [{"tensor": member(k)} for k in range(1, members)]
    others = [{"dp": lax.rem(me + k, parts)} for k in range(1, parts)]
    opposite = {"dp": 2 * line + (1 - side)}
    greet(others + partners[1:])

    local = {}
    slots = iter(range(32))

    def keep(source, target):
        slot = next(slots)
        local[slot] = pltpu.make_async_copy(source, target, home.at[slot])
        local[slot].start()
        return slot

    def finish(slot):
        local.pop(slot).wait()

    near = {}

    def near_start(tag, source, target, k):
        copy = remote(source, target, near_send.at[tag], near_recv.at[tag], partners[k])
        copy.start()
        near[tag] = copy

    across = {}
    ours = {}

    inner = lines == 4

    def line_copy(w, step):
        return remote(
            source(w),
            wholes[w].at[here],
            line_send.at[w, step],
            line_recv.at[w, step],
            {"dp": 2 * lax.rem(line + step, lines) + side},
        )

    def relay_copy(w):
        place = side * lines + 3 * (2 - line)
        return remote(
            wholes[w].at[place],
            wholes[w].at[place],
            line_send.at[w, 0],
            line_recv.at[w, 2 * line - 1],
            {"dp": 6 * (line - 1) + side},
        )

    tail = slice_width // 8 // 16 * 16
    most = slice_width - tail

    def side_copy(w, step):
        place = side * lines + lax.rem(line + lines - step, lines)
        return remote(
            wholes[w].at[place, pl.ds(0, most)],
            wholes[w].at[place, pl.ds(0, most)],
            side_send.at[w, step],
            side_recv.at[w, step],
            opposite,
        )

    there = (1 - side) * lines + line

    def tail_copy(w, step):
        return remote(
            wholes[w].at[there, pl.ds(most, tail)],
            wholes[w].at[there, pl.ds(most, tail)],
            tail_send.at[w, step],
            tail_recv.at[w, step],
            {"dp": 2 * lax.rem(line + step, lines) + side},
        )

    def on_line(w, step, act):
        if inner and step != 2:

            @pl.when(line != (3 if step == 1 else 0))
            def _():
                act(line_copy(w, step))
        else:
            act(line_copy(w, step))

    sends = [2, 1, 3] if inner else list(range(1, lines))

    def prepare(w):
        if w < 2:
            ours[w] = keep(shards[w], wholes[w].at[here])
            return
        copy = pltpu.make_async_copy(shards[w], raw, home.at[home.shape[0] - 1])
        copy.start()
        copy.wait()
        columns = raw.shape[0]
        for at in range(0, columns, 128):
            block = slice(at, min(at + 128, columns))
            flip[:, block] = raw[block, :].T
        copy = pltpu.make_async_copy(flip, wholes[w].at[here], home.at[home.shape[0] - 1])
        copy.start()
        copy.wait()

    def source(w):
        return shards[w] if w < 2 else wholes[w].at[here]

    def start_lines(w):
        prepare(w)
        for step in sends:
            on_line(w, step, lambda copy: copy.start())
        across[w, 0] = remote(
            source(w), wholes[w].at[here], side_send.at[w, 0], side_recv.at[w, 0], opposite
        )
        across[w, 0].start()

    def pass_on(w, third):
        for at in range(third * (lines - 1) // 3, (third + 1) * (lines - 1) // 3):
            step = at + 1
            if inner:
                late = 3 - 2 * ((3 - line) // 3)
                step = [2, 4 - late, late][at]
            if tail and at == 0:
                across[w, 0].wait_recv()
                for hop in range(1, lines):
                    tail_copy(w, hop).start()
            line_copy(w, step).wait_recv()
            if inner and at == 0:

                @pl.when((line == 1) | (line == 2))
                def _():
                    relay_copy(w).start()

            side_copy(w, step).start()

    def complete(w):
        if not tail:
            across[w, 0].wait_recv()
        for step in range(1, lines):
            side_copy(w, step).wait_recv()
            if tail:
                tail_copy(w, step).wait_recv()
        if w in ours:
            finish(ours[w])

    def load(w, target, sem):
        copy = pltpu.make_async_copy(wholes[w], target, sem)
        copy.start()
        copy.wait()

    def stage(w, target, body):
        if w + 1 < WEIGHTS:
            for third in range(3):
                pass_on(w + 1, third)
        if w + 3 < WEIGHTS:
            start_lines(w + 3)
        complete(w)
        load(w, target, home.at[home.shape[0] - 1 - w])
        lax.fori_loop(0, members, body, 0)

    gain_rows[...] = jnp.where(
        lax.broadcasted_iota(jnp.int32, gain_rows.shape, 0) == 0,
        gain_ref[0:1, :].astype(WIDE),
        gain_ref[1:2, :].astype(WIDE),
    )
    gains = []
    for k in range(1, parts):
        copy = remote(
            gain_rows, gain_all.at[here], gain_send.at[k], gain_recv.at[k], others[k - 1]
        )
        copy.start()
        gains.append(copy)
    gain_all[here] = gain_rows[...]
    for w in range(3):
        start_lines(w)

    def scale_into(target, scaled, which):
        for p in range(parts):
            columns = slice(p * slice_width, (p + 1) * slice_width)
            target[0, :, columns] = (
                scaled[:, columns] * gain_all[p][which : which + 1]
            ).astype(LOW)

    resid = hidden_ref[...].astype(WIDE)
    scaled = resid * lax.rsqrt(jnp.mean(resid * resid, axis=-1, keepdims=True) + 1e-06)
    for copy in gains:
        copy.wait_recv()
    scale_into(normed, scaled, 0)
    for k in range(1, members):
        near_start(k - 1, normed.at[0], normed.at[k], k)
    for k in range(1, members):
        near_start(2 + k, grad_ref, mid.at[k], k)
    grad_kept = keep(grad_ref, mid.at[0])
    for third in range(3):
        pass_on(0, third)
    for k in range(1, members):
        near[k - 1].wait_recv()

    def turn_over(source):
        tile = 256

        def body(k, carry):
            at = pl.ds(pl.multiple_of(k * rows, rows), rows)
            for c in range(width // tile):
                columns = slice(c * tile, (c + 1) * tile)
                turned[columns, at] = source[k, :, columns].T
            return carry

        lax.fori_loop(0, members, body, 0)

    turn_over(normed)
    turned_kept = keep(turned, normed_turned)

    def flat(ref):
        return ref[...].reshape(width, ref.shape[2])

    def turn(source, target, scale):
        def body(k, carry):
            pre = jnp.dot(normed[k], flat(source), preferred_element_type=WIDE)
            at = pl.ds(pl.multiple_of(k * rows, rows), rows)
            cosine, sine = cos_ref[at, :], sin_ref[at, :]
            wing = KEY // 2
            for h in range(heads):
                first = pre[:, h * KEY : h * KEY + wing]
                second = pre[:, h * KEY + wing : (h + 1) * KEY]
                target[k, :, h * KEY : h * KEY + wing] = (
                    (first * cosine - second * sine) * scale
                ).astype(LOW)
                target[k, :, h * KEY + wing : (h + 1) * KEY] = (
                    (second * cosine + first * sine) * scale
                ).astype(LOW)
            return carry

        return body

    stage(0, short, turn(short, query, KEY ** (-0.5)))
    keep(query, query_out)
    stage(1, short, turn(short, keys, 1.0))
    keep(keys, keys_out)

    def score(k, carry):
        place = member(k)
        at = pl.multiple_of(place * rows, rows)
        segment = down_seg[pl.ds(at, rows), :]
        for h in range(heads):
            head = slice(h * KEY, (h + 1) * KEY)
            for m in range(members):
                start = pl.multiple_of(member(m) * rows, rows)
                raw = lax.dot_general(
                    query[k, :, head],
                    keys[m, :, head],
                    (((1,), (1,)), ((), ())),
                    preferred_element_type=WIDE,
                )
                distance = (
                    lax.broadcasted_iota(jnp.int32, (rows, rows), 0)
                    - lax.broadcasted_iota(jnp.int32, (rows, rows), 1)
                    + (at - start)
                )
                same = (distance >= 0) & (segment == along_seg[:, pl.ds(start, rows)])
                decay = jnp.exp(
                    rate_ref[h : h + 1, :1] * jnp.maximum(distance, 0).astype(WIDE)
                )
                scores[h, k, :, m * rows : (m + 1) * rows] = (
                    raw * jnp.where(same, decay, 0.0)
                ).astype(LOW)
        return carry

    lax.fori_loop(0, members, score, 0)
    finish(grad_kept)
    for k in range(1, members):
        near[2 + k].wait_recv()
    finish(turned_kept)
    turn_over(mid)
    turned_kept = keep(turned, grad_turned)
    grad_kept = keep(mid, grad_all)

    column = lax.broadcasted_iota(jnp.int32, (rows, value_columns), 1)

    def by_head(parts_of):
        result = parts_of[0]
        for h in range(1, heads):
            result = jnp.where(column < h * VAL, result, parts_of[h])
        return result

    def head_mean(value):
        means = []
        for h in range(heads):
            inside = (column >= h * VAL) & (column < (h + 1) * VAL)
            total = jnp.sum(jnp.where(inside, value, 0.0), axis=-1, keepdims=True)
            means.append(total * (1.0 / VAL))
        return by_head(means)

    def make_values(k, carry):
        values[k] = jnp.dot(normed[k], flat(wide_one), preferred_element_type=WIDE).astype(LOW)
        return carry

    stage(2, wide_one, make_values)
    keep(values, values_out)

    def retain(k, carry):
        every = values[...].reshape(members * rows, value_columns)
        retained[k] = by_head(
            [
                jnp.dot(scores[h, k], every, preferred_element_type=WIDE)
                for h in range(heads)
            ]
        )
        return carry

    lax.fori_loop(0, members, retain, 0)
    retained_kept = keep(retained, retained_out)

    def make_mixed(k, carry):
        pre = jnp.dot(normed[k], flat(wide_two), preferred_element_type=WIDE)
        gate[k] = pre
        value = retained[k]
        centred = value - head_mean(value)
        grouped = centred * lax.rsqrt(head_mean(centred * centred) + 1.0)
        mixed[k] = (grouped * (pre / (1.0 + jnp.exp(-pre)))).astype(LOW)
        return carry

    stage(3, wide_two, make_mixed)
    gate_kept = keep(gate, gate_out)
    keep(mixed, mixed_out)

    def project(k, put):
        for p in range(parts):
            columns = slice(p * slice_width, (p + 1) * slice_width)
            put(
                columns,
                lax.dot_general(
                    mixed[k],
                    wide_one[p],
                    (((1,), (1,)), ((), ())),
                    preferred_element_type=WIDE,
                ),
            )

    def put_low(slot):
        def put(columns, value):
            held[slot, :, columns] = value.astype(LOW)

        return put

    def put_sum(columns, value):
        base[:, columns] = value

    pass_on(5, 0)
    complete(4)
    load(4, wide_one, home.at[home.shape[0] - 5])
    finish(grad_kept)
    project(3, put_low(0))
    near_start(6, held.at[0], got.at[0], 1)
    project(2, put_sum)
    pass_on(5, 1)
    near[6].wait_recv()
    held[1] = (base[...] + got[0].astype(WIDE)).astype(LOW)
    near_start(8, held.at[1], got.at[1], 2)
    project(1, put_low(2))
    near_start(7, held.at[2], got.at[2], 1)
    project(0, put_sum)
    pass_on(5, 2)
    start_lines(7)
    near[7].wait_recv()
    base[...] = base[...] + got[2].astype(WIDE) + hidden_ref[...].astype(WIDE)
    pass_on(6, 0)
    near[8].wait_recv()
    resid = base[...] + got[1].astype(WIDE)
    resid_out[...] = resid
    scaled = resid * lax.rsqrt(jnp.mean(resid * resid, axis=-1, keepdims=True) + 1e-06)
    scale_into(mid, scaled, 1)
    near_start(10, mid.at[0], mid.at[2], 2)
    near_start(9, mid.at[0], mid.at[1], 1)
    pass_on(6, 1)
    pass_on(6, 2)
    near[10].wait_recv()
    near_start(11, mid.at[2], mid.at[3], 1)
    complete(5)
    load(5, wide_two, home.at[home.shape[0] - 6])
    near[9].wait_recv()
    near[11].wait_recv()
    finish(retained_kept)
    finish(gate_kept)

    def make_gate(k, carry):
        gate[k] = jnp.dot(mid[k], flat(wide_two), preferred_element_type=WIDE)
        return carry

    lax.fori_loop(0, members, make_gate, 0)
    keep(gate, gate_hidden_out)
    finish(turned_kept)
    turn_over(mid)
    keep(turned, mid_turned)
    pass_on(7, 0)
    pass_on(7, 1)
    pass_on(7, 2)
    complete(6)
    load(6, wide_one, home.at[home.shape[0] - 7])

    def make_hidden(k, carry):
        up = jnp.dot(mid[k], flat(wide_one), preferred_element_type=WIDE)
        retained[k] = up
        pre = gate[k]
        inner = (2.0 / math.pi) ** 0.5 * (pre + 0.044715 * (pre * pre * pre))
        hidden[k] = (0.5 * pre * (1.0 + jnp.tanh(inner)) * up).astype(LOW)
        return carry

    lax.fori_loop(0, members, make_hidden, 0)
    keep(retained, up_hidden_out)
    keep(hidden, hidden_out)
    complete(7)
    for w in range(WEIGHTS):
        for step in sends:
            on_line(w, step, lambda copy: copy.wait_send())
            side_copy(w, step).wait_send()
            if tail:
                tail_copy(w, step).wait_send()
        across[w, 0].wait_send()
        if inner:

            @pl.when((line == 1) | (line == 2))
            def _():
                relay_copy(w).wait_send()

    for copy in gains:
        copy.wait_send()
    for copy in near.values():
        copy.wait_send()
    for slot in list(local):
        finish(slot)


def forward(hidden, grad, gains, cosine, sine, segments, rates, shards, lines, members):
    parts = 2 * lines
    rows, width = hidden.shape
    heads = rates.shape[0]
    key_columns, value_columns = shards[0].shape[1], shards[2].shape[0]
    chunks = [shard.shape if k < 2 else shard.shape[::-1] for k, shard in enumerate(shards)]
    length = rows * members
    blocks = (members, rows)
    turned = (width, length)
    outs = [
        (turned, LOW),
        (blocks + (width,), LOW),
        ((parts, 8, gains.shape[1]), WIDE),
    ]
    outs += [((parts,) + chunk, LOW) for chunk in chunks]
    outs += [
        (blocks + (key_columns,), LOW),
        (blocks + (key_columns,), LOW),
        (blocks + (value_columns,), LOW),
        (blocks + (value_columns,), WIDE),
        (turned, LOW),
        (blocks + (value_columns,), WIDE),
        (blocks + (value_columns,), LOW),
        ((rows, width), WIDE),
        (turned, LOW),
        (blocks + (value_columns,), WIDE),
        (blocks + (value_columns,), WIDE),
        (blocks + (value_columns,), LOW),
    ]
    places = [ANY] * len(outs)
    places[2] = INSIDE
    places[18] = INSIDE
    tags = 12
    return pl.pallas_call(
        functools.partial(forward_kernel, lines, members),
        out_shape=[jax.ShapeDtypeStruct(shape, dtype) for shape, dtype in outs],
        in_specs=[INSIDE, ANY] + [INSIDE] * 6 + [ANY] * WEIGHTS,
        out_specs=places,
        scratch_shapes=[
            pltpu.VMEM(blocks + (width,), LOW),
            pltpu.VMEM(blocks + (width,), LOW),
            pltpu.VMEM((parts,) + chunks[0], LOW),
            pltpu.VMEM((parts,) + chunks[2], LOW),
            pltpu.VMEM((parts,) + chunks[2], LOW),
            pltpu.VMEM(turned, LOW),
            pltpu.VMEM(blocks + (key_columns,), LOW),
            pltpu.VMEM(blocks + (key_columns,), LOW),
            pltpu.VMEM((heads, members, rows, length), LOW),
            pltpu.VMEM(blocks + (value_columns,), LOW),
            pltpu.VMEM(blocks + (value_columns,), WIDE),
            pltpu.VMEM(blocks + (value_columns,), WIDE),
            pltpu.VMEM(blocks + (value_columns,), LOW),
            pltpu.VMEM(blocks + (value_columns,), LOW),
            pltpu.VMEM((3, rows, width), LOW),
            pltpu.VMEM((3, rows, width), LOW),
            pltpu.VMEM((rows, width), WIDE),
            pltpu.SemaphoreType.DMA((WEIGHTS, lines)),
            pltpu.SemaphoreType.DMA((WEIGHTS, lines)),
            pltpu.SemaphoreType.DMA((WEIGHTS, lines)),
            pltpu.SemaphoreType.DMA((WEIGHTS, lines)),
            pltpu.SemaphoreType.DMA((tags,)),
            pltpu.SemaphoreType.DMA((tags,)),
            pltpu.SemaphoreType.DMA((parts,)),
            pltpu.SemaphoreType.DMA((parts,)),
            pltpu.SemaphoreType.DMA((40,)),
            pltpu.SemaphoreType.DMA((WEIGHTS, lines)),
            pltpu.SemaphoreType.DMA((WEIGHTS, lines)),
            pltpu.VMEM((8, gains.shape[1]), WIDE),
            pltpu.VMEM(shards[2].shape, LOW),
            pltpu.VMEM(shards[2].shape[::-1], LOW),
        ],
        compiler_params=pltpu.CompilerParams(
            collective_id=0, has_side_effects=True, vmem_limit_bytes=ROOM
        ),
        cost_estimate=pl.CostEstimate(
            flops=10**11, bytes_accessed=10**9, transcendentals=0
        ),
        name="forward",
    )(hidden, grad, gains, cosine, sine, segments.T, segments, rates, *shards)


def tail_rows(rows, lines):
    return rows // 8 // 16 * 16 if lines == 4 else 0


class Scatter:
    def __init__(self, lines, held, far_got, near_got, tail_got, spare, tails, sems):
        self.lines = lines
        self.held, self.far_got, self.near_got, self.spare = held, far_got, near_got, spare
        self.tail_got, self.tails = tail_got, tails
        self.side_send, self.side_recv, self.line_send, self.line_recv = sems[:4]
        self.tail_send, self.tail_recv, self.home = sems[4:]
        self.rows = held[0].shape[1]
        self.tail = tail_rows(self.rows, lines)
        self.most = self.rows - self.tail
        me = lax.axis_index("dp")
        self.line, self.side = me // 2, lax.rem(me, 2)
        self.opposite = {"dp": 2 * self.line + (1 - self.side)}

    def peer(self, step):
        return {"dp": 2 * lax.rem(self.line + step, self.lines) + self.side}

    def peers(self):
        return [self.opposite] + [self.peer(step) for step in range(1, self.lines)]

    def far_copy(self, w, place):
        return remote(
            self.held[w].at[place, pl.ds(0, self.most)],
            self.far_got[w].at[place, pl.ds(0, self.most)],
            self.side_send.at[w, place],
            self.side_recv.at[w, place],
            self.opposite,
        )

    def near_copy(self, w, step):
        place = lax.rem(self.line + step, self.lines)
        return remote(
            self.held[w].at[place],
            self.near_got[w].at[step],
            self.line_send.at[w, step],
            self.line_recv.at[w, step],
            self.peer(step),
        )

    def fetch(self, source):
        rows, columns = source.shape
        spare = self.spare[columns].at[pl.ds(0, rows)]
        copy = pltpu.make_async_copy(source, spare, self.home)
        copy.start()
        copy.wait()
        return spare[...].astype(WIDE)


    def tail_copy(self, w, step):
        place = lax.rem(self.line + step, self.lines)
        return remote(
            self.held[w].at[place, pl.ds(self.most, self.tail)],
            self.tail_got[w].at[step],
            self.tail_send.at[w, step],
            self.tail_recv.at[w, step],
            self.peer(step),
        )

    def tail_across(self, w):
        return remote(
            self.tails[w],
            self.tail_got[w].at[0],
            self.tail_send.at[w, 0],
            self.tail_recv.at[w, 0],
            self.opposite,
        )

    def add_tails(self, w):
        total = self.held[w][self.line, self.most :].astype(WIDE)
        for step in range(1, self.lines):
            self.tail_copy(w, step).wait_recv()
            total = total + self.fetch(self.tail_got[w].at[step])
        self.tails[w][...] = total.astype(LOW)
        self.tail_across(w).start()

    def product(self, left, right, place):
        rows = self.held[0].shape[1]
        block = left[pl.ds(pl.multiple_of(place * rows, rows), rows), :]
        every = right[...]
        return jnp.dot(
            block,
            every.reshape(every.shape[0] * every.shape[1], every.shape[2]),
            preferred_element_type=WIDE,
        )


    def extra_copy(self, w, step):
        place = lax.rem(self.line + step, self.lines)
        return remote(
            self.held[w].at[place],
            self.far_got[w].at[self.lines],
            self.line_send.at[w, step],
            self.line_recv.at[w, 0],
            {"dp": 2 * (2 if step == 1 else 1) + self.side},
        )

    def far(self, w, left, right):
        def body(at, carry):
            step = 1 + at
            if self.lines == 4:
                step = 1 + 2 * at - 3 * (at // 2)
            place = lax.rem(self.line + step, self.lines)
            other = (1 - self.side) * self.lines + place
            self.held[w][place] = self.product(left, right, other).astype(LOW)
            self.far_copy(w, place).start()
            if self.tail:

                @pl.when(at < self.lines - 1)
                def _():
                    self.tail_copy(w, step).start()

            return carry

        lax.fori_loop(0, self.lines, body, 0)

    def near(self, w, left, right, quarter):
        def put(place, step):
            part = self.product(left, right, self.side * self.lines + place)
            self.far_copy(w, place).wait_recv()
            got = self.fetch(self.far_got[w].at[place, pl.ds(0, self.most)])
            self.far_copy(w, place).wait_send()
            if self.tail and step is not None:
                self.tail_copy(w, step).wait_send()
            self.held[w][place, : self.most] = (part[: self.most] + got).astype(LOW)
            if self.tail:
                self.held[w][place, self.most :] = part[self.most :].astype(LOW)

        def body(step, carry):
            place = lax.rem(self.line + step, self.lines)
            put(place, step)
            self.near_copy(w, step).start()
            return carry

        if self.lines != 4:
            first, last = [1 + (quarter + k) * self.lines // 4 for k in range(2)]
            lax.fori_loop(first, min(last, self.lines), body, 0)
        elif quarter < 2:
            step = 1 + 2 * quarter
            end = 3 - 3 * quarter
            place = lax.rem(self.line + step, self.lines)
            put(place, step)

            @pl.when(self.line == end)
            def _():
                self.extra_copy(w, step).start()

            @pl.when(self.line != end)
            def _():
                self.near_copy(w, step).start()
        elif quarter == 2:
            place = lax.rem(self.line + 2, self.lines)
            put(place, 2)

            @pl.when((self.line == 1) | (self.line == 2))
            def _():
                self.extra_copy(w, 1).wait_recv()
                self.held[w][place] = (
                    self.held[w][place].astype(WIDE)
                    + self.fetch(self.far_got[w].at[self.lines])
                ).astype(LOW)

            self.near_copy(w, 2).start()
        if quarter < 3:
            return
        if self.tail:
            self.add_tails(w)
        put(self.line, None)
        if not self.tail:
            self.own_copy(w).start()
        if self.lines == 4:

            @pl.when((self.line == 0) | (self.line == 3))
            def _():
                spare = self.spare[self.held[w].shape[2]]
                spare[...] = jnp.zeros(spare.shape, LOW)
                slot = 1 + 2 * (self.line // 3)
                copy = pltpu.make_async_copy(spare, self.near_got[w].at[slot], self.home)
                copy.start()
                copy.wait()

    def own_copy(self, w):
        return pltpu.make_async_copy(
            self.held[w].at[self.line], self.near_got[w].at[0], self.line_send.at[w, 0]
        )

    def finish(self, w):
        if self.lines != 4:

            def body(step, carry):
                self.near_copy(w, step).wait()
                return carry

            lax.fori_loop(1, self.lines, body, 0)
        else:
            for step in range(1, 4):
                copy = self.near_copy(w, step)
                copy.wait_send()
                if step == 2:
                    copy.wait_recv()
                else:

                    @pl.when(self.line != (0 if step == 1 else 3))
                    def _():
                        copy.wait_recv()

        if self.tail:
            self.tail_across(w).wait()
            self.held[w][self.line, self.most :] = (
                self.held[w][self.line, self.most :].astype(WIDE)
                + self.fetch(self.tail_got[w].at[0])
            ).astype(LOW)
            self.own_copy(w).start()
        self.own_copy(w).wait()


class Near:
    def __init__(self, send, recv):
        self.send, self.recv = send, recv
        self.flight = {}
        own = lax.axis_index("tensor")
        half, rest = own // 2, lax.rem(own, 2)
        self.member = lambda k: 2 * lax.rem(half + k // 2, 2) + lax.rem(rest + lax.rem(k, 2), 2)

    def partners(self, members):
        return [{"tensor": self.member(k)} for k in range(1, members)]

    def start(self, tag, source, target, k):
        copy = remote(source, target, self.send.at[tag], self.recv.at[tag], self.partners(4)[k - 1])
        copy.start()
        self.flight[tag] = copy

    def wait(self, tag):
        self.flight[tag].wait_recv()

    def sent(self, tag):
        self.flight[tag].wait_send()


def dot_across(left, right):
    return lax.dot_general(
        left, right, (((1,), (1,)), ((), ())), preferred_element_type=WIDE
    )


def feed_kernel(lines, members, *refs):
    grad_turned, hidden, gain_all = refs[:3]
    later = refs[3:9]
    gate_hidden, up_hidden = refs[9:11]
    near_got, mid_all, mid_grad_out, hidden_out, gain_out = refs[11:14], *refs[14:18]
    mid_low_turned = refs[18]
    far_got, tail_got = refs[19:22], refs[22:25]
    gate_low, up_low, pre, up = refs[25:29]
    scatter_held = refs[29:32]
    spare, held, got, last, base, mid = refs[32:38]
    sems = refs[38:44]
    near_send, near_recv, home, column = refs[44:48]
    loaded, tails = refs[48:54], refs[54:]
    grad_ref, mid_turned, resid_ref, gate_weight, up_weight, down_weight = loaded
    parts = 2 * lines
    rows, width = resid_ref.shape
    loads = []
    for k, order in enumerate((5, 0, 1, 3, 4, 2)):
        loads.append(pltpu.make_async_copy(later[order], loaded[order], home.at[4 + k]))
        loads[k].start()
    slice_width = width // parts
    scatter = Scatter(
        lines,
        scatter_held,
        far_got,
        near_got,
        tail_got,
        {spare.shape[1]: spare},
        tails,
        sems + (home.at[0],),
    )
    near = Near(near_send, near_recv)
    greet(scatter.peers() + near.partners(members))
    scatter.far(0, grad_turned, hidden)

    def flat(ref):
        return ref[...].reshape(width, ref.shape[2])

    def pull(k, carry):
        first = pltpu.make_async_copy(gate_hidden.at[k], pre, home.at[1])
        second = pltpu.make_async_copy(up_hidden.at[k], up, home.at[2])
        first.start()
        second.start()
        grad = jnp.dot(grad_ref[k], flat(down_weight), preferred_element_type=WIDE)
        first.wait()
        second.wait()
        value = pre[...]
        root = (2.0 / math.pi) ** 0.5
        square = value * value
        lift = jnp.tanh(root * (value + 0.044715 * (value * square)))
        ramp = 0.5 * (1.0 + lift)
        slope = ramp + 0.5 * value * (1.0 - lift * lift) * root * (1.0 + 0.134145 * square)
        gate_low[k] = (grad * up[...] * slope).astype(LOW)
        up_low[k] = (grad * (value * ramp)).astype(LOW)
        return carry

    for load in loads:
        load.wait()
    lax.fori_loop(0, members // 2, pull, 0)
    scatter.near(0, grad_turned, hidden, 0)
    lax.fori_loop(members // 2, members, pull, 0)
    scatter.near(0, grad_turned, hidden, 1)
    scatter.far(1, mid_turned, gate_low)

    def back(k, put):
        for p in range(parts):
            columns = slice(p * slice_width, (p + 1) * slice_width)
            put(
                columns,
                dot_across(gate_low[k], gate_weight[p]) + dot_across(up_low[k], up_weight[p]),
            )

    def put_low(slot):
        def put(columns, value):
            held[slot, :, columns] = value.astype(LOW)

        return put

    def put_sum(columns, value):
        base[:, columns] = value

    back(3, put_low(0))
    near.start(0, held.at[0], got.at[0], 1)
    scatter.near(0, grad_turned, hidden, 2)
    back(2, put_sum)
    near.wait(0)
    near.sent(0)
    held[0] = (base[...] + got[0].astype(WIDE)).astype(LOW)
    near.start(1, held.at[0], got.at[1], 2)
    back(1, put_low(1))
    near.start(2, held.at[1], got.at[2], 1)
    scatter.near(0, grad_turned, hidden, 3)
    back(0, put_sum)
    scatter.far(2, mid_turned, up_low)
    scatter.near(1, mid_turned, gate_low, 0)
    near.wait(2)
    base[...] += got[2].astype(WIDE)
    scatter.near(1, mid_turned, gate_low, 1)
    near.wait(1)
    normed_grad = base[...] + got[1].astype(WIDE)
    resid = resid_ref[...]
    scale = lax.rsqrt(jnp.mean(resid * resid, axis=-1, keepdims=True) + 1e-06)
    unit = resid * scale
    base[...] = normed_grad * unit
    gain_out[...] = jnp.broadcast_to(
        jnp.sum(base[...], axis=0, keepdims=True), gain_out.shape
    )
    dot = jnp.zeros((rows, 1), WIDE)
    for p in range(parts):
        columns = slice(p * slice_width, (p + 1) * slice_width)
        dot += jnp.sum(base[:, columns] * gain_all[p][1:2], axis=-1, keepdims=True)
    dot = dot * (1.0 / width)
    base[...] = normed_grad
    for p in range(parts):
        columns = slice(p * slice_width, (p + 1) * slice_width)
        block = resid_ref[:, columns] * scale
        mid_grad = grad_ref[0, :, columns].astype(WIDE) + scale * (
            base[:, columns] * gain_all[p][1:2] - block * dot
        )
        base[:, columns] = mid_grad
        mid[:, columns] = mid_grad.astype(LOW)
    mid_grad_copy = pltpu.make_async_copy(base, mid_grad_out, home.at[1])
    mid_grad_copy.start()
    near.start(3, mid, mid_all.at[2], 2)
    near.start(4, mid, mid_all.at[1], 1)
    own = pltpu.make_async_copy(mid, mid_all.at[0], home.at[3])
    own.start()
    scatter.near(1, mid_turned, gate_low, 2)
    scatter.near(1, mid_turned, gate_low, 3)

    def down(k, put):
        for p in range(parts):
            columns = slice(p * slice_width, (p + 1) * slice_width)
            put(columns, dot_across(hidden[k], down_weight[p]))

    near.sent(1)
    near.sent(2)
    down(3, put_low(0))
    mid_grad_copy.wait()
    near.start(6, held.at[0], last.at[0], 1)
    down(2, put_sum)
    scatter.near(2, mid_turned, up_low, 0)
    near.wait(3)
    near.start(5, mid_all.at[2], mid_all.at[3], 1)
    near.wait(6)
    near.sent(6)
    held[0] = (base[...] + last[0].astype(WIDE)).astype(LOW)
    near.start(7, held.at[0], last.at[1], 2)
    down(1, put_low(1))
    near.start(8, held.at[1], last.at[2], 1)
    scatter.near(2, mid_turned, up_low, 1)
    down(0, put_sum)
    own.wait()
    near.wait(4)
    near.wait(5)
    for k in range(members):
        copy = pltpu.make_async_copy(mid_all.at[k], got.at[0], home.at[9])
        copy.start()
        copy.wait()
        if k:
            turned_copy.wait()
        for c in range(width // 256):
            block = slice(c * 256, (c + 1) * 256)
            column[block, :] = got[0, :, block].T
        turned_copy = pltpu.make_async_copy(
            column, mid_low_turned.at[:, pl.ds(k * rows, rows)], home.at[10]
        )
        turned_copy.start()
    turned_copy.wait()
    scatter.near(2, mid_turned, up_low, 2)
    scatter.near(2, mid_turned, up_low, 3)
    near.wait(8)
    near.wait(7)
    near.sent(3)
    near.sent(4)
    for p in range(parts):
        columns = slice(p * slice_width, (p + 1) * slice_width)
        value = base[:, columns] + last[2, :, columns].astype(WIDE)
        value = value + last[1, :, columns].astype(WIDE) + resid_ref[:, columns]
        start = (2 * (p % lines) + p // lines) * slice_width
        mid[:, start : start + slice_width] = value.astype(LOW)
    own = pltpu.make_async_copy(mid, hidden_out, home.at[3])
    own.start()
    own.wait()
    near.sent(5)
    near.sent(7)
    near.sent(8)
    for w in range(3):
        scatter.finish(w)


def feed_backward(
    grad, grad_turned, mid_turned, hidden, resid, gains, weights, pres, lines, members
):
    parts = 2 * lines
    rows, width = resid.shape
    columns = hidden.shape[2]
    slice_width = width // parts
    blocks = (members, rows)
    piece = (lines, slice_width, columns)
    later = [grad, mid_turned, resid, *weights]
    outs = [(piece, LOW)] * 3
    outs += [
        (blocks + (width,), LOW),
        ((rows, width), WIDE),
        ((rows, width), LOW),
        ((8, width), WIDE),
        ((width, rows * members), LOW),
    ]
    outs += [((lines + 1,) + piece[1:], LOW)] * 3
    tail = max(tail_rows(slice_width, lines), 16)
    outs += [((lines, tail, columns), LOW)] * 3
    return pl.pallas_call(
        functools.partial(feed_kernel, lines, members),
        out_shape=[jax.ShapeDtypeStruct(shape, dtype) for shape, dtype in outs],
        in_specs=[INSIDE] * 3 + [ANY] * 8,
        out_specs=[ANY] * 6 + [INSIDE] + [ANY] * 7,
        scratch_shapes=[
            pltpu.VMEM(blocks + (columns,), LOW),
            pltpu.VMEM(blocks + (columns,), LOW),
            pltpu.VMEM((rows, columns), WIDE),
            pltpu.VMEM((rows, columns), WIDE),
            pltpu.VMEM(piece, LOW),
            pltpu.VMEM(piece, LOW),
            pltpu.VMEM(piece, LOW),
            pltpu.VMEM(piece[1:], LOW),
            pltpu.VMEM((2, rows, width), LOW),
            pltpu.VMEM((3, rows, width), LOW),
            pltpu.VMEM((3, rows, width), LOW),
            pltpu.VMEM((rows, width), WIDE),
            pltpu.VMEM((rows, width), LOW),
            pltpu.SemaphoreType.DMA((3, lines)),
            pltpu.SemaphoreType.DMA((3, lines)),
            pltpu.SemaphoreType.DMA((3, lines)),
            pltpu.SemaphoreType.DMA((3, lines)),
            pltpu.SemaphoreType.DMA((3, lines)),
            pltpu.SemaphoreType.DMA((3, lines)),
            pltpu.SemaphoreType.DMA((9,)),
            pltpu.SemaphoreType.DMA((9,)),
            pltpu.SemaphoreType.DMA((11,)),
            pltpu.VMEM((width, rows), LOW),
        ]
        + [pltpu.VMEM(value.shape, value.dtype) for value in later]
        + [pltpu.VMEM((tail, columns), LOW)] * 3,
        compiler_params=pltpu.CompilerParams(
            collective_id=1, has_side_effects=True, vmem_limit_bytes=ROOM
        ),
        cost_estimate=pl.CostEstimate(flops=10**11, bytes_accessed=10**9, transcendentals=0),
        name="feed_backward",
    )(grad_turned, hidden, gains, *later, *pres)[:8]


def retention_kernel(lines, members, *refs):
    later = refs[:6]
    cos_ref, sin_ref, down_seg, along_seg, rate_ref = refs[6:11]
    hidden_ref, gain_all, gain_part = refs[11:14]
    mid_grad_ref, mid_all, retained_all, gate_all = refs[14:18]
    weights = refs[18:23]
    near_got, in_grad_out, gain_out = refs[23:28], refs[28], refs[29]
    far_got, tail_got = refs[30:35], refs[35:40]
    wide_one, wide_two, short_one, short_two = refs[40:44]
    gate_low, retained_low, query_low, key_low = refs[44:48]
    scatter_held = refs[48:53]
    spare_wide, spare_short, held, got, base, retained, gate = refs[53:60]
    pieces, piece_got, total, total_got = refs[60:64]
    sems = refs[64:70]
    near_send, near_recv, gain_send, gain_recv, home = refs[70:75]
    loaded, tails = refs[75:81], refs[81:]
    mixed, normed_turned, query, keys, values, turned = loaded
    value_low = mixed
    parts = 2 * lines
    rows, width = hidden_ref.shape
    slice_width = width // parts
    heads = rate_ref.shape[0]
    value_columns = values.shape[2]
    length = rows * members
    scatter = Scatter(
        lines,
        scatter_held,
        far_got,
        near_got,
        tail_got,
        {spare_wide.shape[1]: spare_wide, spare_short.shape[1]: spare_short},
        tails,
        sems + (home.at[0],),
    )
    near = Near(near_send, near_recv)
    me = lax.axis_index("dp")
    here = scatter.side * lines + scatter.line
    others = [{"dp": lax.rem(me + k, parts)} for k in range(1, parts)]
    greet(others + near.partners(members))

    def fetch(source, target, sem):
        copy = pltpu.make_async_copy(source, target, home.at[sem])
        copy.start()
        return copy

    loads = [fetch(later[k], loaded[k], 9 + k) for k in (5, 0)]
    out_copy = fetch(weights[0], wide_one, 1)
    loads += [fetch(later[k], loaded[k], 9 + k) for k in range(1, 5)]
    value_copy = fetch(weights[2], wide_two, 2)
    query_copy = fetch(weights[3], short_one, 3)
    key_copy = fetch(weights[4], short_two, 4)
    grad_copy = fetch(mid_grad_ref, in_grad_out, 7)
    loads[0].wait()
    loads[1].wait()
    scatter.far(0, turned, mixed)
    out_copy.wait()
    for load in loads[2:]:
        load.wait()

    column = lax.broadcasted_iota(jnp.int32, (rows, value_columns), 1)

    def by_head(parts_of):
        result = parts_of[0]
        for h in range(1, heads):
            result = jnp.where(column < h * VAL, result, parts_of[h])
        return result

    def inside(h):
        return (column >= h * VAL) & (column < (h + 1) * VAL)

    def head_mean(value):
        return by_head(
            [
                jnp.sum(jnp.where(inside(h), value, 0.0), axis=-1, keepdims=True) * (1.0 / VAL)
                for h in range(heads)
            ]
        )

    def unmix(k, carry):
        first = fetch(retained_all.at[k], retained, 5)
        second = fetch(gate_all.at[k], gate, 6)
        fetch(mid_all.at[k], held.at[0], 8).wait()
        grad = jnp.dot(
            held[0],
            wide_one[...].reshape(width, value_columns),
            preferred_element_type=WIDE,
        )
        first.wait()
        second.wait()
        value = retained[...]
        centred = value - head_mean(value)
        rate = lax.rsqrt(head_mean(centred * centred) + 1.0)
        pre = gate[...]
        sigma = 1.0 / (1.0 + jnp.exp(-pre))
        gate_low[k] = (
            grad * (centred * rate) * (sigma * (1.0 + pre * (1.0 - sigma)))
        ).astype(LOW)
        grouped_grad = grad * (pre * sigma)
        retained_low[k] = (
            rate * (grouped_grad - head_mean(grouped_grad))
            - (rate * rate * rate) * centred * head_mean(grouped_grad * centred)
        ).astype(LOW)
        return carry

    lax.fori_loop(0, members // 2, unmix, 0)
    scatter.near(0, turned, mixed, 0)
    lax.fori_loop(members // 2, members, unmix, 0)
    scatter.near(0, turned, mixed, 1)
    scatter.far(1, normed_turned, gate_low)
    gate_copy = fetch(weights[1], wide_one, 1)

    def decay(h, late, early, late_segment, early_segment, turn):
        sign = -1 if turn else 1
        distance = (
            sign
            * (
                lax.broadcasted_iota(jnp.int32, (rows, rows), 0)
                - lax.broadcasted_iota(jnp.int32, (rows, rows), 1)
            )
            + (late - early)
        )
        same = (distance >= 0) & (late_segment == early_segment)
        return jnp.where(
            same,
            jnp.exp(rate_ref[h : h + 1, :1] * jnp.maximum(distance, 0).astype(WIDE)),
            0.0,
        )

    def start_of(k):
        return pl.multiple_of(near.member(k) * rows, rows)

    wing = KEY // 2
    along = [along_seg[:, pl.ds(start_of(k), rows)] for k in range(members)]

    def turn_back(target, k, h, grad, scale):
        at = pl.ds(pl.multiple_of(k * rows, rows), rows)
        cosine, sine = cos_ref[at, :], sin_ref[at, :]
        first, second = grad[:, :wing], grad[:, wing:]
        target[k, :, h * KEY : h * KEY + wing] = (
            (first * cosine + second * sine) * scale
        ).astype(LOW)
        target[k, :, h * KEY + wing : (h + 1) * KEY] = (
            (second * cosine - first * sine) * scale
        ).astype(LOW)

    def early_side(m, carry):
        early = start_of(m)
        early_segment = down_seg[pl.ds(early, rows), :]
        value_grads = []
        for h in range(heads):
            head = slice(h * KEY, (h + 1) * KEY)
            masked = jnp.where(inside(h), values[m].astype(WIDE), 0.0).astype(LOW)
            value_grad = jnp.zeros((rows, value_columns), WIDE)
            key_grad = jnp.zeros((rows, KEY), WIDE)
            for n in range(members):
                late = start_of(n)
                late_segment = along[n]
                mask = decay(h, late, early, late_segment, early_segment, True)
                score = (dot_across(keys[m, :, head], query[n, :, head]) * mask).astype(LOW)
                raw = (dot_across(masked, retained_low[n]) * mask).astype(LOW)
                value_grad += jnp.dot(score, retained_low[n], preferred_element_type=WIDE)
                key_grad += jnp.dot(raw, query[n, :, head], preferred_element_type=WIDE)
            value_grads.append(value_grad)
            turn_back(key_low, m, h, key_grad, 1.0)
        value_low[m] = by_head(value_grads).astype(LOW)
        return carry

    scatter.near(0, turned, mixed, 2)
    scatter.near(0, turned, mixed, 3)
    early_side(0, 0)
    early_side(1, 0)
    scatter.near(1, normed_turned, gate_low, 0)
    early_side(2, 0)
    early_side(3, 0)
    scatter.far(2, normed_turned, value_low)
    scatter.near(1, normed_turned, gate_low, 1)
    scatter.near(1, normed_turned, gate_low, 2)
    scatter.far(4, normed_turned, key_low)
    scatter.near(1, normed_turned, gate_low, 3)

    def late_side(n, carry):
        late = start_of(n)
        late_segment = down_seg[pl.ds(late, rows), :]
        for h in range(heads):
            head = slice(h * KEY, (h + 1) * KEY)
            masked = jnp.where(inside(h), retained_low[n].astype(WIDE), 0.0).astype(LOW)
            query_grad = jnp.zeros((rows, KEY), WIDE)
            for m in range(members):
                early = start_of(m)
                early_segment = along[m]
                mask = decay(h, late, early, late_segment, early_segment, False)
                raw = (dot_across(masked, values[m]) * mask).astype(LOW)
                query_grad += jnp.dot(raw, keys[m, :, head], preferred_element_type=WIDE)
            turn_back(query_low, n, h, query_grad, KEY ** (-0.5))
        return carry

    lax.fori_loop(0, members // 2, late_side, 0)
    scatter.near(2, normed_turned, value_low, 0)
    lax.fori_loop(members // 2, members, late_side, 0)
    scatter.near(2, normed_turned, value_low, 1)
    scatter.far(3, normed_turned, query_low)
    for copy in (gate_copy, value_copy, query_copy, key_copy, grad_copy):
        copy.wait()

    def back(k, put):
        for p in range(parts):
            columns = slice(p * slice_width, (p + 1) * slice_width)
            put(
                columns,
                dot_across(gate_low[k], wide_one[p])
                + dot_across(value_low[k], wide_two[p])
                + dot_across(query_low[k], short_one[p])
                + dot_across(key_low[k], short_two[p]),
            )

    def put_low(slot):
        def put(columns, value):
            held[slot, :, columns] = value.astype(LOW)

        return put

    def put_sum(columns, value):
        base[:, columns] = value

    back(3, put_low(0))
    near.start(0, held.at[0], got.at[0], 1)
    back(2, put_sum)
    scatter.near(2, normed_turned, value_low, 2)
    near.wait(0)
    near.sent(0)
    held[0] = (base[...] + got[0].astype(WIDE)).astype(LOW)
    near.start(1, held.at[0], got.at[1], 2)
    back(1, put_low(1))
    near.start(2, held.at[1], got.at[2], 1)
    scatter.near(2, normed_turned, value_low, 3)
    back(0, put_sum)
    for quarter in range(4):
        scatter.near(4, normed_turned, key_low, quarter)
    near.wait(2)
    base[...] += got[2].astype(WIDE)
    near.wait(1)
    normed_grad = base[...] + got[1].astype(WIDE)
    base[...] = normed_grad
    resid = hidden_ref[...].astype(WIDE)
    scale = lax.rsqrt(jnp.mean(resid * resid, axis=-1, keepdims=True) + 1e-06)
    dot = jnp.zeros((rows, 1), WIDE)
    for p in range(parts):
        columns = slice(p * slice_width, (p + 1) * slice_width)
        product = base[:, columns] * (hidden_ref[:, columns].astype(WIDE) * scale)
        row = lax.broadcasted_iota(jnp.int32, (8, slice_width), 0)
        pieces[p] = jnp.where(
            row == 0, jnp.sum(product, axis=0, keepdims=True), gain_part[:, columns]
        )
        dot += jnp.sum(product * gain_all[p][0:1], axis=-1, keepdims=True)
    dot = dot * (1.0 / width)
    gains = []
    for k in range(1, parts):
        other = lax.rem(me + k, parts)
        place = lax.rem(other, 2) * lines + other // 2
        copy = remote(
            pieces.at[place], piece_got.at[k], gain_send.at[k], gain_recv.at[k], others[k - 1]
        )
        copy.start()
        gains.append(copy)
    for p in range(parts):
        columns = slice(p * slice_width, (p + 1) * slice_width)
        block = hidden_ref[:, columns].astype(WIDE) * scale
        base[:, columns] = in_grad_out[:, columns] + scale * (
            base[:, columns] * gain_all[p][0:1] - block * dot
        )
    for p in range(parts):
        start = (2 * (p % lines) + p // lines) * slice_width
        in_grad_out[:, start : start + slice_width] = base[
            :, p * slice_width : (p + 1) * slice_width
        ]
    value = pieces[here]
    for k in range(1, parts):
        gains[k - 1].wait_recv()
        value = value + piece_got[k]
    total[...] = value
    for k in range(1, members):
        near.start(2 + k, total, total_got.at[k], k)
    for quarter in range(4):
        scatter.near(3, normed_turned, query_low, quarter)
    for w in (0, 1, 2, 4, 3):
        scatter.finish(w)
    for k in range(1, members):
        near.wait(2 + k)
        value = value + total_got[k]
    gain_out[...] = value
    for tag in range(1, 2 + members):
        near.sent(tag)
    for copy in gains:
        copy.wait_send()


def retention_backward(inside, streamed, weights, lines, members, slice_width):
    parts = 2 * lines
    rows, width = inside[11].shape
    blocks = (members, rows)
    wide, short = weights[0].shape[2], weights[3].shape[2]
    widths = [wide, wide, wide, short, short]
    pieces = [(lines, slice_width, columns) for columns in widths]
    outs = [(piece, LOW) for piece in pieces]
    outs += [((rows, width), WIDE), ((8, slice_width), WIDE)]
    outs += [((lines + 1,) + piece[1:], LOW) for piece in pieces]
    tail = max(tail_rows(slice_width, lines), 16)
    outs += [((lines, tail, columns), LOW) for columns in widths]
    return pl.pallas_call(
        functools.partial(retention_kernel, lines, members),
        out_shape=[jax.ShapeDtypeStruct(shape, dtype) for shape, dtype in outs],
        in_specs=[ANY] * 6 + [INSIDE] * 8 + [ANY] * 9,
        out_specs=[ANY] * 5 + [INSIDE] * 2 + [ANY] * 10,
        scratch_shapes=[
            pltpu.VMEM(weights[0].shape, LOW),
            pltpu.VMEM(weights[0].shape, LOW),
            pltpu.VMEM(weights[3].shape, LOW),
            pltpu.VMEM(weights[3].shape, LOW),
            pltpu.VMEM(blocks + (wide,), LOW),
            pltpu.VMEM(blocks + (wide,), LOW),
            pltpu.VMEM(blocks + (short,), LOW),
            pltpu.VMEM(blocks + (short,), LOW),
        ]
        + [pltpu.VMEM(piece, LOW) for piece in pieces]
        + [
            pltpu.VMEM((slice_width, wide), LOW),
            pltpu.VMEM((slice_width, short), LOW),
            pltpu.VMEM((2, rows, width), LOW),
            pltpu.VMEM((3, rows, width), LOW),
            pltpu.VMEM((rows, width), WIDE),
            pltpu.VMEM((rows, wide), WIDE),
            pltpu.VMEM((rows, wide), WIDE),
            pltpu.VMEM((parts, 8, slice_width), WIDE),
            pltpu.VMEM((parts, 8, slice_width), WIDE),
            pltpu.VMEM((8, slice_width), WIDE),
            pltpu.VMEM((members, 8, slice_width), WIDE),
            pltpu.SemaphoreType.DMA((5, lines)),
            pltpu.SemaphoreType.DMA((5, lines)),
            pltpu.SemaphoreType.DMA((5, lines)),
            pltpu.SemaphoreType.DMA((5, lines)),
            pltpu.SemaphoreType.DMA((5, lines)),
            pltpu.SemaphoreType.DMA((5, lines)),
            pltpu.SemaphoreType.DMA((6,)),
            pltpu.SemaphoreType.DMA((6,)),
            pltpu.SemaphoreType.DMA((parts,)),
            pltpu.SemaphoreType.DMA((parts,)),
            pltpu.SemaphoreType.DMA((15,)),
        ]
        + [pltpu.VMEM(value.shape, value.dtype) for value in inside[:6]]
        + [pltpu.VMEM((tail, columns), LOW) for columns in widths],
        compiler_params=pltpu.CompilerParams(
            collective_id=2, has_side_effects=True, vmem_limit_bytes=ROOM
        ),
        cost_estimate=pl.CostEstimate(flops=10**11, bytes_accessed=10**9, transcendentals=0),
        name="retention_backward",
    )(*inside, *streamed, *weights)[:7]


def on_device(
    hidden_in,
    out_grad,
    segment_ids,
    norm1_gain,
    w_query,
    w_key,
    w_value,
    w_gate,
    w_out,
    norm2_gain,
    w_mlp_gate,
    w_mlp_up,
    w_mlp_down,
):
    _, rows, width = hidden_in.shape
    parts = lax.axis_size("dp")
    lines = parts // 2
    slice_width = width // parts
    own = lax.axis_index("tensor")
    members = lax.axis_size("tensor")
    order = list(range(0, parts, 2)) + list(range(1, parts, 2))

    def to_places(value):
        blocks = [value[:, k * slice_width : (k + 1) * slice_width] for k in order]
        return jnp.concatenate(blocks, axis=1)

    heads_here = w_query.shape[1] // KEY
    resid_low = to_places(hidden_in.reshape(rows, width))
    grad_local = to_places(out_grad.reshape(rows, width))
    gain_rows = jnp.stack([norm1_gain, norm2_gain])
    position = jnp.concatenate(
        [(own ^ k) * rows + jnp.arange(rows, dtype=jnp.int32) for k in range(members)]
    )
    cosine, sine = rotary_tables(position, KEY)
    head_numbers = (jnp.arange(heads_here, dtype=jnp.int32) + own * heads_here).astype(WIDE)
    rates = jnp.log1p(-jnp.exp2(-5.0 - head_numbers))
    rates = jnp.broadcast_to(rates[:, None], (heads_here, 128))
    outs = forward(
        resid_low,
        grad_local,
        gain_rows,
        cosine,
        sine,
        segment_ids,
        rates,
        [w_query, w_key, w_value.T, w_gate.T, w_out, w_mlp_gate.T, w_mlp_up.T, w_mlp_down],
        lines,
        members,
    )
    normed_turned, grad_full, gains = outs[:3]
    query_weight, key_weight, value_weight, gate_weight, out_weight = outs[3:8]
    query, keys, values, gate_pre, grad_turned = outs[11:16]
    retained, mixed, resid_mid, mid_turned, gate_hidden, up_hidden, hidden = outs[16:]
    feed_outs = feed_backward(
        grad_full,
        grad_turned,
        mid_turned,
        hidden,
        resid_mid,
        gains,
        outs[8:11],
        (gate_hidden, up_hidden),
        lines,
        members,
    )
    down_grad, mlp_gate_grad, mlp_up_grad, mid_all, mid_grad = feed_outs[:5]
    hidden_out, gain_part, mid_low_turned = feed_outs[5:]
    out_weight_grad, gate_grad, value_grad, query_grad, key_grad, in_grad, gain_total = (
        retention_backward(
            [
                mixed,
                normed_turned,
                query,
                keys,
                values,
                mid_low_turned,
                cosine,
                sine,
                segment_ids.T,
                segment_ids,
                rates,
                resid_low,
                gains,
                gain_part,
            ],
            [mid_grad, mid_all, retained, gate_pre],
            [out_weight, gate_weight, value_weight, query_weight, key_weight],
            lines,
            members,
            slice_width,
        )
    )
    def add_up(pieces):
        total = pieces[0].astype(WIDE)
        for k in range(1, pieces.shape[0]):
            total = total + pieces[k].astype(WIDE)
        return total

    return (
        hidden_out.reshape(hidden_in.shape),
        in_grad.reshape(hidden_in.shape),
        gain_total[0],
        add_up(query_grad),
        add_up(key_grad),
        add_up(value_grad),
        add_up(gate_grad),
        add_up(out_weight_grad).T,
        gain_total[1],
        add_up(mlp_gate_grad),
        add_up(mlp_up_grad),
        add_up(down_grad).T,
    )


def solution(mesh):
    return jax.shard_map(
        on_device,
        mesh=mesh,
        in_specs=(
            P("dp", "tensor", None),
            P("dp", "tensor", None),
            P("dp", None),
            P("dp"),
            P("dp", "tensor"),
            P("dp", "tensor"),
            P("dp", "tensor"),
            P("dp", "tensor"),
            P("tensor", "dp"),
            P("dp"),
            P("dp", "tensor"),
            P("dp", "tensor"),
            P("tensor", "dp"),
        ),
        out_specs=(
            P("dp", "tensor", None),
            P("dp", "tensor", None),
            P("dp"),
            P("dp", "tensor"),
            P("dp", "tensor"),
            P("dp", "tensor"),
            P("dp", "tensor"),
            P("tensor", "dp"),
            P("dp"),
            P("dp", "tensor"),
            P("dp", "tensor"),
            P("tensor", "dp"),
        ),
        check_vma=False,
    )
```

```python
import functools
import math

import jax
import jax.numpy as jnp
from jax import lax
from jax.experimental import pallas as pl
from jax.experimental.pallas import tpu as pltpu
from jax.sharding import PartitionSpec as P

KEY = 256
VAL = 432
LOW = jnp.bfloat16
WIDE = jnp.float32
WEIGHTS = 8
MESH = pl.DeviceIdType.MESH
ANY = pl.BlockSpec(memory_space=pl.ANY)
INSIDE = pl.BlockSpec(memory_space=pltpu.VMEM)
ROOM = 60 * 1024 * 1024

def rotary_tables(position, width):
    half = width // 2
    frequency = 10000.0 ** (-2.0 * jnp.arange(half, dtype=jnp.int32).astype(WIDE) / width)
    angle = position.astype(WIDE)[:, None] * frequency[None, :]
    return (jnp.cos(angle), jnp.sin(angle))


def greet(peers):
    barrier = pltpu.get_barrier_semaphore()
    for peer in peers:
        pl.semaphore_signal(barrier, inc=1, device_id=peer, device_id_type=MESH)
    pl.semaphore_wait(barrier, len(peers))


def remote(source, target, send, recv, device):
    return pltpu.make_async_remote_copy(
        src_ref=source,
        dst_ref=target,
        send_sem=send,
        recv_sem=recv,
        device_id=device,
        device_id_type=MESH,
    )


def forward_kernel(lines, members, *refs):
    hidden_ref, grad_ref, gain_ref, cos_ref, sin_ref, down_seg, along_seg, rate_ref = refs[:8]
    shards = refs[8:16]
    normed_turned, grad_all, gain_all = refs[16:19]
    wholes = refs[19:27]
    query_out, keys_out, values_out, gate_out, grad_turned = refs[27:32]
    retained_out, mixed_out, resid_out, mid_turned, gate_hidden_out, up_hidden_out = refs[32:38]
    hidden_out = refs[38]
    normed, mid, short, wide_one, wide_two, turned = refs[39:45]
    query, keys, scores, values, retained, gate, mixed, hidden = refs[45:53]
    held, got, base = refs[53:56]
    line_send, line_recv, side_send, side_recv = refs[56:60]
    near_send, near_recv, gain_send, gain_recv, home, tail_send, tail_recv, gain_rows, raw, flip = refs[60:]

    parts = 2 * lines
    rows, width = hidden_ref.shape
    slice_width = gain_rows.shape[1]
    heads = rate_ref.shape[0]
    value_columns = values.shape[2]
    me = lax.axis_index("dp")
    line, side = me // 2, lax.rem(me, 2)
    here = side * lines + line
    own = lax.axis_index("tensor")
    half, rest = own // 2, lax.rem(own, 2)

    def member(k):
        return 2 * lax.rem(half + k // 2, 2) + lax.rem(rest + lax.rem(k, 2), 2)

    partners = [None] + [{"tensor": member(k)} for k in range(1, members)]
    others = [{"dp": lax.rem(me + k, parts)} for k in range(1, parts)]
    opposite = {"dp": 2 * line + (1 - side)}
    greet(others + partners[1:])

    local = {}
    slots = iter(range(32))

    def keep(source, target):
        slot = next(slots)
        local[slot] = pltpu.make_async_copy(source, target, home.at[slot])
        local[slot].start()
        return slot

    def finish(slot):
        local.pop(slot).wait()

    near = {}

    def near_start(tag, source, target, k):
        copy = remote(source, target, near_send.at[tag], near_recv.at[tag], partners[k])
        copy.start()
        near[tag] = copy

    across = {}
    ours = {}

    inner = lines == 4

    def line_copy(w, step):
        return remote(
            source(w),
            wholes[w].at[here],
            line_send.at[w, step],
            line_recv.at[w, step],
            {"dp": 2 * lax.rem(line + step, lines) + side},
        )

    def relay_copy(w):
        place = side * lines + 3 * (2 - line)
        return remote(
            wholes[w].at[place],
            wholes[w].at[place],
            line_send.at[w, 0],
            line_recv.at[w, 2 * line - 1],
            {"dp": 6 * (line - 1) + side},
        )

    tail = slice_width // 8 // 16 * 16
    most = slice_width - tail

    def side_copy(w, step):
        place = side * lines + lax.rem(line + lines - step, lines)
        return remote(
            wholes[w].at[place, pl.ds(0, most)],
            wholes[w].at[place, pl.ds(0, most)],
            side_send.at[w, step],
            side_recv.at[w, step],
            opposite,
        )

    there = (1 - side) * lines + line

    def tail_copy(w, step):
        return remote(
            wholes[w].at[there, pl.ds(most, tail)],
            wholes[w].at[there, pl.ds(most, tail)],
            tail_send.at[w, step],
            tail_recv.at[w, step],
            {"dp": 2 * lax.rem(line + step, lines) + side},
        )

    def on_line(w, step, act):
        if inner and step != 2:

            @pl.when(line != (3 if step == 1 else 0))
            def _():
                act(line_copy(w, step))
        else:
            act(line_copy(w, step))

    sends = [2, 1, 3] if inner else list(range(1, lines))

    def prepare(w):
        if w < 2:
            ours[w] = keep(shards[w], wholes[w].at[here])
            return
        copy = pltpu.make_async_copy(shards[w], raw, home.at[home.shape[0] - 1])
        copy.start()
        copy.wait()
        columns = raw.shape[0]
        for at in range(0, columns, 128):
            block = slice(at, min(at + 128, columns))
            flip[:, block] = raw[block, :].T
        copy = pltpu.make_async_copy(flip, wholes[w].at[here], home.at[home.shape[0] - 1])
        copy.start()
        copy.wait()

    def source(w):
        return shards[w] if w < 2 else wholes[w].at[here]

    def start_lines(w):
        prepare(w)
        for step in sends:
            on_line(w, step, lambda copy: copy.start())
        across[w, 0] = remote(
            source(w), wholes[w].at[here], side_send.at[w, 0], side_recv.at[w, 0], opposite
        )
        across[w, 0].start()

    def pass_on(w, third):
        for at in range(third * (lines - 1) // 3, (third + 1) * (lines - 1) // 3):
            step = at + 1
            if inner:
                late = 3 - 2 * ((3 - line) // 3)
                step = [2, 4 - late, late][at]
            if tail and at == 0:
                across[w, 0].wait_recv()
                for hop in range(1, lines):
                    tail_copy(w, hop).start()
            line_copy(w, step).wait_recv()
            if inner and at == 0:

                @pl.when((line == 1) | (line == 2))
                def _():
                    relay_copy(w).start()

            side_copy(w, step).start()

    def complete(w):
        if not tail:
            across[w, 0].wait_recv()
        for step in range(1, lines):
            side_copy(w, step).wait_recv()
            if tail:
                tail_copy(w, step).wait_recv()
        if w in ours:
            finish(ours[w])

    def load(w, target, sem):
        copy = pltpu.make_async_copy(wholes[w], target, sem)
        copy.start()
        copy.wait()

    def stage(w, target, body):
        if w + 1 < WEIGHTS:
            for third in range(3):
                pass_on(w + 1, third)
        if w + 3 < WEIGHTS:
            start_lines(w + 3)
        complete(w)
        load(w, target, home.at[home.shape[0] - 1 - w])
        lax.fori_loop(0, members, body, 0)

    gain_rows[...] = jnp.where(
        lax.broadcasted_iota(jnp.int32, gain_rows.shape, 0) == 0,
        gain_ref[0:1, :].astype(WIDE),
        gain_ref[1:2, :].astype(WIDE),
    )
    gains = []
    for k in range(1, parts):
        copy = remote(
            gain_rows, gain_all.at[here], gain_send.at[k], gain_recv.at[k], others[k - 1]
        )
        copy.start()
        gains.append(copy)
    gain_all[here] = gain_rows[...]
    for w in range(3):
        start_lines(w)

    def scale_into(target, scaled, which):
        for p in range(parts):
            columns = slice(p * slice_width, (p + 1) * slice_width)
            target[0, :, columns] = (
                scaled[:, columns] * gain_all[p][which : which + 1]
            ).astype(LOW)

    resid = hidden_ref[...].astype(WIDE)
    scaled = resid * lax.rsqrt(jnp.mean(resid * resid, axis=-1, keepdims=True) + 1e-06)
    for copy in gains:
        copy.wait_recv()
    scale_into(normed, scaled, 0)
    for k in range(1, members):
        near_start(k - 1, normed.at[0], normed.at[k], k)
    for k in range(1, members):
        near_start(2 + k, grad_ref, mid.at[k], k)
    grad_kept = keep(grad_ref, mid.at[0])
    for third in range(3):
        pass_on(0, third)
    for k in range(1, members):
        near[k - 1].wait_recv()

    def turn_over(source):
        tile = 256

        def body(k, carry):
            at = pl.ds(pl.multiple_of(k * rows, rows), rows)
            for c in range(width // tile):
                columns = slice(c * tile, (c + 1) * tile)
                turned[columns, at] = source[k, :, columns].T
            return carry

        lax.fori_loop(0, members, body, 0)

    turn_over(normed)
    turned_kept = keep(turned, normed_turned)

    def flat(ref):
        return ref[...].reshape(width, ref.shape[2])

    def turn(source, target, scale):
        def body(k, carry):
            pre = jnp.dot(normed[k], flat(source), preferred_element_type=WIDE)
            at = pl.ds(pl.multiple_of(k * rows, rows), rows)
            cosine, sine = cos_ref[at, :], sin_ref[at, :]
            wing = KEY // 2
            for h in range(heads):
                first = pre[:, h * KEY : h * KEY + wing]
                second = pre[:, h * KEY + wing : (h + 1) * KEY]
                target[k, :, h * KEY : h * KEY + wing] = (
                    (first * cosine - second * sine) * scale
                ).astype(LOW)
                target[k, :, h * KEY + wing : (h + 1) * KEY] = (
                    (second * cosine + first * sine) * scale
                ).astype(LOW)
            return carry

        return body

    stage(0, short, turn(short, query, KEY ** (-0.5)))
    keep(query, query_out)
    stage(1, short, turn(short, keys, 1.0))
    keep(keys, keys_out)

    def score(k, carry):
        place = member(k)
        at = pl.multiple_of(place * rows, rows)
        segment = down_seg[pl.ds(at, rows), :]
        for h in range(heads):
            head = slice(h * KEY, (h + 1) * KEY)
            for m in range(members):
                start = pl.multiple_of(member(m) * rows, rows)
                raw = lax.dot_general(
                    query[k, :, head],
                    keys[m, :, head],
                    (((1,), (1,)), ((), ())),
                    preferred_element_type=WIDE,
                )
                distance = (
                    lax.broadcasted_iota(jnp.int32, (rows, rows), 0)
                    - lax.broadcasted_iota(jnp.int32, (rows, rows), 1)
                    + (at - start)
                )
                same = (distance >= 0) & (segment == along_seg[:, pl.ds(start, rows)])
                decay = jnp.exp(
                    rate_ref[h : h + 1, :1] * jnp.maximum(distance, 0).astype(WIDE)
                )
                scores[h, k, :, m * rows : (m + 1) * rows] = (
                    raw * jnp.where(same, decay, 0.0)
                ).astype(LOW)
        return carry

    lax.fori_loop(0, members, score, 0)
    finish(grad_kept)
    for k in range(1, members):
        near[2 + k].wait_recv()
    finish(turned_kept)
    turn_over(mid)
    turned_kept = keep(turned, grad_turned)
    grad_kept = keep(mid, grad_all)

    column = lax.broadcasted_iota(jnp.int32, (rows, value_columns), 1)

    def by_head(parts_of):
        result = parts_of[0]
        for h in range(1, heads):
            result = jnp.where(column < h * VAL, result, parts_of[h])
        return result

    def head_mean(value):
        means = []
        for h in range(heads):
            inside = (column >= h * VAL) & (column < (h + 1) * VAL)
            total = jnp.sum(jnp.where(inside, value, 0.0), axis=-1, keepdims=True)
            means.append(total * (1.0 / VAL))
        return by_head(means)

    def make_values(k, carry):
        values[k] = jnp.dot(normed[k], flat(wide_one), preferred_element_type=WIDE).astype(LOW)
        return carry

    stage(2, wide_one, make_values)
    keep(values, values_out)

    def retain(k, carry):
        every = values[...].reshape(members * rows, value_columns)
        retained[k] = by_head(
            [
                jnp.dot(scores[h, k], every, preferred_element_type=WIDE)
                for h in range(heads)
            ]
        )
        return carry

    lax.fori_loop(0, members, retain, 0)
    retained_kept = keep(retained, retained_out)

    def make_mixed(k, carry):
        pre = jnp.dot(normed[k], flat(wide_two), preferred_element_type=WIDE)
        gate[k] = pre
        value = retained[k]
        centred = value - head_mean(value)
        grouped = centred * lax.rsqrt(head_mean(centred * centred) + 1.0)
        mixed[k] = (grouped * (pre / (1.0 + jnp.exp(-pre)))).astype(LOW)
        return carry

    stage(3, wide_two, make_mixed)
    gate_kept = keep(gate, gate_out)
    keep(mixed, mixed_out)

    def project(k, put):
        for p in range(parts):
            columns = slice(p * slice_width, (p + 1) * slice_width)
            put(
                columns,
                lax.dot_general(
                    mixed[k],
                    wide_one[p],
                    (((1,), (1,)), ((), ())),
                    preferred_element_type=WIDE,
                ),
            )

    def put_low(slot):
        def put(columns, value):
            held[slot, :, columns] = value.astype(LOW)

        return put

    def put_sum(columns, value):
        base[:, columns] = value

    pass_on(5, 0)
    complete(4)
    load(4, wide_one, home.at[home.shape[0] - 5])
    finish(grad_kept)
    project(3, put_low(0))
    near_start(6, held.at[0], got.at[0], 1)
    project(2, put_sum)
    pass_on(5, 1)
    near[6].wait_recv()
    held[1] = (base[...] + got[0].astype(WIDE)).astype(LOW)
    near_start(8, held.at[1], got.at[1], 2)
    project(1, put_low(2))
    near_start(7, held.at[2], got.at[2], 1)
    project(0, put_sum)
    pass_on(5, 2)
    start_lines(7)
    near[7].wait_recv()
    base[...] = base[...] + got[2].astype(WIDE) + hidden_ref[...].astype(WIDE)
    pass_on(6, 0)
    near[8].wait_recv()
    resid = base[...] + got[1].astype(WIDE)
    resid_out[...] = resid
    scaled = resid * lax.rsqrt(jnp.mean(resid * resid, axis=-1, keepdims=True) + 1e-06)
    scale_into(mid, scaled, 1)
    near_start(10, mid.at[0], mid.at[2], 2)
    near_start(9, mid.at[0], mid.at[1], 1)
    pass_on(6, 1)
    pass_on(6, 2)
    near[10].wait_recv()
    near_start(11, mid.at[2], mid.at[3], 1)
    complete(5)
    load(5, wide_two, home.at[home.shape[0] - 6])
    near[9].wait_recv()
    near[11].wait_recv()
    finish(retained_kept)
    finish(gate_kept)

    def make_gate(k, carry):
        gate[k] = jnp.dot(mid[k], flat(wide_two), preferred_element_type=WIDE)
        return carry

    lax.fori_loop(0, members, make_gate, 0)
    keep(gate, gate_hidden_out)
    finish(turned_kept)
    turn_over(mid)
    keep(turned, mid_turned)
    pass_on(7, 0)
    pass_on(7, 1)
    pass_on(7, 2)
    complete(6)
    load(6, wide_one, home.at[home.shape[0] - 7])

    def make_hidden(k, carry):
        up = jnp.dot(mid[k], flat(wide_one), preferred_element_type=WIDE)
        retained[k] = up
        pre = gate[k]
        inner = (2.0 / math.pi) ** 0.5 * (pre + 0.044715 * (pre * pre * pre))
        hidden[k] = (0.5 * pre * (1.0 + jnp.tanh(inner)) * up).astype(LOW)
        return carry

    lax.fori_loop(0, members, make_hidden, 0)
    keep(retained, up_hidden_out)
    keep(hidden, hidden_out)
    complete(7)
    for w in range(WEIGHTS):
        for step in sends:
            on_line(w, step, lambda copy: copy.wait_send())
            side_copy(w, step).wait_send()
            if tail:
                tail_copy(w, step).wait_send()
        across[w, 0].wait_send()
        if inner:

            @pl.when((line == 1) | (line == 2))
            def _():
                relay_copy(w).wait_send()

    for copy in gains:
        copy.wait_send()
    for copy in near.values():
        copy.wait_send()
    for slot in list(local):
        finish(slot)


def forward(hidden, grad, gains, cosine, sine, segments, rates, shards, lines, members):
    parts = 2 * lines
    rows, width = hidden.shape
    heads = rates.shape[0]
    key_columns, value_columns = shards[0].shape[1], shards[2].shape[0]
    chunks = [shard.shape if k < 2 else shard.shape[::-1] for k, shard in enumerate(shards)]
    length = rows * members
    blocks = (members, rows)
    turned = (width, length)
    outs = [
        (turned, LOW),
        (blocks + (width,), LOW),
        ((parts, 8, gains.shape[1]), WIDE),
    ]
    outs += [((parts,) + chunk, LOW) for chunk in chunks]
    outs += [
        (blocks + (key_columns,), LOW),
        (blocks + (key_columns,), LOW),
        (blocks + (value_columns,), LOW),
        (blocks + (value_columns,), WIDE),
        (turned, LOW),
        (blocks + (value_columns,), WIDE),
        (blocks + (value_columns,), LOW),
        ((rows, width), WIDE),
        (turned, LOW),
        (blocks + (value_columns,), WIDE),
        (blocks + (value_columns,), WIDE),
        (blocks + (value_columns,), LOW),
    ]
    places = [ANY] * len(outs)
    places[2] = INSIDE
    places[18] = INSIDE
    tags = 12
    return pl.pallas_call(
        functools.partial(forward_kernel, lines, members),
        out_shape=[jax.ShapeDtypeStruct(shape, dtype) for shape, dtype in outs],
        in_specs=[INSIDE, ANY] + [INSIDE] * 6 + [ANY] * WEIGHTS,
        out_specs=places,
        scratch_shapes=[
            pltpu.VMEM(blocks + (width,), LOW),
            pltpu.VMEM(blocks + (width,), LOW),
            pltpu.VMEM((parts,) + chunks[0], LOW),
            pltpu.VMEM((parts,) + chunks[2], LOW),
            pltpu.VMEM((parts,) + chunks[2], LOW),
            pltpu.VMEM(turned, LOW),
            pltpu.VMEM(blocks + (key_columns,), LOW),
            pltpu.VMEM(blocks + (key_columns,), LOW),
            pltpu.VMEM((heads, members, rows, length), LOW),
            pltpu.VMEM(blocks + (value_columns,), LOW),
            pltpu.VMEM(blocks + (value_columns,), WIDE),
            pltpu.VMEM(blocks + (value_columns,), WIDE),
            pltpu.VMEM(blocks + (value_columns,), LOW),
            pltpu.VMEM(blocks + (value_columns,), LOW),
            pltpu.VMEM((3, rows, width), LOW),
            pltpu.VMEM((3, rows, width), LOW),
            pltpu.VMEM((rows, width), WIDE),
            pltpu.SemaphoreType.DMA((WEIGHTS, lines)),
            pltpu.SemaphoreType.DMA((WEIGHTS, lines)),
            pltpu.SemaphoreType.DMA((WEIGHTS, lines)),
            pltpu.SemaphoreType.DMA((WEIGHTS, lines)),
            pltpu.SemaphoreType.DMA((tags,)),
            pltpu.SemaphoreType.DMA((tags,)),
            pltpu.SemaphoreType.DMA((parts,)),
            pltpu.SemaphoreType.DMA((parts,)),
            pltpu.SemaphoreType.DMA((40,)),
            pltpu.SemaphoreType.DMA((WEIGHTS, lines)),
            pltpu.SemaphoreType.DMA((WEIGHTS, lines)),
            pltpu.VMEM((8, gains.shape[1]), WIDE),
            pltpu.VMEM(shards[2].shape, LOW),
            pltpu.VMEM(shards[2].shape[::-1], LOW),
        ],
        compiler_params=pltpu.CompilerParams(
            collective_id=0, has_side_effects=True, vmem_limit_bytes=ROOM
        ),
        cost_estimate=pl.CostEstimate(
            flops=10**11, bytes_accessed=10**9, transcendentals=0
        ),
        name="forward",
    )(hidden, grad, gains, cosine, sine, segments.T, segments, rates, *shards)


def tail_rows(rows, lines, sixteenths):
    return rows * sixteenths // 16 // 16 * 16 if lines == 4 else 0


class Scatter:
    def __init__(self, lines, held, far_got, near_got, tail_got, spare, tails, sixteenths, sems):
        self.lines = lines
        self.held, self.far_got, self.near_got, self.spare = held, far_got, near_got, spare
        self.tail_got, self.tails = tail_got, tails
        self.side_send, self.side_recv, self.line_send, self.line_recv = sems[:4]
        self.tail_send, self.tail_recv, self.home = sems[4:]
        self.rows = held[0].shape[1]
        self.tail = tail_rows(self.rows, lines, sixteenths)
        self.most = self.rows - self.tail
        me = lax.axis_index("dp")
        self.line, self.side = me // 2, lax.rem(me, 2)
        self.opposite = {"dp": 2 * self.line + (1 - self.side)}

    def peer(self, step):
        return {"dp": 2 * lax.rem(self.line + step, self.lines) + self.side}

    def peers(self):
        return [self.opposite] + [self.peer(step) for step in range(1, self.lines)]

    def far_copy(self, w, place):
        return remote(
            self.held[w].at[place, pl.ds(0, self.most)],
            self.far_got[w].at[place, pl.ds(0, self.most)],
            self.side_send.at[w, place],
            self.side_recv.at[w, place],
            self.opposite,
        )

    def near_copy(self, w, step):
        place = lax.rem(self.line + step, self.lines)
        return remote(
            self.held[w].at[place],
            self.near_got[w].at[step],
            self.line_send.at[w, step],
            self.line_recv.at[w, step],
            self.peer(step),
        )

    def fetch(self, source):
        rows, columns = source.shape
        spare = self.spare[columns].at[pl.ds(0, rows)]
        copy = pltpu.make_async_copy(source, spare, self.home)
        copy.start()
        copy.wait()
        return spare[...].astype(WIDE)


    def tail_copy(self, w, step):
        place = lax.rem(self.line + step, self.lines)
        return remote(
            self.held[w].at[place, pl.ds(self.most, self.tail)],
            self.tail_got[w].at[step],
            self.tail_send.at[w, step],
            self.tail_recv.at[w, step],
            self.peer(step),
        )

    def tail_across(self, w):
        return remote(
            self.tails[w],
            self.tail_got[w].at[0],
            self.tail_send.at[w, 0],
            self.tail_recv.at[w, 0],
            self.opposite,
        )

    def add_tails(self, w):
        total = self.held[w][self.line, self.most :].astype(WIDE)
        for step in range(1, self.lines):
            self.tail_copy(w, step).wait_recv()
            total = total + self.fetch(self.tail_got[w].at[step])
        self.tails[w][...] = total.astype(LOW)
        self.tail_across(w).start()

    def product(self, left, right, place):
        rows = self.held[0].shape[1]
        block = left[pl.ds(pl.multiple_of(place * rows, rows), rows), :]
        every = right[...]
        return jnp.dot(
            block,
            every.reshape(every.shape[0] * every.shape[1], every.shape[2]),
            preferred_element_type=WIDE,
        )


    def extra_copy(self, w, step):
        place = lax.rem(self.line + step, self.lines)
        return remote(
            self.held[w].at[place],
            self.far_got[w].at[self.lines],
            self.line_send.at[w, step],
            self.line_recv.at[w, 0],
            {"dp": 2 * (2 if step == 1 else 1) + self.side},
        )

    def far(self, w, left, right):
        def body(at, carry):
            step = 1 + at
            if self.lines == 4:
                step = 1 + 2 * at - 3 * (at // 2)
            place = lax.rem(self.line + step, self.lines)
            other = (1 - self.side) * self.lines + place
            self.held[w][place] = self.product(left, right, other).astype(LOW)
            self.far_copy(w, place).start()
            if self.tail:

                @pl.when(at < self.lines - 1)
                def _():
                    self.tail_copy(w, step).start()

            return carry

        lax.fori_loop(0, self.lines, body, 0)

    def near(self, w, left, right, quarter):
        def put(place, step):
            part = self.product(left, right, self.side * self.lines + place)
            self.far_copy(w, place).wait_recv()
            got = self.fetch(self.far_got[w].at[place, pl.ds(0, self.most)])
            self.far_copy(w, place).wait_send()
            if self.tail and step is not None:
                self.tail_copy(w, step).wait_send()
            self.held[w][place, : self.most] = (part[: self.most] + got).astype(LOW)
            if self.tail:
                self.held[w][place, self.most :] = part[self.most :].astype(LOW)

        def body(step, carry):
            place = lax.rem(self.line + step, self.lines)
            put(place, step)
            self.near_copy(w, step).start()
            return carry

        if self.lines != 4:
            first, last = [1 + (quarter + k) * self.lines // 4 for k in range(2)]
            lax.fori_loop(first, min(last, self.lines), body, 0)
        elif quarter < 2:
            step = 1 + 2 * quarter
            end = 3 - 3 * quarter
            place = lax.rem(self.line + step, self.lines)
            put(place, step)

            @pl.when(self.line == end)
            def _():
                self.extra_copy(w, step).start()

            @pl.when(self.line != end)
            def _():
                self.near_copy(w, step).start()
        elif quarter == 2:
            place = lax.rem(self.line + 2, self.lines)
            put(place, 2)

            @pl.when((self.line == 1) | (self.line == 2))
            def _():
                self.extra_copy(w, 1).wait_recv()
                self.held[w][place] = (
                    self.held[w][place].astype(WIDE)
                    + self.fetch(self.far_got[w].at[self.lines])
                ).astype(LOW)

            self.near_copy(w, 2).start()
        if quarter < 3:
            return
        if self.tail:
            self.add_tails(w)
        put(self.line, None)
        if not self.tail:
            self.own_copy(w).start()
        if self.lines == 4:

            @pl.when((self.line == 0) | (self.line == 3))
            def _():
                spare = self.spare[self.held[w].shape[2]]
                spare[...] = jnp.zeros(spare.shape, LOW)
                slot = 1 + 2 * (self.line // 3)
                copy = pltpu.make_async_copy(spare, self.near_got[w].at[slot], self.home)
                copy.start()
                copy.wait()

    def own_copy(self, w):
        return pltpu.make_async_copy(
            self.held[w].at[self.line], self.near_got[w].at[0], self.line_send.at[w, 0]
        )

    def finish(self, w):
        if self.lines != 4:

            def body(step, carry):
                self.near_copy(w, step).wait()
                return carry

            lax.fori_loop(1, self.lines, body, 0)
        else:
            for step in range(1, 4):
                copy = self.near_copy(w, step)
                copy.wait_send()
                if step == 2:
                    copy.wait_recv()
                else:

                    @pl.when(self.line != (0 if step == 1 else 3))
                    def _():
                        copy.wait_recv()

        if self.tail:
            self.tail_across(w).wait()
            self.held[w][self.line, self.most :] = (
                self.held[w][self.line, self.most :].astype(WIDE)
                + self.fetch(self.tail_got[w].at[0])
            ).astype(LOW)
            self.own_copy(w).start()
        self.own_copy(w).wait()


class Near:
    def __init__(self, send, recv):
        self.send, self.recv = send, recv
        self.flight = {}
        own = lax.axis_index("tensor")
        half, rest = own // 2, lax.rem(own, 2)
        self.member = lambda k: 2 * lax.rem(half + k // 2, 2) + lax.rem(rest + lax.rem(k, 2), 2)

    def partners(self, members):
        return [{"tensor": self.member(k)} for k in range(1, members)]

    def start(self, tag, source, target, k):
        copy = remote(source, target, self.send.at[tag], self.recv.at[tag], self.partners(4)[k - 1])
        copy.start()
        self.flight[tag] = copy

    def wait(self, tag):
        self.flight[tag].wait_recv()

    def sent(self, tag):
        self.flight[tag].wait_send()


def dot_across(left, right):
    return lax.dot_general(
        left, right, (((1,), (1,)), ((), ())), preferred_element_type=WIDE
    )


def feed_kernel(lines, members, *refs):
    grad_turned, hidden, gain_all = refs[:3]
    later = refs[3:9]
    gate_hidden, up_hidden = refs[9:11]
    near_got, mid_all, mid_grad_out, hidden_out, gain_out = refs[11:14], *refs[14:18]
    mid_low_turned = refs[18]
    far_got, tail_got = refs[19:22], refs[22:25]
    gate_low, up_low, pre, up = refs[25:29]
    scatter_held = refs[29:32]
    spare, held, got, last, base, mid = refs[32:38]
    sems = refs[38:44]
    near_send, near_recv, home, column = refs[44:48]
    loaded, tails = refs[48:54], refs[54:]
    grad_ref, mid_turned, resid_ref, gate_weight, up_weight, down_weight = loaded
    parts = 2 * lines
    rows, width = resid_ref.shape
    loads = []
    for k, order in enumerate((5, 0, 1, 3, 4, 2)):
        loads.append(pltpu.make_async_copy(later[order], loaded[order], home.at[4 + k]))
        loads[k].start()
    slice_width = width // parts
    scatter = Scatter(
        lines,
        scatter_held,
        far_got,
        near_got,
        tail_got,
        {spare.shape[1]: spare},
        tails,
        3,
        sems + (home.at[0],),
    )
    near = Near(near_send, near_recv)
    greet(scatter.peers() + near.partners(members))
    scatter.far(0, grad_turned, hidden)

    def flat(ref):
        return ref[...].reshape(width, ref.shape[2])

    def pull(k, carry):
        first = pltpu.make_async_copy(gate_hidden.at[k], pre, home.at[1])
        second = pltpu.make_async_copy(up_hidden.at[k], up, home.at[2])
        first.start()
        second.start()
        grad = jnp.dot(grad_ref[k], flat(down_weight), preferred_element_type=WIDE)
        first.wait()
        second.wait()
        value = pre[...]
        root = (2.0 / math.pi) ** 0.5
        square = value * value
        lift = jnp.tanh(root * (value + 0.044715 * (value * square)))
        ramp = 0.5 * (1.0 + lift)
        slope = ramp + 0.5 * value * (1.0 - lift * lift) * root * (1.0 + 0.134145 * square)
        gate_low[k] = (grad * up[...] * slope).astype(LOW)
        up_low[k] = (grad * (value * ramp)).astype(LOW)
        return carry

    for load in loads:
        load.wait()
    lax.fori_loop(0, members // 2, pull, 0)
    scatter.near(0, grad_turned, hidden, 0)
    lax.fori_loop(members // 2, members, pull, 0)
    scatter.near(0, grad_turned, hidden, 1)
    scatter.far(1, mid_turned, gate_low)

    def back(k, put):
        for p in range(parts):
            columns = slice(p * slice_width, (p + 1) * slice_width)
            put(
                columns,
                dot_across(gate_low[k], gate_weight[p]) + dot_across(up_low[k], up_weight[p]),
            )

    def put_low(slot):
        def put(columns, value):
            held[slot, :, columns] = value.astype(LOW)

        return put

    def put_sum(columns, value):
        base[:, columns] = value

    back(3, put_low(0))
    near.start(0, held.at[0], got.at[0], 1)
    scatter.near(0, grad_turned, hidden, 2)
    back(2, put_sum)
    near.wait(0)
    near.sent(0)
    held[0] = (base[...] + got[0].astype(WIDE)).astype(LOW)
    near.start(1, held.at[0], got.at[1], 2)
    back(1, put_low(1))
    near.start(2, held.at[1], got.at[2], 1)
    scatter.near(0, grad_turned, hidden, 3)
    back(0, put_sum)
    scatter.far(2, mid_turned, up_low)
    scatter.near(1, mid_turned, gate_low, 0)
    near.wait(2)
    base[...] += got[2].astype(WIDE)
    scatter.near(1, mid_turned, gate_low, 1)
    near.wait(1)
    normed_grad = base[...] + got[1].astype(WIDE)
    resid = resid_ref[...]
    scale = lax.rsqrt(jnp.mean(resid * resid, axis=-1, keepdims=True) + 1e-06)
    unit = resid * scale
    base[...] = normed_grad * unit
    gain_out[...] = jnp.broadcast_to(
        jnp.sum(base[...], axis=0, keepdims=True), gain_out.shape
    )
    dot = jnp.zeros((rows, 1), WIDE)
    for p in range(parts):
        columns = slice(p * slice_width, (p + 1) * slice_width)
        dot += jnp.sum(base[:, columns] * gain_all[p][1:2], axis=-1, keepdims=True)
    dot = dot * (1.0 / width)
    base[...] = normed_grad
    for p in range(parts):
        columns = slice(p * slice_width, (p + 1) * slice_width)
        block = resid_ref[:, columns] * scale
        mid_grad = grad_ref[0, :, columns].astype(WIDE) + scale * (
            base[:, columns] * gain_all[p][1:2] - block * dot
        )
        base[:, columns] = mid_grad
        mid[:, columns] = mid_grad.astype(LOW)
    mid_grad_copy = pltpu.make_async_copy(base, mid_grad_out, home.at[1])
    mid_grad_copy.start()
    near.start(3, mid, mid_all.at[2], 2)
    near.start(4, mid, mid_all.at[1], 1)
    own = pltpu.make_async_copy(mid, mid_all.at[0], home.at[3])
    own.start()
    scatter.near(1, mid_turned, gate_low, 2)
    scatter.near(1, mid_turned, gate_low, 3)

    def down(k, put):
        for p in range(parts):
            columns = slice(p * slice_width, (p + 1) * slice_width)
            put(columns, dot_across(hidden[k], down_weight[p]))

    near.sent(1)
    near.sent(2)
    down(3, put_low(0))
    mid_grad_copy.wait()
    near.start(6, held.at[0], last.at[0], 1)
    down(2, put_sum)
    scatter.near(2, mid_turned, up_low, 0)
    near.wait(3)
    near.start(5, mid_all.at[2], mid_all.at[3], 1)
    near.wait(6)
    near.sent(6)
    held[0] = (base[...] + last[0].astype(WIDE)).astype(LOW)
    near.start(7, held.at[0], last.at[1], 2)
    down(1, put_low(1))
    near.start(8, held.at[1], last.at[2], 1)
    scatter.near(2, mid_turned, up_low, 1)
    down(0, put_sum)
    own.wait()
    near.wait(4)
    near.wait(5)
    for k in range(members):
        copy = pltpu.make_async_copy(mid_all.at[k], got.at[0], home.at[9])
        copy.start()
        copy.wait()
        if k:
            turned_copy.wait()
        for c in range(width // 256):
            block = slice(c * 256, (c + 1) * 256)
            column[block, :] = got[0, :, block].T
        turned_copy = pltpu.make_async_copy(
            column, mid_low_turned.at[:, pl.ds(k * rows, rows)], home.at[10]
        )
        turned_copy.start()
    turned_copy.wait()
    scatter.near(2, mid_turned, up_low, 2)
    scatter.finish(0)
    scatter.near(2, mid_turned, up_low, 3)
    near.wait(8)
    near.wait(7)
    near.sent(3)
    near.sent(4)
    for p in range(parts):
        columns = slice(p * slice_width, (p + 1) * slice_width)
        value = base[:, columns] + last[2, :, columns].astype(WIDE)
        value = value + last[1, :, columns].astype(WIDE) + resid_ref[:, columns]
        start = (2 * (p % lines) + p // lines) * slice_width
        mid[:, start : start + slice_width] = value.astype(LOW)
    own = pltpu.make_async_copy(mid, hidden_out, home.at[3])
    own.start()
    own.wait()
    near.sent(5)
    near.sent(7)
    near.sent(8)
    scatter.finish(1)
    scatter.finish(2)


def feed_backward(
    grad, grad_turned, mid_turned, hidden, resid, gains, weights, pres, lines, members
):
    parts = 2 * lines
    rows, width = resid.shape
    columns = hidden.shape[2]
    slice_width = width // parts
    blocks = (members, rows)
    piece = (lines, slice_width, columns)
    later = [grad, mid_turned, resid, *weights]
    outs = [(piece, LOW)] * 3
    outs += [
        (blocks + (width,), LOW),
        ((rows, width), WIDE),
        ((rows, width), LOW),
        ((8, width), WIDE),
        ((width, rows * members), LOW),
    ]
    outs += [((lines + 1,) + piece[1:], LOW)] * 3
    tail = max(tail_rows(slice_width, lines, 3), 16)
    outs += [((lines, tail, columns), LOW)] * 3
    return pl.pallas_call(
        functools.partial(feed_kernel, lines, members),
        out_shape=[jax.ShapeDtypeStruct(shape, dtype) for shape, dtype in outs],
        in_specs=[INSIDE] * 3 + [ANY] * 8,
        out_specs=[ANY] * 6 + [INSIDE] + [ANY] * 7,
        scratch_shapes=[
            pltpu.VMEM(blocks + (columns,), LOW),
            pltpu.VMEM(blocks + (columns,), LOW),
            pltpu.VMEM((rows, columns), WIDE),
            pltpu.VMEM((rows, columns), WIDE),
            pltpu.VMEM(piece, LOW),
            pltpu.VMEM(piece, LOW),
            pltpu.VMEM(piece, LOW),
            pltpu.VMEM(piece[1:], LOW),
            pltpu.VMEM((2, rows, width), LOW),
            pltpu.VMEM((3, rows, width), LOW),
            pltpu.VMEM((3, rows, width), LOW),
            pltpu.VMEM((rows, width), WIDE),
            pltpu.VMEM((rows, width), LOW),
            pltpu.SemaphoreType.DMA((3, lines)),
            pltpu.SemaphoreType.DMA((3, lines)),
            pltpu.SemaphoreType.DMA((3, lines)),
            pltpu.SemaphoreType.DMA((3, lines)),
            pltpu.SemaphoreType.DMA((3, lines)),
            pltpu.SemaphoreType.DMA((3, lines)),
            pltpu.SemaphoreType.DMA((9,)),
            pltpu.SemaphoreType.DMA((9,)),
            pltpu.SemaphoreType.DMA((11,)),
            pltpu.VMEM((width, rows), LOW),
        ]
        + [pltpu.VMEM(value.shape, value.dtype) for value in later]
        + [pltpu.VMEM((tail, columns), LOW)] * 3,
        compiler_params=pltpu.CompilerParams(
            collective_id=1, has_side_effects=True, vmem_limit_bytes=ROOM
        ),
        cost_estimate=pl.CostEstimate(flops=10**11, bytes_accessed=10**9, transcendentals=0),
        name="feed_backward",
    )(grad_turned, hidden, gains, *later, *pres)[:8]


def retention_kernel(lines, members, *refs):
    later = refs[:6]
    cos_ref, sin_ref, down_seg, along_seg, rate_ref = refs[6:11]
    hidden_ref, gain_all, gain_part = refs[11:14]
    mid_grad_ref, mid_all, retained_all, gate_all = refs[14:18]
    weights = refs[18:23]
    near_got, in_grad_out, gain_out = refs[23:28], refs[28], refs[29]
    far_got, tail_got = refs[30:35], refs[35:40]
    wide_one, wide_two, short_one, short_two = refs[40:44]
    gate_low, retained_low, query_low, key_low = refs[44:48]
    scatter_held = refs[48:53]
    spare_wide, spare_short, held, got, base, retained, gate = refs[53:60]
    pieces, piece_got, total, total_got = refs[60:64]
    sems = refs[64:70]
    near_send, near_recv, gain_send, gain_recv, home = refs[70:75]
    loaded, tails = refs[75:81], refs[81:]
    mixed, normed_turned, query, keys, values, turned = loaded
    value_low = mixed
    parts = 2 * lines
    rows, width = hidden_ref.shape
    slice_width = width // parts
    heads = rate_ref.shape[0]
    value_columns = values.shape[2]
    length = rows * members
    scatter = Scatter(
        lines,
        scatter_held,
        far_got,
        near_got,
        tail_got,
        {spare_wide.shape[1]: spare_wide, spare_short.shape[1]: spare_short},
        tails,
        2,
        sems + (home.at[0],),
    )
    near = Near(near_send, near_recv)
    me = lax.axis_index("dp")
    here = scatter.side * lines + scatter.line
    others = [{"dp": lax.rem(me + k, parts)} for k in range(1, parts)]
    greet(others + near.partners(members))

    def fetch(source, target, sem):
        copy = pltpu.make_async_copy(source, target, home.at[sem])
        copy.start()
        return copy

    loads = [fetch(later[k], loaded[k], 9 + k) for k in (5, 0)]
    out_copy = fetch(weights[0], wide_one, 1)
    loads += [fetch(later[k], loaded[k], 9 + k) for k in range(1, 5)]
    value_copy = fetch(weights[2], wide_two, 2)
    query_copy = fetch(weights[3], short_one, 3)
    key_copy = fetch(weights[4], short_two, 4)
    grad_copy = fetch(mid_grad_ref, in_grad_out, 7)
    loads[0].wait()
    loads[1].wait()
    scatter.far(0, turned, mixed)
    out_copy.wait()
    for load in loads[2:]:
        load.wait()

    column = lax.broadcasted_iota(jnp.int32, (rows, value_columns), 1)

    def by_head(parts_of):
        result = parts_of[0]
        for h in range(1, heads):
            result = jnp.where(column < h * VAL, result, parts_of[h])
        return result

    def inside(h):
        return (column >= h * VAL) & (column < (h + 1) * VAL)

    def head_mean(value):
        return by_head(
            [
                jnp.sum(jnp.where(inside(h), value, 0.0), axis=-1, keepdims=True) * (1.0 / VAL)
                for h in range(heads)
            ]
        )

    def unmix(k, carry):
        first = fetch(retained_all.at[k], retained, 5)
        second = fetch(gate_all.at[k], gate, 6)
        fetch(mid_all.at[k], held.at[0], 8).wait()
        grad = jnp.dot(
            held[0],
            wide_one[...].reshape(width, value_columns),
            preferred_element_type=WIDE,
        )
        first.wait()
        second.wait()
        value = retained[...]
        centred = value - head_mean(value)
        rate = lax.rsqrt(head_mean(centred * centred) + 1.0)
        pre = gate[...]
        sigma = 1.0 / (1.0 + jnp.exp(-pre))
        gate_low[k] = (
            grad * (centred * rate) * (sigma * (1.0 + pre * (1.0 - sigma)))
        ).astype(LOW)
        grouped_grad = grad * (pre * sigma)
        retained_low[k] = (
            rate * (grouped_grad - head_mean(grouped_grad))
            - (rate * rate * rate) * centred * head_mean(grouped_grad * centred)
        ).astype(LOW)
        return carry

    lax.fori_loop(0, members // 2, unmix, 0)
    scatter.near(0, turned, mixed, 0)
    lax.fori_loop(members // 2, members, unmix, 0)
    scatter.near(0, turned, mixed, 1)
    scatter.far(1, normed_turned, gate_low)
    gate_copy = fetch(weights[1], wide_one, 1)

    def decay(h, late, early, late_segment, early_segment, turn):
        sign = -1 if turn else 1
        distance = (
            sign
            * (
                lax.broadcasted_iota(jnp.int32, (rows, rows), 0)
                - lax.broadcasted_iota(jnp.int32, (rows, rows), 1)
            )
            + (late - early)
        )
        same = (distance >= 0) & (late_segment == early_segment)
        return jnp.where(
            same,
            jnp.exp(rate_ref[h : h + 1, :1] * jnp.maximum(distance, 0).astype(WIDE)),
            0.0,
        )

    def start_of(k):
        return pl.multiple_of(near.member(k) * rows, rows)

    wing = KEY // 2
    along = [along_seg[:, pl.ds(start_of(k), rows)] for k in range(members)]

    def turn_back(target, k, h, grad, scale):
        at = pl.ds(pl.multiple_of(k * rows, rows), rows)
        cosine, sine = cos_ref[at, :], sin_ref[at, :]
        first, second = grad[:, :wing], grad[:, wing:]
        target[k, :, h * KEY : h * KEY + wing] = (
            (first * cosine + second * sine) * scale
        ).astype(LOW)
        target[k, :, h * KEY + wing : (h + 1) * KEY] = (
            (second * cosine - first * sine) * scale
        ).astype(LOW)

    def early_side(m, carry):
        early = start_of(m)
        early_segment = down_seg[pl.ds(early, rows), :]
        value_grads = []
        for h in range(heads):
            head = slice(h * KEY, (h + 1) * KEY)
            masked = jnp.where(inside(h), values[m].astype(WIDE), 0.0).astype(LOW)
            value_grad = jnp.zeros((rows, value_columns), WIDE)
            key_grad = jnp.zeros((rows, KEY), WIDE)
            for n in range(members):
                late = start_of(n)
                late_segment = along[n]
                mask = decay(h, late, early, late_segment, early_segment, True)
                score = (dot_across(keys[m, :, head], query[n, :, head]) * mask).astype(LOW)
                raw = (dot_across(masked, retained_low[n]) * mask).astype(LOW)
                value_grad += jnp.dot(score, retained_low[n], preferred_element_type=WIDE)
                key_grad += jnp.dot(raw, query[n, :, head], preferred_element_type=WIDE)
            value_grads.append(value_grad)
            turn_back(key_low, m, h, key_grad, 1.0)
        value_low[m] = by_head(value_grads).astype(LOW)
        return carry

    scatter.near(0, turned, mixed, 2)
    scatter.near(0, turned, mixed, 3)
    early_side(0, 0)
    early_side(1, 0)
    scatter.near(1, normed_turned, gate_low, 0)
    early_side(2, 0)
    early_side(3, 0)
    scatter.far(2, normed_turned, value_low)
    scatter.near(1, normed_turned, gate_low, 1)
    scatter.near(1, normed_turned, gate_low, 2)
    scatter.far(4, normed_turned, key_low)
    scatter.near(1, normed_turned, gate_low, 3)

    def late_side(n, carry):
        late = start_of(n)
        late_segment = down_seg[pl.ds(late, rows), :]
        for h in range(heads):
            head = slice(h * KEY, (h + 1) * KEY)
            masked = jnp.where(inside(h), retained_low[n].astype(WIDE), 0.0).astype(LOW)
            query_grad = jnp.zeros((rows, KEY), WIDE)
            for m in range(members):
                early = start_of(m)
                early_segment = along[m]
                mask = decay(h, late, early, late_segment, early_segment, False)
                raw = (dot_across(masked, values[m]) * mask).astype(LOW)
                query_grad += jnp.dot(raw, keys[m, :, head], preferred_element_type=WIDE)
            turn_back(query_low, n, h, query_grad, KEY ** (-0.5))
        return carry

    lax.fori_loop(0, members // 2, late_side, 0)
    scatter.near(2, normed_turned, value_low, 0)
    lax.fori_loop(members // 2, members, late_side, 0)
    scatter.near(2, normed_turned, value_low, 1)
    scatter.far(3, normed_turned, query_low)
    for copy in (gate_copy, value_copy, query_copy, key_copy, grad_copy):
        copy.wait()

    def back(k, put):
        for p in range(parts):
            columns = slice(p * slice_width, (p + 1) * slice_width)
            put(
                columns,
                dot_across(gate_low[k], wide_one[p])
                + dot_across(value_low[k], wide_two[p])
                + dot_across(query_low[k], short_one[p])
                + dot_across(key_low[k], short_two[p]),
            )

    def put_low(slot):
        def put(columns, value):
            held[slot, :, columns] = value.astype(LOW)

        return put

    def put_sum(columns, value):
        base[:, columns] = value

    back(3, put_low(0))
    near.start(0, held.at[0], got.at[0], 1)
    back(2, put_sum)
    scatter.near(2, normed_turned, value_low, 2)
    near.wait(0)
    near.sent(0)
    held[0] = (base[...] + got[0].astype(WIDE)).astype(LOW)
    near.start(1, held.at[0], got.at[1], 2)
    back(1, put_low(1))
    near.start(2, held.at[1], got.at[2], 1)
    scatter.near(2, normed_turned, value_low, 3)
    back(0, put_sum)
    for quarter in range(4):
        scatter.near(4, normed_turned, key_low, quarter)
    near.wait(2)
    base[...] += got[2].astype(WIDE)
    near.wait(1)
    normed_grad = base[...] + got[1].astype(WIDE)
    base[...] = normed_grad
    resid = hidden_ref[...].astype(WIDE)
    scale = lax.rsqrt(jnp.mean(resid * resid, axis=-1, keepdims=True) + 1e-06)
    dot = jnp.zeros((rows, 1), WIDE)
    for p in range(parts):
        columns = slice(p * slice_width, (p + 1) * slice_width)
        product = base[:, columns] * (hidden_ref[:, columns].astype(WIDE) * scale)
        row = lax.broadcasted_iota(jnp.int32, (8, slice_width), 0)
        pieces[p] = jnp.where(
            row == 0, jnp.sum(product, axis=0, keepdims=True), gain_part[:, columns]
        )
        dot += jnp.sum(product * gain_all[p][0:1], axis=-1, keepdims=True)
    dot = dot * (1.0 / width)
    gains = []
    for k in range(1, parts):
        other = lax.rem(me + k, parts)
        place = lax.rem(other, 2) * lines + other // 2
        copy = remote(
            pieces.at[place], piece_got.at[k], gain_send.at[k], gain_recv.at[k], others[k - 1]
        )
        copy.start()
        gains.append(copy)
    for p in range(parts):
        columns = slice(p * slice_width, (p + 1) * slice_width)
        block = hidden_ref[:, columns].astype(WIDE) * scale
        base[:, columns] = in_grad_out[:, columns] + scale * (
            base[:, columns] * gain_all[p][0:1] - block * dot
        )
    for p in range(parts):
        start = (2 * (p % lines) + p // lines) * slice_width
        in_grad_out[:, start : start + slice_width] = base[
            :, p * slice_width : (p + 1) * slice_width
        ]
    value = pieces[here]
    for k in range(1, parts):
        gains[k - 1].wait_recv()
        value = value + piece_got[k]
    total[...] = value
    for k in range(1, members):
        near.start(2 + k, total, total_got.at[k], k)
    scatter.near(3, normed_turned, query_low, 0)
    scatter.finish(0)
    scatter.near(3, normed_turned, query_low, 1)
    scatter.finish(1)
    scatter.near(3, normed_turned, query_low, 2)
    scatter.finish(2)
    scatter.near(3, normed_turned, query_low, 3)
    scatter.finish(4)
    scatter.finish(3)
    for k in range(1, members):
        near.wait(2 + k)
        value = value + total_got[k]
    gain_out[...] = value
    for tag in range(1, 2 + members):
        near.sent(tag)
    for copy in gains:
        copy.wait_send()


def retention_backward(inside, streamed, weights, lines, members, slice_width):
    parts = 2 * lines
    rows, width = inside[11].shape
    blocks = (members, rows)
    wide, short = weights[0].shape[2], weights[3].shape[2]
    widths = [wide, wide, wide, short, short]
    pieces = [(lines, slice_width, columns) for columns in widths]
    outs = [(piece, LOW) for piece in pieces]
    outs += [((rows, width), WIDE), ((8, slice_width), WIDE)]
    outs += [((lines + 1,) + piece[1:], LOW) for piece in pieces]
    tail = max(tail_rows(slice_width, lines, 2), 16)
    outs += [((lines, tail, columns), LOW) for columns in widths]
    return pl.pallas_call(
        functools.partial(retention_kernel, lines, members),
        out_shape=[jax.ShapeDtypeStruct(shape, dtype) for shape, dtype in outs],
        in_specs=[ANY] * 6 + [INSIDE] * 8 + [ANY] * 9,
        out_specs=[ANY] * 5 + [INSIDE] * 2 + [ANY] * 10,
        scratch_shapes=[
            pltpu.VMEM(weights[0].shape, LOW),
            pltpu.VMEM(weights[0].shape, LOW),
            pltpu.VMEM(weights[3].shape, LOW),
            pltpu.VMEM(weights[3].shape, LOW),
            pltpu.VMEM(blocks + (wide,), LOW),
            pltpu.VMEM(blocks + (wide,), LOW),
            pltpu.VMEM(blocks + (short,), LOW),
            pltpu.VMEM(blocks + (short,), LOW),
        ]
        + [pltpu.VMEM(piece, LOW) for piece in pieces]
        + [
            pltpu.VMEM((slice_width, wide), LOW),
            pltpu.VMEM((slice_width, short), LOW),
            pltpu.VMEM((2, rows, width), LOW),
            pltpu.VMEM((3, rows, width), LOW),
            pltpu.VMEM((rows, width), WIDE),
            pltpu.VMEM((rows, wide), WIDE),
            pltpu.VMEM((rows, wide), WIDE),
            pltpu.VMEM((parts, 8, slice_width), WIDE),
            pltpu.VMEM((parts, 8, slice_width), WIDE),
            pltpu.VMEM((8, slice_width), WIDE),
            pltpu.VMEM((members, 8, slice_width), WIDE),
            pltpu.SemaphoreType.DMA((5, lines)),
            pltpu.SemaphoreType.DMA((5, lines)),
            pltpu.SemaphoreType.DMA((5, lines)),
            pltpu.SemaphoreType.DMA((5, lines)),
            pltpu.SemaphoreType.DMA((5, lines)),
            pltpu.SemaphoreType.DMA((5, lines)),
            pltpu.SemaphoreType.DMA((6,)),
            pltpu.SemaphoreType.DMA((6,)),
            pltpu.SemaphoreType.DMA((parts,)),
            pltpu.SemaphoreType.DMA((parts,)),
            pltpu.SemaphoreType.DMA((15,)),
        ]
        + [pltpu.VMEM(value.shape, value.dtype) for value in inside[:6]]
        + [pltpu.VMEM((tail, columns), LOW) for columns in widths],
        compiler_params=pltpu.CompilerParams(
            collective_id=2, has_side_effects=True, vmem_limit_bytes=ROOM
        ),
        cost_estimate=pl.CostEstimate(flops=10**11, bytes_accessed=10**9, transcendentals=0),
        name="retention_backward",
    )(*inside, *streamed, *weights)[:7]


def on_device(
    hidden_in,
    out_grad,
    segment_ids,
    norm1_gain,
    w_query,
    w_key,
    w_value,
    w_gate,
    w_out,
    norm2_gain,
    w_mlp_gate,
    w_mlp_up,
    w_mlp_down,
):
    _, rows, width = hidden_in.shape
    parts = lax.axis_size("dp")
    lines = parts // 2
    slice_width = width // parts
    own = lax.axis_index("tensor")
    members = lax.axis_size("tensor")
    order = list(range(0, parts, 2)) + list(range(1, parts, 2))

    def to_places(value):
        blocks = [value[:, k * slice_width : (k + 1) * slice_width] for k in order]
        return jnp.concatenate(blocks, axis=1)

    heads_here = w_query.shape[1] // KEY
    resid_low = to_places(hidden_in.reshape(rows, width))
    grad_local = to_places(out_grad.reshape(rows, width))
    gain_rows = jnp.stack([norm1_gain, norm2_gain])
    position = jnp.concatenate(
        [(own ^ k) * rows + jnp.arange(rows, dtype=jnp.int32) for k in range(members)]
    )
    cosine, sine = rotary_tables(position, KEY)
    head_numbers = (jnp.arange(heads_here, dtype=jnp.int32) + own * heads_here).astype(WIDE)
    rates = jnp.log1p(-jnp.exp2(-5.0 - head_numbers))
    rates = jnp.broadcast_to(rates[:, None], (heads_here, 128))
    outs = forward(
        resid_low,
        grad_local,
        gain_rows,
        cosine,
        sine,
        segment_ids,
        rates,
        [w_query, w_key, w_value.T, w_gate.T, w_out, w_mlp_gate.T, w_mlp_up.T, w_mlp_down],
        lines,
        members,
    )
    normed_turned, grad_full, gains = outs[:3]
    query_weight, key_weight, value_weight, gate_weight, out_weight = outs[3:8]
    query, keys, values, gate_pre, grad_turned = outs[11:16]
    retained, mixed, resid_mid, mid_turned, gate_hidden, up_hidden, hidden = outs[16:]
    feed_outs = feed_backward(
        grad_full,
        grad_turned,
        mid_turned,
        hidden,
        resid_mid,
        gains,
        outs[8:11],
        (gate_hidden, up_hidden),
        lines,
        members,
    )
    down_grad, mlp_gate_grad, mlp_up_grad, mid_all, mid_grad = feed_outs[:5]
    hidden_out, gain_part, mid_low_turned = feed_outs[5:]
    out_weight_grad, gate_grad, value_grad, query_grad, key_grad, in_grad, gain_total = (
        retention_backward(
            [
                mixed,
                normed_turned,
                query,
                keys,
                values,
                mid_low_turned,
                cosine,
                sine,
                segment_ids.T,
                segment_ids,
                rates,
                resid_low,
                gains,
                gain_part,
            ],
            [mid_grad, mid_all, retained, gate_pre],
            [out_weight, gate_weight, value_weight, query_weight, key_weight],
            lines,
            members,
            slice_width,
        )
    )
    def add_up(pieces):
        total = pieces[0].astype(WIDE)
        for k in range(1, pieces.shape[0]):
            total = total + pieces[k].astype(WIDE)
        return total

    return (
        hidden_out.reshape(hidden_in.shape),
        in_grad.reshape(hidden_in.shape),
        gain_total[0],
        add_up(query_grad),
        add_up(key_grad),
        add_up(value_grad),
        add_up(gate_grad),
        add_up(out_weight_grad).T,
        gain_total[1],
        add_up(mlp_gate_grad),
        add_up(mlp_up_grad),
        add_up(down_grad).T,
    )


def solution(mesh):
    return jax.shard_map(
        on_device,
        mesh=mesh,
        in_specs=(
            P("dp", "tensor", None),
            P("dp", "tensor", None),
            P("dp", None),
            P("dp"),
            P("dp", "tensor"),
            P("dp", "tensor"),
            P("dp", "tensor"),
            P("dp", "tensor"),
            P("tensor", "dp"),
            P("dp"),
            P("dp", "tensor"),
            P("dp", "tensor"),
            P("tensor", "dp"),
        ),
        out_specs=(
            P("dp", "tensor", None),
            P("dp", "tensor", None),
            P("dp"),
            P("dp", "tensor"),
            P("dp", "tensor"),
            P("dp", "tensor"),
            P("dp", "tensor"),
            P("tensor", "dp"),
            P("dp"),
            P("dp", "tensor"),
            P("dp", "tensor"),
            P("tensor", "dp"),
        ),
        check_vma=False,
    )
```

```python
import functools
import math

import jax
import jax.numpy as jnp
from jax import lax
from jax.experimental import pallas as pl
from jax.experimental.pallas import tpu as pltpu
from jax.sharding import PartitionSpec as P

KEY = 256
VAL = 432
LOW = jnp.bfloat16
WIDE = jnp.float32
WEIGHTS = 8
MESH = pl.DeviceIdType.MESH
ANY = pl.BlockSpec(memory_space=pl.ANY)
INSIDE = pl.BlockSpec(memory_space=pltpu.VMEM)
ROOM = 60 * 1024 * 1024

def rotary_tables(position, width):
    half = width // 2
    frequency = 10000.0 ** (-2.0 * jnp.arange(half, dtype=jnp.int32).astype(WIDE) / width)
    angle = position.astype(WIDE)[:, None] * frequency[None, :]
    return (jnp.cos(angle), jnp.sin(angle))


def greet(peers):
    barrier = pltpu.get_barrier_semaphore()
    for peer in peers:
        pl.semaphore_signal(barrier, inc=1, device_id=peer, device_id_type=MESH)
    pl.semaphore_wait(barrier, len(peers))


def remote(source, target, send, recv, device):
    return pltpu.make_async_remote_copy(
        src_ref=source,
        dst_ref=target,
        send_sem=send,
        recv_sem=recv,
        device_id=device,
        device_id_type=MESH,
    )


def forward_kernel(lines, members, *refs):
    hidden_ref, grad_ref, gain_ref, cos_ref, sin_ref, down_seg, along_seg, rate_ref = refs[:8]
    shards = refs[8:16]
    normed_turned, grad_all, gain_all = refs[16:19]
    wholes = refs[19:27]
    query_out, keys_out, values_out, gate_out, grad_turned = refs[27:32]
    retained_out, mixed_out, resid_out, mid_turned, gate_hidden_out, up_hidden_out = refs[32:38]
    hidden_out = refs[38]
    normed, mid, short, wide_one, wide_two, turned = refs[39:45]
    query, keys, scores, values, retained, gate, mixed, hidden = refs[45:53]
    held, got, base = refs[53:56]
    line_send, line_recv, side_send, side_recv = refs[56:60]
    near_send, near_recv, gain_send, gain_recv, home, tail_send, tail_recv, gain_rows, raw, flip = refs[60:]

    parts = 2 * lines
    rows, width = hidden_ref.shape
    slice_width = gain_rows.shape[1]
    heads = rate_ref.shape[0]
    value_columns = values.shape[2]
    me = lax.axis_index("dp")
    line, side = me // 2, lax.rem(me, 2)
    here = side * lines + line
    own = lax.axis_index("tensor")
    half, rest = own // 2, lax.rem(own, 2)

    def member(k):
        return 2 * lax.rem(half + k // 2, 2) + lax.rem(rest + lax.rem(k, 2), 2)

    partners = [None] + [{"tensor": member(k)} for k in range(1, members)]
    others = [{"dp": lax.rem(me + k, parts)} for k in range(1, parts)]
    opposite = {"dp": 2 * line + (1 - side)}
    greet(others + partners[1:])

    local = {}
    slots = iter(range(32))

    def keep(source, target):
        slot = next(slots)
        local[slot] = pltpu.make_async_copy(source, target, home.at[slot])
        local[slot].start()
        return slot

    def finish(slot):
        local.pop(slot).wait()

    near = {}

    def near_start(tag, source, target, k):
        copy = remote(source, target, near_send.at[tag], near_recv.at[tag], partners[k])
        copy.start()
        near[tag] = copy

    across = {}
    ours = {}

    inner = lines == 4

    def line_copy(w, step):
        return remote(
            source(w),
            wholes[w].at[here],
            line_send.at[w, step],
            line_recv.at[w, step],
            {"dp": 2 * lax.rem(line + step, lines) + side},
        )

    def relay_copy(w):
        place = side * lines + 3 * (2 - line)
        return remote(
            wholes[w].at[place],
            wholes[w].at[place],
            line_send.at[w, 0],
            line_recv.at[w, 2 * line - 1],
            {"dp": 6 * (line - 1) + side},
        )

    tail = slice_width // 8 // 16 * 16
    most = slice_width - tail

    def side_copy(w, step):
        place = side * lines + lax.rem(line + lines - step, lines)
        return remote(
            wholes[w].at[place, pl.ds(0, most)],
            wholes[w].at[place, pl.ds(0, most)],
            side_send.at[w, step],
            side_recv.at[w, step],
            opposite,
        )

    there = (1 - side) * lines + line

    def tail_copy(w, step):
        return remote(
            wholes[w].at[there, pl.ds(most, tail)],
            wholes[w].at[there, pl.ds(most, tail)],
            tail_send.at[w, step],
            tail_recv.at[w, step],
            {"dp": 2 * lax.rem(line + step, lines) + side},
        )

    def on_line(w, step, act):
        if inner and step != 2:

            @pl.when(line != (3 if step == 1 else 0))
            def _():
                act(line_copy(w, step))
        else:
            act(line_copy(w, step))

    sends = [2, 1, 3] if inner else list(range(1, lines))

    def prepare(w):
        if w < 2:
            ours[w] = keep(shards[w], wholes[w].at[here])
            return
        copy = pltpu.make_async_copy(shards[w], raw, home.at[home.shape[0] - 1])
        copy.start()
        copy.wait()
        columns = raw.shape[0]
        for at in range(0, columns, 128):
            block = slice(at, min(at + 128, columns))
            flip[:, block] = raw[block, :].T
        copy = pltpu.make_async_copy(flip, wholes[w].at[here], home.at[home.shape[0] - 1])
        copy.start()
        copy.wait()

    def source(w):
        return shards[w] if w < 2 else wholes[w].at[here]

    def start_lines(w):
        prepare(w)
        for step in sends:
            on_line(w, step, lambda copy: copy.start())
        across[w, 0] = remote(
            source(w), wholes[w].at[here], side_send.at[w, 0], side_recv.at[w, 0], opposite
        )
        across[w, 0].start()

    def pass_on(w, third):
        for at in range(third * (lines - 1) // 3, (third + 1) * (lines - 1) // 3):
            step = at + 1
            if inner:
                late = 3 - 2 * ((3 - line) // 3)
                step = [2, 4 - late, late][at]
            if tail and at == 0:
                across[w, 0].wait_recv()
                for hop in range(1, lines):
                    tail_copy(w, hop).start()
            line_copy(w, step).wait_recv()
            if inner and at == 0:

                @pl.when((line == 1) | (line == 2))
                def _():
                    relay_copy(w).start()

            side_copy(w, step).start()

    def complete(w):
        if not tail:
            across[w, 0].wait_recv()
        for step in range(1, lines):
            side_copy(w, step).wait_recv()
            if tail:
                tail_copy(w, step).wait_recv()
        if w in ours:
            finish(ours[w])

    def load(w, target, sem):
        copy = pltpu.make_async_copy(wholes[w], target, sem)
        copy.start()
        copy.wait()

    def stage(w, target, body):
        if w + 1 < WEIGHTS:
            for third in range(3):
                pass_on(w + 1, third)
        if w + 3 < WEIGHTS:
            start_lines(w + 3)
        complete(w)
        load(w, target, home.at[home.shape[0] - 1 - w])
        lax.fori_loop(0, members, body, 0)

    gain_rows[...] = jnp.where(
        lax.broadcasted_iota(jnp.int32, gain_rows.shape, 0) == 0,
        gain_ref[0:1, :].astype(WIDE),
        gain_ref[1:2, :].astype(WIDE),
    )
    gains = []
    for k in range(1, parts):
        copy = remote(
            gain_rows, gain_all.at[here], gain_send.at[k], gain_recv.at[k], others[k - 1]
        )
        copy.start()
        gains.append(copy)
    gain_all[here] = gain_rows[...]
    for w in range(3):
        start_lines(w)

    def scale_into(target, scaled, which):
        for p in range(parts):
            columns = slice(p * slice_width, (p + 1) * slice_width)
            target[0, :, columns] = (
                scaled[:, columns] * gain_all[p][which : which + 1]
            ).astype(LOW)

    resid = hidden_ref[...].astype(WIDE)
    scaled = resid * lax.rsqrt(jnp.mean(resid * resid, axis=-1, keepdims=True) + 1e-06)
    for copy in gains:
        copy.wait_recv()
    scale_into(normed, scaled, 0)
    for k in range(1, members):
        near_start(k - 1, normed.at[0], normed.at[k], k)
    for k in range(1, members):
        near_start(2 + k, grad_ref, mid.at[k], k)
    grad_kept = keep(grad_ref, mid.at[0])
    for third in range(3):
        pass_on(0, third)
    for k in range(1, members):
        near[k - 1].wait_recv()

    def turn_over(source):
        tile = 256

        def body(k, carry):
            at = pl.ds(pl.multiple_of(k * rows, rows), rows)
            for c in range(width // tile):
                columns = slice(c * tile, (c + 1) * tile)
                turned[columns, at] = source[k, :, columns].T
            return carry

        lax.fori_loop(0, members, body, 0)

    turn_over(normed)
    turned_kept = keep(turned, normed_turned)

    def flat(ref):
        return ref[...].reshape(width, ref.shape[2])

    def turn(source, target, scale):
        def body(k, carry):
            pre = jnp.dot(normed[k], flat(source), preferred_element_type=WIDE)
            at = pl.ds(pl.multiple_of(k * rows, rows), rows)
            cosine, sine = cos_ref[at, :], sin_ref[at, :]
            wing = KEY // 2
            for h in range(heads):
                first = pre[:, h * KEY : h * KEY + wing]
                second = pre[:, h * KEY + wing : (h + 1) * KEY]
                target[k, :, h * KEY : h * KEY + wing] = (
                    (first * cosine - second * sine) * scale
                ).astype(LOW)
                target[k, :, h * KEY + wing : (h + 1) * KEY] = (
                    (second * cosine + first * sine) * scale
                ).astype(LOW)
            return carry

        return body

    stage(0, short, turn(short, query, KEY ** (-0.5)))
    keep(query, query_out)
    stage(1, short, turn(short, keys, 1.0))
    keep(keys, keys_out)

    def score(k, carry):
        place = member(k)
        at = pl.multiple_of(place * rows, rows)
        segment = down_seg[pl.ds(at, rows), :]
        for h in range(heads):
            head = slice(h * KEY, (h + 1) * KEY)
            for m in range(members):
                start = pl.multiple_of(member(m) * rows, rows)
                raw = lax.dot_general(
                    query[k, :, head],
                    keys[m, :, head],
                    (((1,), (1,)), ((), ())),
                    preferred_element_type=WIDE,
                )
                distance = (
                    lax.broadcasted_iota(jnp.int32, (rows, rows), 0)
                    - lax.broadcasted_iota(jnp.int32, (rows, rows), 1)
                    + (at - start)
                )
                same = (distance >= 0) & (segment == along_seg[:, pl.ds(start, rows)])
                decay = jnp.exp(
                    rate_ref[h : h + 1, :1] * jnp.maximum(distance, 0).astype(WIDE)
                )
                scores[h, k, :, m * rows : (m + 1) * rows] = (
                    raw * jnp.where(same, decay, 0.0)
                ).astype(LOW)
        return carry

    lax.fori_loop(0, members, score, 0)
    finish(grad_kept)
    for k in range(1, members):
        near[2 + k].wait_recv()
    finish(turned_kept)
    turn_over(mid)
    turned_kept = keep(turned, grad_turned)
    grad_kept = keep(mid, grad_all)

    column = lax.broadcasted_iota(jnp.int32, (rows, value_columns), 1)

    def by_head(parts_of):
        result = parts_of[0]
        for h in range(1, heads):
            result = jnp.where(column < h * VAL, result, parts_of[h])
        return result

    def head_mean(value):
        means = []
        for h in range(heads):
            inside = (column >= h * VAL) & (column < (h + 1) * VAL)
            total = jnp.sum(jnp.where(inside, value, 0.0), axis=-1, keepdims=True)
            means.append(total * (1.0 / VAL))
        return by_head(means)

    def make_values(k, carry):
        values[k] = jnp.dot(normed[k], flat(wide_one), preferred_element_type=WIDE).astype(LOW)
        return carry

    stage(2, wide_one, make_values)
    keep(values, values_out)

    def retain(k, carry):
        every = values[...].reshape(members * rows, value_columns)
        retained[k] = by_head(
            [
                jnp.dot(scores[h, k], every, preferred_element_type=WIDE)
                for h in range(heads)
            ]
        )
        return carry

    lax.fori_loop(0, members, retain, 0)
    retained_kept = keep(retained, retained_out)

    def make_mixed(k, carry):
        pre = jnp.dot(normed[k], flat(wide_two), preferred_element_type=WIDE)
        gate[k] = pre
        value = retained[k]
        centred = value - head_mean(value)
        grouped = centred * lax.rsqrt(head_mean(centred * centred) + 1.0)
        mixed[k] = (grouped * (pre / (1.0 + jnp.exp(-pre)))).astype(LOW)
        return carry

    stage(3, wide_two, make_mixed)
    gate_kept = keep(gate, gate_out)
    keep(mixed, mixed_out)

    def project(k, put):
        for p in range(parts):
            columns = slice(p * slice_width, (p + 1) * slice_width)
            put(
                columns,
                lax.dot_general(
                    mixed[k],
                    wide_one[p],
                    (((1,), (1,)), ((), ())),
                    preferred_element_type=WIDE,
                ),
            )

    def put_low(slot):
        def put(columns, value):
            held[slot, :, columns] = value.astype(LOW)

        return put

    def put_sum(columns, value):
        base[:, columns] = value

    pass_on(5, 0)
    complete(4)
    load(4, wide_one, home.at[home.shape[0] - 5])
    finish(grad_kept)
    project(3, put_low(0))
    near_start(6, held.at[0], got.at[0], 1)
    project(2, put_sum)
    pass_on(5, 1)
    near[6].wait_recv()
    held[1] = (base[...] + got[0].astype(WIDE)).astype(LOW)
    near_start(8, held.at[1], got.at[1], 2)
    project(1, put_low(2))
    near_start(7, held.at[2], got.at[2], 1)
    project(0, put_sum)
    pass_on(5, 2)
    start_lines(7)
    near[7].wait_recv()
    base[...] = base[...] + got[2].astype(WIDE) + hidden_ref[...].astype(WIDE)
    pass_on(6, 0)
    near[8].wait_recv()
    resid = base[...] + got[1].astype(WIDE)
    resid_out[...] = resid
    scaled = resid * lax.rsqrt(jnp.mean(resid * resid, axis=-1, keepdims=True) + 1e-06)
    scale_into(mid, scaled, 1)
    near_start(10, mid.at[0], mid.at[2], 2)
    near_start(9, mid.at[0], mid.at[1], 1)
    pass_on(6, 1)
    pass_on(6, 2)
    near[10].wait_recv()
    near_start(11, mid.at[2], mid.at[3], 1)
    complete(5)
    load(5, wide_two, home.at[home.shape[0] - 6])
    near[9].wait_recv()
    near[11].wait_recv()
    finish(retained_kept)
    finish(gate_kept)

    def make_gate(k, carry):
        gate[k] = jnp.dot(mid[k], flat(wide_two), preferred_element_type=WIDE)
        return carry

    lax.fori_loop(0, members, make_gate, 0)
    keep(gate, gate_hidden_out)
    finish(turned_kept)
    turn_over(mid)
    keep(turned, mid_turned)
    pass_on(7, 0)
    pass_on(7, 1)
    pass_on(7, 2)
    complete(6)
    load(6, wide_one, home.at[home.shape[0] - 7])

    def make_hidden(k, carry):
        up = jnp.dot(mid[k], flat(wide_one), preferred_element_type=WIDE)
        retained[k] = up
        pre = gate[k]
        inner = (2.0 / math.pi) ** 0.5 * (pre + 0.044715 * (pre * pre * pre))
        hidden[k] = (0.5 * pre * (1.0 + jnp.tanh(inner)) * up).astype(LOW)
        return carry

    lax.fori_loop(0, members, make_hidden, 0)
    keep(retained, up_hidden_out)
    keep(hidden, hidden_out)
    complete(7)
    for w in range(WEIGHTS):
        for step in sends:
            on_line(w, step, lambda copy: copy.wait_send())
            side_copy(w, step).wait_send()
            if tail:
                tail_copy(w, step).wait_send()
        across[w, 0].wait_send()
        if inner:

            @pl.when((line == 1) | (line == 2))
            def _():
                relay_copy(w).wait_send()

    for copy in gains:
        copy.wait_send()
    for copy in near.values():
        copy.wait_send()
    for slot in list(local):
        finish(slot)


def forward(hidden, grad, gains, cosine, sine, segments, rates, shards, lines, members):
    parts = 2 * lines
    rows, width = hidden.shape
    heads = rates.shape[0]
    key_columns, value_columns = shards[0].shape[1], shards[2].shape[0]
    chunks = [shard.shape if k < 2 else shard.shape[::-1] for k, shard in enumerate(shards)]
    length = rows * members
    blocks = (members, rows)
    turned = (width, length)
    outs = [
        (turned, LOW),
        (blocks + (width,), LOW),
        ((parts, 8, gains.shape[1]), WIDE),
    ]
    outs += [((parts,) + chunk, LOW) for chunk in chunks]
    outs += [
        (blocks + (key_columns,), LOW),
        (blocks + (key_columns,), LOW),
        (blocks + (value_columns,), LOW),
        (blocks + (value_columns,), WIDE),
        (turned, LOW),
        (blocks + (value_columns,), WIDE),
        (blocks + (value_columns,), LOW),
        ((rows, width), WIDE),
        (turned, LOW),
        (blocks + (value_columns,), WIDE),
        (blocks + (value_columns,), WIDE),
        (blocks + (value_columns,), LOW),
    ]
    places = [ANY] * len(outs)
    places[2] = INSIDE
    places[18] = INSIDE
    tags = 12
    return pl.pallas_call(
        functools.partial(forward_kernel, lines, members),
        out_shape=[jax.ShapeDtypeStruct(shape, dtype) for shape, dtype in outs],
        in_specs=[INSIDE, ANY] + [INSIDE] * 6 + [ANY] * WEIGHTS,
        out_specs=places,
        scratch_shapes=[
            pltpu.VMEM(blocks + (width,), LOW),
            pltpu.VMEM(blocks + (width,), LOW),
            pltpu.VMEM((parts,) + chunks[0], LOW),
            pltpu.VMEM((parts,) + chunks[2], LOW),
            pltpu.VMEM((parts,) + chunks[2], LOW),
            pltpu.VMEM(turned, LOW),
            pltpu.VMEM(blocks + (key_columns,), LOW),
            pltpu.VMEM(blocks + (key_columns,), LOW),
            pltpu.VMEM((heads, members, rows, length), LOW),
            pltpu.VMEM(blocks + (value_columns,), LOW),
            pltpu.VMEM(blocks + (value_columns,), WIDE),
            pltpu.VMEM(blocks + (value_columns,), WIDE),
            pltpu.VMEM(blocks + (value_columns,), LOW),
            pltpu.VMEM(blocks + (value_columns,), LOW),
            pltpu.VMEM((3, rows, width), LOW),
            pltpu.VMEM((3, rows, width), LOW),
            pltpu.VMEM((rows, width), WIDE),
            pltpu.SemaphoreType.DMA((WEIGHTS, lines)),
            pltpu.SemaphoreType.DMA((WEIGHTS, lines)),
            pltpu.SemaphoreType.DMA((WEIGHTS, lines)),
            pltpu.SemaphoreType.DMA((WEIGHTS, lines)),
            pltpu.SemaphoreType.DMA((tags,)),
            pltpu.SemaphoreType.DMA((tags,)),
            pltpu.SemaphoreType.DMA((parts,)),
            pltpu.SemaphoreType.DMA((parts,)),
            pltpu.SemaphoreType.DMA((40,)),
            pltpu.SemaphoreType.DMA((WEIGHTS, lines)),
            pltpu.SemaphoreType.DMA((WEIGHTS, lines)),
            pltpu.VMEM((8, gains.shape[1]), WIDE),
            pltpu.VMEM(shards[2].shape, LOW),
            pltpu.VMEM(shards[2].shape[::-1], LOW),
        ],
        compiler_params=pltpu.CompilerParams(
            collective_id=0, has_side_effects=True, vmem_limit_bytes=ROOM
        ),
        cost_estimate=pl.CostEstimate(
            flops=10**11, bytes_accessed=10**9, transcendentals=0
        ),
        name="forward",
    )(hidden, grad, gains, cosine, sine, segments.T, segments, rates, *shards)


def tail_rows(rows, lines, sixteenths):
    return rows * sixteenths // 16 // 16 * 16 if lines == 4 else 0


class Scatter:
    def __init__(self, lines, held, far_got, near_got, tail_got, spare, tails, sixteenths, sems):
        self.lines = lines
        self.held, self.far_got, self.near_got, self.spare = held, far_got, near_got, spare
        self.tail_got, self.tails = tail_got, tails
        self.side_send, self.side_recv, self.line_send, self.line_recv = sems[:4]
        self.tail_send, self.tail_recv, self.home = sems[4:]
        self.rows = held[0].shape[1]
        self.tail = tail_rows(self.rows, lines, sixteenths)
        self.most = self.rows - self.tail
        me = lax.axis_index("dp")
        self.line, self.side = me // 2, lax.rem(me, 2)
        self.opposite = {"dp": 2 * self.line + (1 - self.side)}

    def peer(self, step):
        return {"dp": 2 * lax.rem(self.line + step, self.lines) + self.side}

    def peers(self):
        return [self.opposite] + [self.peer(step) for step in range(1, self.lines)]

    def far_copy(self, w, place):
        return remote(
            self.held[w].at[place, pl.ds(0, self.most)],
            self.far_got[w].at[place, pl.ds(0, self.most)],
            self.side_send.at[w, place],
            self.side_recv.at[w, place],
            self.opposite,
        )

    def near_copy(self, w, step):
        place = lax.rem(self.line + step, self.lines)
        return remote(
            self.held[w].at[place],
            self.near_got[w].at[step],
            self.line_send.at[w, step],
            self.line_recv.at[w, step],
            self.peer(step),
        )

    def fetch(self, source):
        rows, columns = source.shape
        spare = self.spare[columns].at[pl.ds(0, rows)]
        copy = pltpu.make_async_copy(source, spare, self.home)
        copy.start()
        copy.wait()
        return spare[...].astype(WIDE)


    def tail_copy(self, w, step):
        place = lax.rem(self.line + step, self.lines)
        return remote(
            self.held[w].at[place, pl.ds(self.most, self.tail)],
            self.tail_got[w].at[step],
            self.tail_send.at[w, step],
            self.tail_recv.at[w, step],
            self.peer(step),
        )

    def tail_across(self, w):
        return remote(
            self.tails[w],
            self.tail_got[w].at[0],
            self.tail_send.at[w, 0],
            self.tail_recv.at[w, 0],
            self.opposite,
        )

    def add_tails(self, w):
        total = self.held[w][self.line, self.most :].astype(WIDE)
        for step in range(1, self.lines):
            self.tail_copy(w, step).wait_recv()
            total = total + self.fetch(self.tail_got[w].at[step])
        self.tails[w][...] = total.astype(LOW)
        self.tail_across(w).start()

    def product(self, left, right, place):
        rows = self.held[0].shape[1]
        block = left[pl.ds(pl.multiple_of(place * rows, rows), rows), :]
        every = right[...]
        return jnp.dot(
            block,
            every.reshape(every.shape[0] * every.shape[1], every.shape[2]),
            preferred_element_type=WIDE,
        )


    def extra_copy(self, w, step):
        place = lax.rem(self.line + step, self.lines)
        return remote(
            self.held[w].at[place],
            self.far_got[w].at[self.lines],
            self.line_send.at[w, step],
            self.line_recv.at[w, 0],
            {"dp": 2 * (2 if step == 1 else 1) + self.side},
        )

    def far(self, w, left, right):
        def body(at, carry):
            step = 1 + at
            if self.lines == 4:
                step = 1 + 2 * at - 3 * (at // 2)
            place = lax.rem(self.line + step, self.lines)
            other = (1 - self.side) * self.lines + place
            self.held[w][place] = self.product(left, right, other).astype(LOW)
            self.far_copy(w, place).start()
            if self.tail:

                @pl.when(at < self.lines - 1)
                def _():
                    self.tail_copy(w, step).start()

            return carry

        lax.fori_loop(0, self.lines, body, 0)

    def near(self, w, left, right, quarter):
        def put(place, step):
            part = self.product(left, right, self.side * self.lines + place)
            self.far_copy(w, place).wait_recv()
            got = self.fetch(self.far_got[w].at[place, pl.ds(0, self.most)])
            self.far_copy(w, place).wait_send()
            if self.tail and step is not None:
                self.tail_copy(w, step).wait_send()
            self.held[w][place, : self.most] = (part[: self.most] + got).astype(LOW)
            if self.tail:
                self.held[w][place, self.most :] = part[self.most :].astype(LOW)

        def body(step, carry):
            place = lax.rem(self.line + step, self.lines)
            put(place, step)
            self.near_copy(w, step).start()
            return carry

        if self.lines != 4:
            first, last = [1 + (quarter + k) * self.lines // 4 for k in range(2)]
            lax.fori_loop(first, min(last, self.lines), body, 0)
        elif quarter < 2:
            step = 1 + 2 * quarter
            end = 3 - 3 * quarter
            place = lax.rem(self.line + step, self.lines)
            put(place, step)

            @pl.when(self.line == end)
            def _():
                self.extra_copy(w, step).start()

            @pl.when(self.line != end)
            def _():
                self.near_copy(w, step).start()
        elif quarter == 2:
            place = lax.rem(self.line + 2, self.lines)
            put(place, 2)

            @pl.when((self.line == 1) | (self.line == 2))
            def _():
                self.extra_copy(w, 1).wait_recv()
                self.held[w][place] = (
                    self.held[w][place].astype(WIDE)
                    + self.fetch(self.far_got[w].at[self.lines])
                ).astype(LOW)

            self.near_copy(w, 2).start()
        if quarter < 3:
            return
        if self.tail:
            self.add_tails(w)
        put(self.line, None)
        if not self.tail:
            self.own_copy(w).start()
        if self.lines == 4:

            @pl.when((self.line == 0) | (self.line == 3))
            def _():
                spare = self.spare[self.held[w].shape[2]]
                spare[...] = jnp.zeros(spare.shape, LOW)
                slot = 1 + 2 * (self.line // 3)
                copy = pltpu.make_async_copy(spare, self.near_got[w].at[slot], self.home)
                copy.start()
                copy.wait()

    def own_copy(self, w):
        return pltpu.make_async_copy(
            self.held[w].at[self.line], self.near_got[w].at[0], self.line_send.at[w, 0]
        )

    def finish(self, w):
        if self.lines != 4:

            def body(step, carry):
                self.near_copy(w, step).wait()
                return carry

            lax.fori_loop(1, self.lines, body, 0)
        else:
            for step in range(1, 4):
                copy = self.near_copy(w, step)
                copy.wait_send()
                if step == 2:
                    copy.wait_recv()
                else:

                    @pl.when(self.line != (0 if step == 1 else 3))
                    def _():
                        copy.wait_recv()

        if self.tail:
            self.tail_across(w).wait()
            self.held[w][self.line, self.most :] = (
                self.held[w][self.line, self.most :].astype(WIDE)
                + self.fetch(self.tail_got[w].at[0])
            ).astype(LOW)
            self.own_copy(w).start()
        self.own_copy(w).wait()


class Near:
    def __init__(self, send, recv):
        self.send, self.recv = send, recv
        self.flight = {}
        own = lax.axis_index("tensor")
        half, rest = own // 2, lax.rem(own, 2)
        self.member = lambda k: 2 * lax.rem(half + k // 2, 2) + lax.rem(rest + lax.rem(k, 2), 2)

    def partners(self, members):
        return [{"tensor": self.member(k)} for k in range(1, members)]

    def start(self, tag, source, target, k):
        copy = remote(source, target, self.send.at[tag], self.recv.at[tag], self.partners(4)[k - 1])
        copy.start()
        self.flight[tag] = copy

    def wait(self, tag):
        self.flight[tag].wait_recv()

    def sent(self, tag):
        self.flight[tag].wait_send()


def dot_across(left, right):
    return lax.dot_general(
        left, right, (((1,), (1,)), ((), ())), preferred_element_type=WIDE
    )


def feed_kernel(lines, members, *refs):
    grad_turned, hidden, gain_all = refs[:3]
    later = refs[3:9]
    gate_hidden, up_hidden = refs[9:11]
    near_got, mid_all, mid_grad_out, hidden_out, gain_out = refs[11:14], *refs[14:18]
    mid_low_turned = refs[18]
    far_got, tail_got = refs[19:22], refs[22:25]
    gate_low, up_low, pre, up = refs[25:29]
    scatter_held = refs[29:32]
    spare, held, got, last, base, mid = refs[32:38]
    sems = refs[38:44]
    near_send, near_recv, home, column = refs[44:48]
    loaded, tails = refs[48:54], refs[54:]
    grad_ref, mid_turned, resid_ref, gate_weight, up_weight, down_weight = loaded
    parts = 2 * lines
    rows, width = resid_ref.shape
    loads = []
    for k, order in enumerate((5, 0, 1, 3, 4, 2)):
        loads.append(pltpu.make_async_copy(later[order], loaded[order], home.at[4 + k]))
        loads[k].start()
    slice_width = width // parts
    scatter = Scatter(
        lines,
        scatter_held,
        far_got,
        near_got,
        tail_got,
        {spare.shape[1]: spare},
        tails,
        3,
        sems + (home.at[0],),
    )
    near = Near(near_send, near_recv)
    greet(scatter.peers() + near.partners(members))
    scatter.far(0, grad_turned, hidden)

    def flat(ref):
        return ref[...].reshape(width, ref.shape[2])

    def pull(k, carry):
        first = pltpu.make_async_copy(gate_hidden.at[k], pre, home.at[1])
        second = pltpu.make_async_copy(up_hidden.at[k], up, home.at[2])
        first.start()
        second.start()
        grad = jnp.dot(grad_ref[k], flat(down_weight), preferred_element_type=WIDE)
        first.wait()
        second.wait()
        value = pre[...]
        root = (2.0 / math.pi) ** 0.5
        square = value * value
        lift = jnp.tanh(root * (value + 0.044715 * (value * square)))
        ramp = 0.5 * (1.0 + lift)
        slope = ramp + 0.5 * value * (1.0 - lift * lift) * root * (1.0 + 0.134145 * square)
        gate_low[k] = (grad * up[...] * slope).astype(LOW)
        up_low[k] = (grad * (value * ramp)).astype(LOW)
        return carry

    for load in loads:
        load.wait()
    lax.fori_loop(0, members // 2, pull, 0)
    scatter.near(0, grad_turned, hidden, 0)
    lax.fori_loop(members // 2, members, pull, 0)
    scatter.near(0, grad_turned, hidden, 1)
    scatter.far(1, mid_turned, gate_low)

    def back(k, put):
        for p in range(parts):
            columns = slice(p * slice_width, (p + 1) * slice_width)
            put(
                columns,
                dot_across(gate_low[k], gate_weight[p]) + dot_across(up_low[k], up_weight[p]),
            )

    def put_low(slot):
        def put(columns, value):
            held[slot, :, columns] = value.astype(LOW)

        return put

    def put_sum(columns, value):
        base[:, columns] = value

    back(3, put_low(0))
    near.start(0, held.at[0], got.at[0], 1)
    scatter.near(0, grad_turned, hidden, 2)
    back(2, put_sum)
    near.wait(0)
    near.sent(0)
    held[0] = (base[...] + got[0].astype(WIDE)).astype(LOW)
    near.start(1, held.at[0], got.at[1], 2)
    back(1, put_low(1))
    near.start(2, held.at[1], got.at[2], 1)
    scatter.near(0, grad_turned, hidden, 3)
    back(0, put_sum)
    scatter.far(2, mid_turned, up_low)
    scatter.near(1, mid_turned, gate_low, 0)
    near.wait(2)
    base[...] += got[2].astype(WIDE)
    scatter.near(1, mid_turned, gate_low, 1)
    near.wait(1)
    normed_grad = base[...] + got[1].astype(WIDE)
    resid = resid_ref[...]
    scale = lax.rsqrt(jnp.mean(resid * resid, axis=-1, keepdims=True) + 1e-06)
    unit = resid * scale
    base[...] = normed_grad * unit
    gain_out[...] = jnp.broadcast_to(
        jnp.sum(base[...], axis=0, keepdims=True), gain_out.shape
    )
    dot = jnp.zeros((rows, 1), WIDE)
    for p in range(parts):
        columns = slice(p * slice_width, (p + 1) * slice_width)
        dot += jnp.sum(base[:, columns] * gain_all[p][1:2], axis=-1, keepdims=True)
    dot = dot * (1.0 / width)
    base[...] = normed_grad
    for p in range(parts):
        columns = slice(p * slice_width, (p + 1) * slice_width)
        block = resid_ref[:, columns] * scale
        mid_grad = grad_ref[0, :, columns].astype(WIDE) + scale * (
            base[:, columns] * gain_all[p][1:2] - block * dot
        )
        base[:, columns] = mid_grad
        mid[:, columns] = mid_grad.astype(LOW)
    mid_grad_copy = pltpu.make_async_copy(base, mid_grad_out, home.at[1])
    mid_grad_copy.start()
    near.start(3, mid, mid_all.at[2], 2)
    near.start(4, mid, mid_all.at[1], 1)
    own = pltpu.make_async_copy(mid, mid_all.at[0], home.at[3])
    own.start()
    scatter.near(1, mid_turned, gate_low, 2)
    scatter.near(1, mid_turned, gate_low, 3)

    def down(k, put):
        for p in range(parts):
            columns = slice(p * slice_width, (p + 1) * slice_width)
            put(columns, dot_across(hidden[k], down_weight[p]))

    near.sent(1)
    near.sent(2)
    down(3, put_low(0))
    mid_grad_copy.wait()
    near.start(6, held.at[0], last.at[0], 1)
    down(2, put_sum)
    scatter.near(2, mid_turned, up_low, 0)
    near.wait(3)
    near.start(5, mid_all.at[2], mid_all.at[3], 1)
    near.wait(6)
    near.sent(6)
    held[0] = (base[...] + last[0].astype(WIDE)).astype(LOW)
    near.start(7, held.at[0], last.at[1], 2)
    down(1, put_low(1))
    near.start(8, held.at[1], last.at[2], 1)
    scatter.near(2, mid_turned, up_low, 1)
    down(0, put_sum)
    own.wait()
    near.wait(4)
    near.wait(5)
    for k in range(members):
        copy = pltpu.make_async_copy(mid_all.at[k], got.at[0], home.at[9])
        copy.start()
        copy.wait()
        if k:
            turned_copy.wait()
        for c in range(width // 256):
            block = slice(c * 256, (c + 1) * 256)
            column[block, :] = got[0, :, block].T
        turned_copy = pltpu.make_async_copy(
            column, mid_low_turned.at[:, pl.ds(k * rows, rows)], home.at[10]
        )
        turned_copy.start()
    turned_copy.wait()
    scatter.near(2, mid_turned, up_low, 2)
    scatter.finish(0)
    scatter.finish(1)
    scatter.near(2, mid_turned, up_low, 3)
    near.wait(8)
    near.wait(7)
    near.sent(3)
    near.sent(4)
    for p in range(parts):
        columns = slice(p * slice_width, (p + 1) * slice_width)
        value = base[:, columns] + last[2, :, columns].astype(WIDE)
        value = value + last[1, :, columns].astype(WIDE) + resid_ref[:, columns]
        start = (2 * (p % lines) + p // lines) * slice_width
        mid[:, start : start + slice_width] = value.astype(LOW)
    own = pltpu.make_async_copy(mid, hidden_out, home.at[3])
    own.start()
    own.wait()
    near.sent(5)
    near.sent(7)
    near.sent(8)
    scatter.finish(2)


def feed_backward(
    grad, grad_turned, mid_turned, hidden, resid, gains, weights, pres, lines, members
):
    parts = 2 * lines
    rows, width = resid.shape
    columns = hidden.shape[2]
    slice_width = width // parts
    blocks = (members, rows)
    piece = (lines, slice_width, columns)
    later = [grad, mid_turned, resid, *weights]
    outs = [(piece, LOW)] * 3
    outs += [
        (blocks + (width,), LOW),
        ((rows, width), WIDE),
        ((rows, width), LOW),
        ((8, width), WIDE),
        ((width, rows * members), LOW),
    ]
    outs += [((lines + 1,) + piece[1:], LOW)] * 3
    tail = max(tail_rows(slice_width, lines, 3), 16)
    outs += [((lines, tail, columns), LOW)] * 3
    return pl.pallas_call(
        functools.partial(feed_kernel, lines, members),
        out_shape=[jax.ShapeDtypeStruct(shape, dtype) for shape, dtype in outs],
        in_specs=[INSIDE] * 3 + [ANY] * 8,
        out_specs=[ANY] * 6 + [INSIDE] + [ANY] * 7,
        scratch_shapes=[
            pltpu.VMEM(blocks + (columns,), LOW),
            pltpu.VMEM(blocks + (columns,), LOW),
            pltpu.VMEM((rows, columns), WIDE),
            pltpu.VMEM((rows, columns), WIDE),
            pltpu.VMEM(piece, LOW),
            pltpu.VMEM(piece, LOW),
            pltpu.VMEM(piece, LOW),
            pltpu.VMEM(piece[1:], LOW),
            pltpu.VMEM((2, rows, width), LOW),
            pltpu.VMEM((3, rows, width), LOW),
            pltpu.VMEM((3, rows, width), LOW),
            pltpu.VMEM((rows, width), WIDE),
            pltpu.VMEM((rows, width), LOW),
            pltpu.SemaphoreType.DMA((3, lines)),
            pltpu.SemaphoreType.DMA((3, lines)),
            pltpu.SemaphoreType.DMA((3, lines)),
            pltpu.SemaphoreType.DMA((3, lines)),
            pltpu.SemaphoreType.DMA((3, lines)),
            pltpu.SemaphoreType.DMA((3, lines)),
            pltpu.SemaphoreType.DMA((9,)),
            pltpu.SemaphoreType.DMA((9,)),
            pltpu.SemaphoreType.DMA((11,)),
            pltpu.VMEM((width, rows), LOW),
        ]
        + [pltpu.VMEM(value.shape, value.dtype) for value in later]
        + [pltpu.VMEM((tail, columns), LOW)] * 3,
        compiler_params=pltpu.CompilerParams(
            collective_id=1, has_side_effects=True, vmem_limit_bytes=ROOM
        ),
        cost_estimate=pl.CostEstimate(flops=10**11, bytes_accessed=10**9, transcendentals=0),
        name="feed_backward",
    )(grad_turned, hidden, gains, *later, *pres)[:8]


def retention_kernel(lines, members, *refs):
    later = refs[:6]
    cos_ref, sin_ref, down_seg, along_seg, rate_ref = refs[6:11]
    hidden_ref, gain_all, gain_part = refs[11:14]
    mid_grad_ref, mid_all, retained_all, gate_all = refs[14:18]
    weights = refs[18:23]
    near_got, in_grad_out, gain_out = refs[23:28], refs[28], refs[29]
    far_got, tail_got = refs[30:35], refs[35:40]
    wide_one, wide_two, short_one, short_two = refs[40:44]
    gate_low, retained_low, query_low, key_low = refs[44:48]
    scatter_held = refs[48:53]
    spare_wide, spare_short, held, got, base, retained, gate = refs[53:60]
    pieces, piece_got, total, total_got = refs[60:64]
    sems = refs[64:70]
    near_send, near_recv, gain_send, gain_recv, home = refs[70:75]
    loaded, tails = refs[75:81], refs[81:]
    mixed, normed_turned, query, keys, values, turned = loaded
    value_low = mixed
    parts = 2 * lines
    rows, width = hidden_ref.shape
    slice_width = width // parts
    heads = rate_ref.shape[0]
    value_columns = values.shape[2]
    length = rows * members
    scatter = Scatter(
        lines,
        scatter_held,
        far_got,
        near_got,
        tail_got,
        {spare_wide.shape[1]: spare_wide, spare_short.shape[1]: spare_short},
        tails,
        2,
        sems + (home.at[0],),
    )
    near = Near(near_send, near_recv)
    me = lax.axis_index("dp")
    here = scatter.side * lines + scatter.line
    others = [{"dp": lax.rem(me + k, parts)} for k in range(1, parts)]
    greet(others + near.partners(members))

    def fetch(source, target, sem):
        copy = pltpu.make_async_copy(source, target, home.at[sem])
        copy.start()
        return copy

    loads = [fetch(later[k], loaded[k], 9 + k) for k in (5, 0)]
    out_copy = fetch(weights[0], wide_one, 1)
    loads += [fetch(later[k], loaded[k], 9 + k) for k in range(1, 5)]
    value_copy = fetch(weights[2], wide_two, 2)
    query_copy = fetch(weights[3], short_one, 3)
    key_copy = fetch(weights[4], short_two, 4)
    grad_copy = fetch(mid_grad_ref, in_grad_out, 7)
    loads[0].wait()
    loads[1].wait()
    scatter.far(0, turned, mixed)
    out_copy.wait()
    for load in loads[2:]:
        load.wait()

    column = lax.broadcasted_iota(jnp.int32, (rows, value_columns), 1)

    def by_head(parts_of):
        result = parts_of[0]
        for h in range(1, heads):
            result = jnp.where(column < h * VAL, result, parts_of[h])
        return result

    def inside(h):
        return (column >= h * VAL) & (column < (h + 1) * VAL)

    def head_mean(value):
        return by_head(
            [
                jnp.sum(jnp.where(inside(h), value, 0.0), axis=-1, keepdims=True) * (1.0 / VAL)
                for h in range(heads)
            ]
        )

    def unmix(k, carry):
        first = fetch(retained_all.at[k], retained, 5)
        second = fetch(gate_all.at[k], gate, 6)
        fetch(mid_all.at[k], held.at[0], 8).wait()
        grad = jnp.dot(
            held[0],
            wide_one[...].reshape(width, value_columns),
            preferred_element_type=WIDE,
        )
        first.wait()
        second.wait()
        value = retained[...]
        centred = value - head_mean(value)
        rate = lax.rsqrt(head_mean(centred * centred) + 1.0)
        pre = gate[...]
        sigma = 1.0 / (1.0 + jnp.exp(-pre))
        gate_low[k] = (
            grad * (centred * rate) * (sigma * (1.0 + pre * (1.0 - sigma)))
        ).astype(LOW)
        grouped_grad = grad * (pre * sigma)
        retained_low[k] = (
            rate * (grouped_grad - head_mean(grouped_grad))
            - (rate * rate * rate) * centred * head_mean(grouped_grad * centred)
        ).astype(LOW)
        return carry

    lax.fori_loop(0, members // 2, unmix, 0)
    scatter.near(0, turned, mixed, 0)
    lax.fori_loop(members // 2, members, unmix, 0)
    scatter.near(0, turned, mixed, 1)
    scatter.far(1, normed_turned, gate_low)
    gate_copy = fetch(weights[1], wide_one, 1)

    def decay(h, late, early, late_segment, early_segment, turn):
        sign = -1 if turn else 1
        distance = (
            sign
            * (
                lax.broadcasted_iota(jnp.int32, (rows, rows), 0)
                - lax.broadcasted_iota(jnp.int32, (rows, rows), 1)
            )
            + (late - early)
        )
        same = (distance >= 0) & (late_segment == early_segment)
        return jnp.where(
            same,
            jnp.exp(rate_ref[h : h + 1, :1] * jnp.maximum(distance, 0).astype(WIDE)),
            0.0,
        )

    def start_of(k):
        return pl.multiple_of(near.member(k) * rows, rows)

    wing = KEY // 2
    along = [along_seg[:, pl.ds(start_of(k), rows)] for k in range(members)]

    def turn_back(target, k, h, grad, scale):
        at = pl.ds(pl.multiple_of(k * rows, rows), rows)
        cosine, sine = cos_ref[at, :], sin_ref[at, :]
        first, second = grad[:, :wing], grad[:, wing:]
        target[k, :, h * KEY : h * KEY + wing] = (
            (first * cosine + second * sine) * scale
        ).astype(LOW)
        target[k, :, h * KEY + wing : (h + 1) * KEY] = (
            (second * cosine - first * sine) * scale
        ).astype(LOW)

    def early_side(m, carry):
        early = start_of(m)
        early_segment = down_seg[pl.ds(early, rows), :]
        value_grads = []
        for h in range(heads):
            head = slice(h * KEY, (h + 1) * KEY)
            masked = jnp.where(inside(h), values[m].astype(WIDE), 0.0).astype(LOW)
            value_grad = jnp.zeros((rows, value_columns), WIDE)
            key_grad = jnp.zeros((rows, KEY), WIDE)
            for n in range(members):
                late = start_of(n)
                late_segment = along[n]
                mask = decay(h, late, early, late_segment, early_segment, True)
                score = (dot_across(keys[m, :, head], query[n, :, head]) * mask).astype(LOW)
                raw = (dot_across(masked, retained_low[n]) * mask).astype(LOW)
                value_grad += jnp.dot(score, retained_low[n], preferred_element_type=WIDE)
                key_grad += jnp.dot(raw, query[n, :, head], preferred_element_type=WIDE)
            value_grads.append(value_grad)
            turn_back(key_low, m, h, key_grad, 1.0)
        value_low[m] = by_head(value_grads).astype(LOW)
        return carry

    scatter.near(0, turned, mixed, 2)
    scatter.near(0, turned, mixed, 3)
    early_side(0, 0)
    early_side(1, 0)
    scatter.near(1, normed_turned, gate_low, 0)
    early_side(2, 0)
    early_side(3, 0)
    scatter.far(2, normed_turned, value_low)
    scatter.near(1, normed_turned, gate_low, 1)
    scatter.near(1, normed_turned, gate_low, 2)
    scatter.far(4, normed_turned, key_low)
    scatter.near(1, normed_turned, gate_low, 3)

    def late_side(n, carry):
        late = start_of(n)
        late_segment = down_seg[pl.ds(late, rows), :]
        for h in range(heads):
            head = slice(h * KEY, (h + 1) * KEY)
            masked = jnp.where(inside(h), retained_low[n].astype(WIDE), 0.0).astype(LOW)
            query_grad = jnp.zeros((rows, KEY), WIDE)
            for m in range(members):
                early = start_of(m)
                early_segment = along[m]
                mask = decay(h, late, early, late_segment, early_segment, False)
                raw = (dot_across(masked, values[m]) * mask).astype(LOW)
                query_grad += jnp.dot(raw, keys[m, :, head], preferred_element_type=WIDE)
            turn_back(query_low, n, h, query_grad, KEY ** (-0.5))
        return carry

    lax.fori_loop(0, members // 2, late_side, 0)
    scatter.near(2, normed_turned, value_low, 0)
    lax.fori_loop(members // 2, members, late_side, 0)
    scatter.near(2, normed_turned, value_low, 1)
    scatter.far(3, normed_turned, query_low)
    for copy in (gate_copy, value_copy, query_copy, key_copy, grad_copy):
        copy.wait()

    def back(k, put):
        for p in range(parts):
            columns = slice(p * slice_width, (p + 1) * slice_width)
            put(
                columns,
                dot_across(gate_low[k], wide_one[p])
                + dot_across(value_low[k], wide_two[p])
                + dot_across(query_low[k], short_one[p])
                + dot_across(key_low[k], short_two[p]),
            )

    def put_low(slot):
        def put(columns, value):
            held[slot, :, columns] = value.astype(LOW)

        return put

    def put_sum(columns, value):
        base[:, columns] = value

    back(3, put_low(0))
    near.start(0, held.at[0], got.at[0], 1)
    back(2, put_sum)
    scatter.near(2, normed_turned, value_low, 2)
    near.wait(0)
    near.sent(0)
    held[0] = (base[...] + got[0].astype(WIDE)).astype(LOW)
    near.start(1, held.at[0], got.at[1], 2)
    back(1, put_low(1))
    near.start(2, held.at[1], got.at[2], 1)
    scatter.near(2, normed_turned, value_low, 3)
    back(0, put_sum)
    for quarter in range(4):
        scatter.near(4, normed_turned, key_low, quarter)
    near.wait(2)
    base[...] += got[2].astype(WIDE)
    near.wait(1)
    normed_grad = base[...] + got[1].astype(WIDE)
    base[...] = normed_grad
    resid = hidden_ref[...].astype(WIDE)
    scale = lax.rsqrt(jnp.mean(resid * resid, axis=-1, keepdims=True) + 1e-06)
    dot = jnp.zeros((rows, 1), WIDE)
    for p in range(parts):
        columns = slice(p * slice_width, (p + 1) * slice_width)
        product = base[:, columns] * (hidden_ref[:, columns].astype(WIDE) * scale)
        row = lax.broadcasted_iota(jnp.int32, (8, slice_width), 0)
        pieces[p] = jnp.where(
            row == 0, jnp.sum(product, axis=0, keepdims=True), gain_part[:, columns]
        )
        dot += jnp.sum(product * gain_all[p][0:1], axis=-1, keepdims=True)
    dot = dot * (1.0 / width)
    gains = []
    for k in range(1, parts):
        other = lax.rem(me + k, parts)
        place = lax.rem(other, 2) * lines + other // 2
        copy = remote(
            pieces.at[place], piece_got.at[k], gain_send.at[k], gain_recv.at[k], others[k - 1]
        )
        copy.start()
        gains.append(copy)
    for p in range(parts):
        columns = slice(p * slice_width, (p + 1) * slice_width)
        block = hidden_ref[:, columns].astype(WIDE) * scale
        base[:, columns] = in_grad_out[:, columns] + scale * (
            base[:, columns] * gain_all[p][0:1] - block * dot
        )
    for p in range(parts):
        start = (2 * (p % lines) + p // lines) * slice_width
        in_grad_out[:, start : start + slice_width] = base[
            :, p * slice_width : (p + 1) * slice_width
        ]
    value = pieces[here]
    for k in range(1, parts):
        gains[k - 1].wait_recv()
        value = value + piece_got[k]
    total[...] = value
    for k in range(1, members):
        near.start(2 + k, total, total_got.at[k], k)
    scatter.near(3, normed_turned, query_low, 0)
    scatter.finish(0)
    scatter.near(3, normed_turned, query_low, 1)
    scatter.finish(1)
    scatter.near(3, normed_turned, query_low, 2)
    scatter.finish(2)
    scatter.finish(4)
    scatter.near(3, normed_turned, query_low, 3)
    scatter.finish(3)
    for k in range(1, members):
        near.wait(2 + k)
        value = value + total_got[k]
    gain_out[...] = value
    for tag in range(1, 2 + members):
        near.sent(tag)
    for copy in gains:
        copy.wait_send()


def retention_backward(inside, streamed, weights, lines, members, slice_width):
    parts = 2 * lines
    rows, width = inside[11].shape
    blocks = (members, rows)
    wide, short = weights[0].shape[2], weights[3].shape[2]
    widths = [wide, wide, wide, short, short]
    pieces = [(lines, slice_width, columns) for columns in widths]
    outs = [(piece, LOW) for piece in pieces]
    outs += [((rows, width), WIDE), ((8, slice_width), WIDE)]
    outs += [((lines + 1,) + piece[1:], LOW) for piece in pieces]
    tail = max(tail_rows(slice_width, lines, 2), 16)
    outs += [((lines, tail, columns), LOW) for columns in widths]
    return pl.pallas_call(
        functools.partial(retention_kernel, lines, members),
        out_shape=[jax.ShapeDtypeStruct(shape, dtype) for shape, dtype in outs],
        in_specs=[ANY] * 6 + [INSIDE] * 8 + [ANY] * 9,
        out_specs=[ANY] * 5 + [INSIDE] * 2 + [ANY] * 10,
        scratch_shapes=[
            pltpu.VMEM(weights[0].shape, LOW),
            pltpu.VMEM(weights[0].shape, LOW),
            pltpu.VMEM(weights[3].shape, LOW),
            pltpu.VMEM(weights[3].shape, LOW),
            pltpu.VMEM(blocks + (wide,), LOW),
            pltpu.VMEM(blocks + (wide,), LOW),
            pltpu.VMEM(blocks + (short,), LOW),
            pltpu.VMEM(blocks + (short,), LOW),
        ]
        + [pltpu.VMEM(piece, LOW) for piece in pieces]
        + [
            pltpu.VMEM((slice_width, wide), LOW),
            pltpu.VMEM((slice_width, short), LOW),
            pltpu.VMEM((2, rows, width), LOW),
            pltpu.VMEM((3, rows, width), LOW),
            pltpu.VMEM((rows, width), WIDE),
            pltpu.VMEM((rows, wide), WIDE),
            pltpu.VMEM((rows, wide), WIDE),
            pltpu.VMEM((parts, 8, slice_width), WIDE),
            pltpu.VMEM((parts, 8, slice_width), WIDE),
            pltpu.VMEM((8, slice_width), WIDE),
            pltpu.VMEM((members, 8, slice_width), WIDE),
            pltpu.SemaphoreType.DMA((5, lines)),
            pltpu.SemaphoreType.DMA((5, lines)),
            pltpu.SemaphoreType.DMA((5, lines)),
            pltpu.SemaphoreType.DMA((5, lines)),
            pltpu.SemaphoreType.DMA((5, lines)),
            pltpu.SemaphoreType.DMA((5, lines)),
            pltpu.SemaphoreType.DMA((6,)),
            pltpu.SemaphoreType.DMA((6,)),
            pltpu.SemaphoreType.DMA((parts,)),
            pltpu.SemaphoreType.DMA((parts,)),
            pltpu.SemaphoreType.DMA((15,)),
        ]
        + [pltpu.VMEM(value.shape, value.dtype) for value in inside[:6]]
        + [pltpu.VMEM((tail, columns), LOW) for columns in widths],
        compiler_params=pltpu.CompilerParams(
            collective_id=2, has_side_effects=True, vmem_limit_bytes=ROOM
        ),
        cost_estimate=pl.CostEstimate(flops=10**11, bytes_accessed=10**9, transcendentals=0),
        name="retention_backward",
    )(*inside, *streamed, *weights)[:7]


def on_device(
    hidden_in,
    out_grad,
    segment_ids,
    norm1_gain,
    w_query,
    w_key,
    w_value,
    w_gate,
    w_out,
    norm2_gain,
    w_mlp_gate,
    w_mlp_up,
    w_mlp_down,
):
    _, rows, width = hidden_in.shape
    parts = lax.axis_size("dp")
    lines = parts // 2
    slice_width = width // parts
    own = lax.axis_index("tensor")
    members = lax.axis_size("tensor")
    order = list(range(0, parts, 2)) + list(range(1, parts, 2))

    def to_places(value):
        blocks = [value[:, k * slice_width : (k + 1) * slice_width] for k in order]
        return jnp.concatenate(blocks, axis=1)

    heads_here = w_query.shape[1] // KEY
    resid_low = to_places(hidden_in.reshape(rows, width))
    grad_local = to_places(out_grad.reshape(rows, width))
    gain_rows = jnp.stack([norm1_gain, norm2_gain])
    position = jnp.concatenate(
        [(own ^ k) * rows + jnp.arange(rows, dtype=jnp.int32) for k in range(members)]
    )
    cosine, sine = rotary_tables(position, KEY)
    head_numbers = (jnp.arange(heads_here, dtype=jnp.int32) + own * heads_here).astype(WIDE)
    rates = jnp.log1p(-jnp.exp2(-5.0 - head_numbers))
    rates = jnp.broadcast_to(rates[:, None], (heads_here, 128))
    outs = forward(
        resid_low,
        grad_local,
        gain_rows,
        cosine,
        sine,
        segment_ids,
        rates,
        [w_query, w_key, w_value.T, w_gate.T, w_out, w_mlp_gate.T, w_mlp_up.T, w_mlp_down],
        lines,
        members,
    )
    normed_turned, grad_full, gains = outs[:3]
    query_weight, key_weight, value_weight, gate_weight, out_weight = outs[3:8]
    query, keys, values, gate_pre, grad_turned = outs[11:16]
    retained, mixed, resid_mid, mid_turned, gate_hidden, up_hidden, hidden = outs[16:]
    feed_outs = feed_backward(
        grad_full,
        grad_turned,
        mid_turned,
        hidden,
        resid_mid,
        gains,
        outs[8:11],
        (gate_hidden, up_hidden),
        lines,
        members,
    )
    down_grad, mlp_gate_grad, mlp_up_grad, mid_all, mid_grad = feed_outs[:5]
    hidden_out, gain_part, mid_low_turned = feed_outs[5:]
    out_weight_grad, gate_grad, value_grad, query_grad, key_grad, in_grad, gain_total = (
        retention_backward(
            [
                mixed,
                normed_turned,
                query,
                keys,
                values,
                mid_low_turned,
                cosine,
                sine,
                segment_ids.T,
                segment_ids,
                rates,
                resid_low,
                gains,
                gain_part,
            ],
            [mid_grad, mid_all, retained, gate_pre],
            [out_weight, gate_weight, value_weight, query_weight, key_weight],
            lines,
            members,
            slice_width,
        )
    )
    def add_up(pieces):
        total = pieces[0].astype(WIDE)
        for k in range(1, pieces.shape[0]):
            total = total + pieces[k].astype(WIDE)
        return total

    return (
        hidden_out.reshape(hidden_in.shape),
        in_grad.reshape(hidden_in.shape),
        gain_total[0],
        add_up(query_grad),
        add_up(key_grad),
        add_up(value_grad),
        add_up(gate_grad),
        add_up(out_weight_grad).T,
        gain_total[1],
        add_up(mlp_gate_grad),
        add_up(mlp_up_grad),
        add_up(down_grad).T,
    )


def solution(mesh):
    return jax.shard_map(
        on_device,
        mesh=mesh,
        in_specs=(
            P("dp", "tensor", None),
            P("dp", "tensor", None),
            P("dp", None),
            P("dp"),
            P("dp", "tensor"),
            P("dp", "tensor"),
            P("dp", "tensor"),
            P("dp", "tensor"),
            P("tensor", "dp"),
            P("dp"),
            P("dp", "tensor"),
            P("dp", "tensor"),
            P("tensor", "dp"),
        ),
        out_specs=(
            P("dp", "tensor", None),
            P("dp", "tensor", None),
            P("dp"),
            P("dp", "tensor"),
            P("dp", "tensor"),
            P("dp", "tensor"),
            P("dp", "tensor"),
            P("tensor", "dp"),
            P("dp"),
            P("dp", "tensor"),
            P("dp", "tensor"),
            P("tensor", "dp"),
        ),
        check_vma=False,
    )
```
